32 devices in a mesh: fam: 4 (over z), ctx: 8 (over y, x, core).
Axes of the slice: x: 2, y: 2, z: 4, core: 2. Of those that a mesh axis runs over, the one named last changes fastest.
Arguments:
- queries: bfloat16 [4, 4096, 1024], P('fam', 'ctx'), may hold values from -7 to 7
- key_rows: bfloat16 [4, 4096, 1024], P('fam', 'ctx'), may hold values from -4 to 4
- value_rows: bfloat16 [4, 4096, 1024], P('fam', 'ctx'), may hold values from -6 to 6
- cotangent: bfloat16 [4, 4096, 1024], P('fam', 'ctx'), may hold values from -6 to 6
- out_weight: bfloat16 [1024, 1024], replicated, may hold values from -0.1875 to 0.1875
- prot_blocks: int32 [4, 8], P('fam'), may hold values from 1 to 8, 32 in all within a row
- last_fill: int32 [4, 8], P('fam'), may hold values from 1 to 128
- memory_slots: int32 [4, 128], P('fam'), may hold values from 0 to 511
Outputs:
- query_grad: bfloat16 [4, 4096, 1024], P('fam', 'ctx')
- key_grad: bfloat16 [4, 4096, 1024], P('fam', 'ctx')
- value_grad: bfloat16 [4, 4096, 1024], P('fam', 'ctx')
- weight_grad: float32 [1024, 1024], replicated
The draws below stay inside these ranges and needn't reach their ends.
Inputs may be any that keep to these rules, and one draw needn't show every extreme that they name: `prot_blocks`: each family's protein lengths, in blocks, sum to 32, and the longest has exactly 8 blocks.
All inputs are finite; a program needn't handle non-finite values.
Results may differ from the reference program's by a relative error of at most 0.015.
Values may be sent and summed in bfloat16 or wider, within the bound.
No kernel may reach another device: no remote copies, remote signals or barrier semaphores. Data moves between devices by JAX's collectives and lax.ppermute only.
A program may use at most 128 MiB of HBM per device.

```python
import math
import jax
import jax.numpy as jnp
import numpy as np
from jax import lax

D = 1024
HEADS = 16
HEAD_DIM = 64
W = 512
BLK = 128
MOST_BLK = 8
MEM_DEV = 16
TOK_DEV = 512
FAMS = 4
LEN = 4096
NBLK = 32
NPROT = 8
MEMS = 128


def paired_rows(key):
    shape = (FAMS, LEN, D)
    query_base = jnp.clip(jax.random.normal(jax.random.fold_in(key, 11), shape, jnp.float32), -4.0, 4.0)
    key_base = jnp.clip(jax.random.normal(jax.random.fold_in(key, 12), shape, jnp.float32), -4.0, 4.0)
    return (query_base, key_base)


def draw_queries(key, part):
    return paired_rows(key)[0].astype(jnp.bfloat16)


def draw_key_rows(key, part):
    return paired_rows(key)[1].astype(jnp.bfloat16)


def place_ends(drawn, own_key, smallest, largest):
    longest = drawn.shape.index(max(drawn.shape))
    spots = []
    for shift in (0, 1):
        where = [jax.random.randint(jax.random.fold_in(own_key, axis), (), 0, length) for axis, length in enumerate(drawn.shape)]
        where[longest] = (where[longest] + shift) % drawn.shape[longest]
        spots.append(tuple(where))
    return drawn.at[spots[0]].set(smallest).at[spots[1]].set(largest)


def level_of(key, extent, shards, least, largest):
    factor_of = 1.0
    for dim, blocks in shards:
        heights = jax.random.uniform(jax.random.fold_in(jax.random.fold_in(key, 6), dim), (blocks,), jnp.float32, least / len(shards), largest / len(shards))
        factor_of = factor_of * jnp.repeat(jnp.exp(heights), extent[dim] // blocks).reshape((-1,) + (1,) * (len(extent) - 1 - dim))
    return factor_of


def length_profile(count, total, bound, skew):
    loads = [(1 << 20) // math.isqrt(rank ** skew) + 1 for rank in range(2, count + 1)]
    rest, given = total - bound - (count - 1), [1] * (count - 1)
    while rest > 0:
        free = [i for i in range(count - 1) if given[i] < bound]
        mass, remaining = sum([loads[i] for i in free]), rest
        for i in free:
            extra = min(bound - given[i], max(1, remaining * loads[i] // mass), rest)
            given[i] = given[i] + extra
            rest = rest - extra
    return np.array([bound] + given)


def uneven(key, amount, total, reach, lean):
    if amount == 2:
        one = jax.random.randint(key, (), max(1, total - reach), min(reach, total - 1) + 1)
        return jnp.stack([one, total - one])
    tallies = jnp.asarray(length_profile(amount, total, reach, lean), jnp.int32)
    pairs = (amount - 1) // 2
    giver, receiver = tallies[1:1 + 2 * pairs:2], tallies[2:2 + 2 * pairs:2]
    margin = jnp.minimum(giver - 1, reach - receiver)
    moved = jax.random.randint(jax.random.fold_in(key, 1), (pairs,), 0, 1 << 20) % (margin + 1)
    tallies = tallies.at[1:1 + 2 * pairs:2].set(giver - moved).at[2:2 + 2 * pairs:2].set(receiver + moved)
    return tallies[jax.random.permutation(jax.random.fold_in(key, 2), amount)]


def centred(stream_key, shape, spread, bound, shards=(), kind=jnp.bfloat16):
    entries = spread * jax.random.normal(stream_key, shape, jnp.float32)
    if shards:
        entries = entries * level_of(stream_key, shape, shards, -0.22, 0.18)
    return jnp.clip(entries, -bound, bound).astype(kind)


def setup_inputs(seed: int = 0) -> dict:
    splits = jax.random.split(jax.random.key(seed), 9)
    queries = draw_queries(jax.random.fold_in(splits[8], 71), 0)
    key_rows = draw_key_rows(jax.random.fold_in(splits[8], 71), 0)
    value_rows = centred(splits[2], (FAMS, LEN, D), 1.0, 6.0, ((0, 4), (1, 8)))
    cotangent = centred(splits[3], (FAMS, LEN, D), 1.0, 6.0, ((0, 4), (1, 8)))
    out_weight = centred(splits[4], (D, D), D ** -0.5, 0.1875)
    prot_blocks = jax.vmap(lambda own: uneven(own, NPROT, NBLK, MOST_BLK, 2))(jax.random.split(splits[5], FAMS)).reshape((FAMS, NPROT)).astype(jnp.int32)
    last_fill = place_ends(jax.random.randint(splits[6], (FAMS, NPROT), 1, BLK + 1), jax.random.fold_in(splits[6], 1), 1, BLK).astype(jnp.int32)
    memory_slots = place_ends(jax.random.randint(splits[7], (FAMS, MEMS), 0, TOK_DEV), jax.random.fold_in(splits[7], 1), 0, TOK_DEV - 1).astype(jnp.int32)
    return dict(queries=queries, key_rows=key_rows, value_rows=value_rows, cotangent=cotangent, out_weight=out_weight, prot_blocks=prot_blocks, last_fill=last_fill, memory_slots=memory_slots)


NEG_FILL = -1e30


def protein_tables(prot_blocks, last_fill):
    prot_ends = jnp.cumsum(prot_blocks).astype(jnp.int32)
    starts = (prot_ends - prot_blocks).astype(jnp.int32)
    valid_len = ((prot_blocks - 1) * BLK + last_fill).astype(jnp.int32)
    return prot_ends, starts, valid_len


def token_info(positions, tables):
    prot_ends, starts, valid_len = tables
    prot_count = prot_ends.shape[0]
    block_ids = jnp.floor_divide(positions, BLK)
    protein = jnp.sum((block_ids[:, None] >= prot_ends[None, :]).astype(jnp.int32), axis=1).astype(jnp.int32)
    onehot = protein[:, None] == jnp.arange(prot_count, dtype=jnp.int32)[None, :]
    first_block = jnp.sum(jnp.where(onehot, starts[None, :], 0), axis=1).astype(jnp.int32)
    allowed = jnp.sum(jnp.where(onehot, valid_len[None, :], 0), axis=1).astype(jnp.int32)
    is_valid = (positions >= 0) & (protein < prot_count) & (positions - first_block * BLK < allowed)
    return protein, is_valid


def band_mask(query_pos, query_info, key_pos, key_info):
    return (query_info[1][:, None] & key_info[1][None, :]
            & (query_info[0][:, None] == key_info[0][None, :])
            & (key_pos[None, :] <= query_pos[:, None])
            & (query_pos[:, None] - key_pos[None, :] < W))


def attend(query_blk, grad_blk, key_blk, value_blk, live_mask):
    scale = HEAD_DIM ** -0.5
    query_f = query_blk.astype(jnp.float32)
    grad_f = grad_blk.astype(jnp.float32)
    key_f = key_blk.astype(jnp.float32)
    value_f = value_blk.astype(jnp.float32)
    scores = jnp.einsum('qhe,khe->hqk', query_f, key_f) * scale
    live = live_mask[None]
    shifted = jnp.where(live, scores, NEG_FILL)
    row_max = jnp.max(shifted, axis=-1, keepdims=True)
    expo = jnp.where(live, jnp.exp(shifted - row_max), 0.0)
    row_sum = jnp.maximum(jnp.sum(expo, axis=-1, keepdims=True), 1.0)
    attn_prob = expo / row_sum
    prob_half = attn_prob.astype(jnp.bfloat16)
    prob_back = prob_half.astype(jnp.float32)
    attended = jnp.einsum('hqk,khe->qhe', prob_back, value_f).astype(jnp.bfloat16)
    grad_prob = jnp.einsum('qhe,khe->hqk', grad_f, value_f)
    row_dot = jnp.sum(attn_prob * grad_prob, axis=-1, keepdims=True)
    grad_score = (attn_prob * (grad_prob - row_dot) * scale).astype(jnp.bfloat16).astype(jnp.float32)
    grad_query = jnp.einsum('hqk,khe->qhe', grad_score, key_f)
    grad_key = jnp.einsum('hqk,qhe->khe', grad_score, query_f)
    grad_value = jnp.einsum('hqk,qhe->khe', prob_back, grad_f)
    return attended, grad_query, grad_key, grad_value


def family_grads(query_all, key_all, value_all, grad_out, out_weight, prot_blocks, last_fill, slots):
    tables = protein_tables(prot_blocks, last_fill)
    positions = jnp.arange(LEN, dtype=jnp.int32)
    protein, is_valid = token_info(positions, tables)
    source = (jnp.arange(MEMS, dtype=jnp.int32) // MEM_DEV) * TOK_DEV + slots
    mem_prot = protein[source]
    mem_valid = is_valid[source]
    key_memory = key_all[source].reshape(MEMS, HEADS, HEAD_DIM)
    value_memory = value_all[source].reshape(MEMS, HEADS, HEAD_DIM)
    grad_attn = jnp.dot(grad_out, out_weight.T, preferred_element_type=jnp.float32).astype(jnp.bfloat16)
    padding = jnp.zeros((W, D), jnp.bfloat16)
    key_pad = jnp.concatenate([padding, key_all], axis=0)
    value_pad = jnp.concatenate([padding, value_all], axis=0)
    pad_pos = jnp.arange(LEN + W, dtype=jnp.int32) - W
    pad_prot, pad_valid = token_info(pad_pos, tables)

    def step(carry, block_num):
        band_kgrad, band_vgrad, mem_kgrad, mem_vgrad = carry
        row_start = block_num * W
        query_blk = lax.dynamic_slice_in_dim(query_all, row_start, W).reshape(W, HEADS, HEAD_DIM)
        grad_blk = lax.dynamic_slice_in_dim(grad_attn, row_start, W).reshape(W, HEADS, HEAD_DIM)
        key_band = lax.dynamic_slice_in_dim(key_pad, row_start, 2 * W).reshape(2 * W, HEADS, HEAD_DIM)
        value_band = lax.dynamic_slice_in_dim(value_pad, row_start, 2 * W).reshape(2 * W, HEADS, HEAD_DIM)
        query_pos = row_start + jnp.arange(W, dtype=jnp.int32)
        query_info = (lax.dynamic_slice_in_dim(protein, row_start, W), lax.dynamic_slice_in_dim(is_valid, row_start, W))
        key_pos = row_start - W + jnp.arange(2 * W, dtype=jnp.int32)
        key_info = (lax.dynamic_slice_in_dim(pad_prot, row_start, 2 * W), lax.dynamic_slice_in_dim(pad_valid, row_start, 2 * W))
        band = band_mask(query_pos, query_info, key_pos, key_info)
        memory = query_info[1][:, None] & mem_valid[None, :] & (mem_prot[None, :] < query_info[0][:, None])
        live_mask = jnp.concatenate([band, memory], axis=1)
        key_blk = jnp.concatenate([key_band, key_memory], axis=0)
        value_blk = jnp.concatenate([value_band, value_memory], axis=0)
        attended, grad_query, grad_key, grad_value = attend(query_blk, grad_blk, key_blk, value_blk, live_mask)
        old_k = lax.dynamic_slice_in_dim(band_kgrad, row_start, 2 * W)
        band_kgrad = lax.dynamic_update_slice_in_dim(band_kgrad, old_k + grad_key[:2 * W].reshape(2 * W, D), row_start, 0)
        old_v = lax.dynamic_slice_in_dim(band_vgrad, row_start, 2 * W)
        band_vgrad = lax.dynamic_update_slice_in_dim(band_vgrad, old_v + grad_value[:2 * W].reshape(2 * W, D), row_start, 0)
        mem_kgrad = mem_kgrad + grad_key[2 * W:].reshape(MEMS, D)
        mem_vgrad = mem_vgrad + grad_value[2 * W:].reshape(MEMS, D)
        return (band_kgrad, band_vgrad, mem_kgrad, mem_vgrad), (attended.reshape(W, D), grad_query.reshape(W, D))

    init = (jnp.zeros((LEN + W, D), jnp.float32), jnp.zeros((LEN + W, D), jnp.float32),
            jnp.zeros((MEMS, D), jnp.float32), jnp.zeros((MEMS, D), jnp.float32))
    carry, stacked = lax.scan(step, init, jnp.arange(LEN // W, dtype=jnp.int32))
    band_kgrad, band_vgrad, mem_kgrad, mem_vgrad = carry
    attended = stacked[0].reshape(LEN, D)
    query_grad = stacked[1].reshape(LEN, D)
    key_grad = band_kgrad[W:].at[source].add(mem_kgrad)
    value_grad = band_vgrad[W:].at[source].add(mem_vgrad)
    weight_part = jnp.dot(attended.T, grad_out, preferred_element_type=jnp.float32)
    return query_grad.astype(jnp.bfloat16), key_grad.astype(jnp.bfloat16), value_grad.astype(jnp.bfloat16), weight_part


def reference(queries, key_rows, value_rows, cotangent, out_weight, prot_blocks, last_fill, memory_slots):
    query_list = []
    key_list = []
    value_list = []
    weight_total = jnp.zeros((D, D), jnp.float32)
    for family in range(FAMS):
        query_grad, key_grad, value_grad, weight_part = family_grads(
            queries[family], key_rows[family], value_rows[family], cotangent[family], out_weight,
            prot_blocks[family], last_fill[family], memory_slots[family])
        query_list.append(query_grad)
        key_list.append(key_grad)
        value_list.append(value_grad)
        weight_total = weight_total + weight_part
    weight_grad = weight_total * (FAMS * LEN) ** -0.5
    return jnp.stack(query_list), jnp.stack(key_list), jnp.stack(value_list), weight_grad
```

```python
import functools
import jax, jax.numpy as jnp
from jax import lax
from jax.experimental import pallas as pl
from jax.experimental.pallas import tpu as pltpu
HEAD_DIM=64; W=512; BLK=128; NEG=-1e30
NT=(((1,),(1,)),((),())); NN=(((1,),(0,)),((),())); TN=(((0,),(0,)),((),()))
f32=jnp.float32; bf16=jnp.bfloat16
def dot(a,b,d): return lax.dot_general(a,b,d,preferred_element_type=f32)

def attn_kernel(info_ref, q_ref, g_ref, ko_ref, vo_ref, kh_ref, vh_ref, km_ref, vm_ref, mb_ref,
                dq_ref, at_ref, dko_ref, dvo_ref, dkh_ref, dvh_ref, dkm_ref, dvm_ref,
                ke, ve, q2, g2, pt, dst, *, nb, far):
    slots = km_ref.shape[0]
    span = 2*HEAD_DIM
    hrows = kh_ref.shape[0]; orows = ko_ref.shape[0]
    ext = hrows+orows
    two = 2*BLK
    ke[0:hrows,:] = kh_ref[...]; ke[hrows:ext,:] = ko_ref[...]; ke[ext:,:] = km_ref[...]
    ve[0:hrows,:span] = vh_ref[...]; ve[hrows:ext,:span] = vo_ref[...]; ve[ext:,:span] = vm_ref[...]
    ve[:, span:] = jnp.ones((ext+slots, span), bf16)
    lane = lax.broadcasted_iota(jnp.int32,(BLK,span),1)
    first = lane < HEAD_DIM
    kk = lax.broadcasted_iota(jnp.int32,(BLK,two),0)
    qq = lax.broadcasted_iota(jnp.int32,(BLK,two),1) % BLK
    tri = kk <= qq
    lane2 = lax.broadcasted_iota(jnp.int32,(two,span),1)
    row2 = lax.broadcasted_iota(jnp.int32,(two,span),0) % BLK
    zero = jnp.zeros((BLK,span),bf16)
    for b in range(nb):
        rows = slice(b*BLK,(b+1)*BLK); r2 = slice(b*two,(b+1)*two)
        q = q_ref[rows,:]*jnp.asarray(HEAD_DIM**-0.5,bf16)
        q2b = jnp.concatenate([jnp.where(first,q,zero), jnp.where(first,zero,q)],0)
        q2[r2,:] = q2b
        s = dot(ke[b*BLK:(b+far+1)*BLK,:], q2b, NT)
        sm = dot(ke[ext:,:], q2b, NT) + jnp.concatenate([mb_ref[b],mb_ref[b]],1)
        lo = info_ref[0,b]
        off = [jnp.where(e+b >= lo, 0.0, NEG).astype(f32) for e in range(far)]
        s0 = jnp.where(tri, s[far*BLK:,:], s[:BLK,:]+off[0])
        mid = [s[e*BLK:(e+1)*BLK,:] for e in range(1,far)]
        m = jnp.maximum(jnp.max(s0,0,keepdims=True), jnp.max(sm,0,keepdims=True))
        for e in range(1,far):
            m = jnp.maximum(m, jnp.max(mid[e-1],0,keepdims=True)+off[e])
        p0 = jnp.exp(s0-m).astype(bf16)
        zb = jnp.zeros_like(p0)
        pt[b*BLK:(b+1)*BLK, r2] = jnp.where(tri, zb, p0)
        pt[(b+far)*BLK:(b+far+1)*BLK, r2] = jnp.where(tri, p0, zb)
        for e in range(1,far):
            pt[(b+e)*BLK:(b+e+1)*BLK, r2] = jnp.exp(mid[e-1]-(m-off[e])).astype(bf16)
        pt[ext:, r2] = jnp.exp(sm-m).astype(bf16)
        o = dot(pt[b*BLK:(b+far+1)*BLK, r2], ve[b*BLK:(b+far+1)*BLK,:], TN) + dot(pt[ext:, r2], ve[ext:,:], TN)
        scale = jnp.where(row2 < info_ref[1,b], 1.0/o[:,span:], 0.0)
        on = o[:,:span]*scale
        at_ref[rows,:] = jnp.where(first, on[:BLK], on[BLK:]).astype(bf16)
        g = g_ref[rows,:].astype(f32)
        gz = jnp.zeros_like(g)
        g2f = jnp.concatenate([jnp.where(first,g,gz), jnp.where(first,gz,g)],0)*scale
        g2b = g2f.astype(bf16)
        g2[r2,:] = g2b
        dd = -jnp.sum(g2b.astype(f32)*on,1,keepdims=True)
        dhi = dd.astype(bf16).astype(f32)
        daug = jnp.where(lane2==0, dhi, jnp.where(lane2==1, dd-dhi, 0.0)).astype(bf16)
        gaug = jnp.concatenate([g2b,daug],1)
        dp = dot(ve[b*BLK:(b+far+1)*BLK,:], gaug, NT)
        dst[b*BLK:(b+far+1)*BLK, r2] = (pt[b*BLK:(b+far+1)*BLK, r2].astype(f32)*dp).astype(bf16)
        dpm = dot(ve[ext:,:], gaug, NT)
        dst[ext:, r2] = (pt[ext:, r2].astype(f32)*dpm).astype(bf16)
        dq = dot(dst[b*BLK:(b+far+1)*BLK, r2], ke[b*BLK:(b+far+1)*BLK,:], TN) + dot(dst[ext:, r2], ke[ext:,:], TN)
        dq_ref[rows,:] = (jnp.where(first, dq[:BLK], dq[BLK:])*(HEAD_DIM**-0.5)).astype(bf16)
    hb = hrows//BLK
    for e in range(ext//BLK):
        b0, b1 = max(0,e-far), min(nb-1,e)
        cr = slice(b0*two,(b1+1)*two)
        er = slice(e*BLK,(e+1)*BLK)
        dv = dot(pt[er,cr], g2[cr,:], NN)
        dk = dot(dst[er,cr], q2[cr,:], NN)
        if e < hb:
            dvh_ref[er,:] = dv.astype(bf16); dkh_ref[er,:] = dk.astype(bf16)
        else:
            orr = slice((e-hb)*BLK,(e-hb+1)*BLK)
            dvo_ref[orr,:] = dv; dko_ref[orr,:] = dk
    dvm_ref[...] = dot(pt[ext:,:], g2[...], NN).astype(bf16)
    dkm_ref[...] = dot(dst[ext:,:], q2[...], NN).astype(bf16)

def attn(info, q, g, ko, vo, kh, vh, km, vm, mb, *, p0=0, np_=None):
    tokens, width = q.shape; slots = km.shape[0]
    nb = tokens//BLK; far = W//BLK; span=2*HEAD_DIM
    np_ = np_ or width//span
    ext = kh.shape[0]+tokens
    col = lambda r: pl.BlockSpec((r,span), lambda p,*_: (0,p+p0))
    ocol = lambda r: pl.BlockSpec((r,span), lambda p,*_: (0,p))
    hw = np_*span
    outs = [((tokens,hw),bf16),((tokens,hw),bf16),((tokens,hw),f32),((tokens,hw),f32),
            ((kh.shape[0],hw),bf16),((kh.shape[0],hw),bf16),((slots,hw),bf16),((slots,hw),bf16)]
    return pl.pallas_call(
        functools.partial(attn_kernel, nb=nb, far=far),
        grid_spec=pltpu.PrefetchScalarGridSpec(
            num_scalar_prefetch=1, grid=(np_,),
            in_specs=[col(tokens),col(tokens),col(tokens),col(tokens),col(kh.shape[0]),col(kh.shape[0]),col(slots),col(slots),
                      pl.BlockSpec(mb.shape, lambda p,*_:(0,0,0))],
            out_specs=[ocol(s[0]) for s,_ in outs],
            scratch_shapes=[pltpu.VMEM((ext+slots,span),bf16), pltpu.VMEM((ext+slots,2*span),bf16),
                            pltpu.VMEM((nb*2*BLK,span),bf16), pltpu.VMEM((nb*2*BLK,span),bf16),
                            pltpu.VMEM((ext+slots,nb*2*BLK),bf16), pltpu.VMEM((ext+slots,nb*2*BLK),bf16)]),
        out_shape=[jax.ShapeDtypeStruct(s,d) for s,d in outs],
        compiler_params=pltpu.CompilerParams(vmem_limit_bytes=48<<20),
        name="band_grad",
    )(info, q, g, ko, vo, kh, vh, km, vm, mb)


from jax.sharding import PartitionSpec as P


def protein_tables(prot_blocks, last_fill):
    prot_ends = jnp.cumsum(prot_blocks)
    starts = prot_ends - prot_blocks
    valid_len = (prot_blocks - 1) * BLK + last_fill
    return prot_ends, starts, valid_len


def token_info(positions, tables):
    prot_ends, starts, valid_len = tables
    count = prot_ends.shape[0]
    blocks = jnp.floor_divide(positions, BLK)
    protein = jnp.sum((blocks[:, None] >= prot_ends[None, :]).astype(jnp.int32), axis=1)
    onehot = protein[:, None] == jnp.arange(count, dtype=jnp.int32)[None, :]
    first = jnp.sum(jnp.where(onehot, starts[None, :], 0), axis=1)
    length = jnp.sum(jnp.where(onehot, valid_len[None, :], 0), axis=1)
    left = length - (positions - first * BLK)
    return protein, first, left


def swap(x, axis, bit):
    n = lax.axis_size(axis)
    return lax.ppermute(x, axis, [(i, i ^ bit) for i in range(n)])


def bits_of(n):
    out, b = [], 1
    while b < n:
        out.append(b)
        b *= 2
    return out


def gather_rows(x, axis):
    me = lax.axis_index(axis)
    for bit in bits_of(lax.axis_size(axis)):
        other = swap(x, axis, bit)
        upper = (me & bit) != 0
        x = jnp.where(upper, jnp.concatenate([other, x], 0), jnp.concatenate([x, other], 0))
    return x


def scatter_rows(x, axis):
    me = lax.axis_index(axis)
    for bit in reversed(bits_of(lax.axis_size(axis))):
        half = x.shape[0] // 2
        upper = (me & bit) != 0
        lo, hi = x[:half], x[half:]
        keep = jnp.where(upper, hi, lo)
        send = jnp.where(upper, lo, hi)
        x = keep.astype(f32) + swap(send.astype(bf16), axis, bit).astype(f32)
    return x


def per_device(queries, key_rows, value_rows, cotangent, out_weight, prot_blocks, last_fill, memory_slots):
    q, k, v, cot = queries[0], key_rows[0], value_rows[0], cotangent[0]
    tables = protein_tables(prot_blocks[0], last_fill[0])
    slots = memory_slots[0]
    tokens, width = q.shape
    nctx = lax.axis_size("ctx")
    me = lax.axis_index("ctx")
    total = slots.shape[0]
    mine = total // nctx
    nb = tokens // BLK
    own_slots = lax.dynamic_slice_in_dim(slots, me * mine, mine)
    mem = gather_rows(jnp.concatenate([k[own_slots], v[own_slots]], 1), "ctx")
    shift = [(i, i + 1) for i in range(nctx - 1)]
    kh, vh = lax.ppermute(k, "ctx", shift), lax.ppermute(v, "ctx", shift)
    grad_attn = jnp.einsum("te,de->td", cot, out_weight, preferred_element_type=f32).astype(bf16)
    heads = me * tokens + jnp.arange(nb, dtype=jnp.int32) * BLK
    prot_q, first_q, left_q = token_info(heads, tables)
    lo = jnp.clip(first_q - (me * tokens - W) // BLK, 0, 2 * W)
    info = jnp.stack([lo, jnp.clip(left_q, 0, BLK)])
    source = jnp.arange(total, dtype=jnp.int32) // mine * tokens + slots
    prot_m, _, left_m = token_info(source, tables)
    seen = (left_m > 0)[None, :] & (prot_m[None, :] < prot_q[:, None])
    bias = jnp.broadcast_to(jnp.where(seen, 0.0, NEG).astype(f32)[:, :, None], (nb, total, BLK))
    dq, att, dko, dvo, dkh, dvh, dkm, dvm = attn(
        info, q, grad_attn, k, v, kh, vh, mem[:, :width], mem[:, width:], bias)
    weight = lax.dot_general(att, cot, TN, preferred_element_type=f32)
    piece = scatter_rows(scatter_rows(weight, "ctx"), "fam")
    scale = (lax.axis_size("fam") * nctx * tokens) ** -0.5
    weight = gather_rows(gather_rows(piece.astype(bf16), "fam"), "ctx").astype(f32) * scale
    back = [(i + 1, i) for i in range(nctx - 1)]
    bk, bv = lax.ppermute(dkh, "ctx", back), lax.ppermute(dvh, "ctx", back)
    dmem = scatter_rows(jnp.concatenate([dkm, dvm], 1), "ctx")
    pick = (jnp.arange(tokens, dtype=jnp.int32)[:, None] == own_slots[None, :]).astype(bf16)
    dmem = jnp.dot(pick, dmem.astype(bf16), preferred_element_type=f32)
    dk = (dko + bk.astype(f32) + dmem[:, :width]).astype(bf16)
    dv = (dvo + bv.astype(f32) + dmem[:, width:]).astype(bf16)
    return dq[None], dk[None], dv[None], weight


def solution(mesh):
    row = P("fam", "ctx", None)
    small = P("fam", None)
    return jax.shard_map(
        per_device,
        mesh=mesh,
        in_specs=(row, row, row, row, P(), small, small, small),
        out_specs=(row, row, row, P()),
        check_vma=False,
    )
```

```python
import functools
import math

import jax
import jax.numpy as jnp
from jax import lax
from jax.experimental import pallas as pl
from jax.experimental.pallas import tpu as pltpu
from jax.sharding import PartitionSpec as P

HEAD_DIM = 64
W = 512
BLK = 128
SPAN = 2 * HEAD_DIM
TWO = 2 * BLK
FAR = W // BLK
NEG = -1e30
NT = (((1,), (1,)), ((), ()))
NN = (((1,), (0,)), ((), ()))
TN = (((0,), (0,)), ((), ()))
f32 = jnp.float32
bf16 = jnp.bfloat16


def dot(a, b, dims):
    return lax.dot_general(a, b, dims, preferred_element_type=f32)


def by_head(x, first):
    zero = jnp.zeros_like(x)
    return jnp.concatenate([jnp.where(first, x, zero), jnp.where(first, zero, x)], 0)


def join_heads(x, first):
    return jnp.where(first, x[:BLK], x[BLK:])


def fill_keys(dst, halo, own, memory):
    h, o = halo.shape[0], own.shape[0]
    dst[0:h, :SPAN] = halo[...]
    dst[h : h + o, :SPAN] = own[...]
    dst[h + o :, :SPAN] = memory[...]


def forward_kernel(
    info_ref, q_ref, g_ref, ko_ref, vo_ref, kh_ref, vh_ref, km_ref, vm_ref, mb_ref, *rest, nb
):
    at_ref, pt, ga_ref, ke, ve = rest[-5:]
    ext = kh_ref.shape[0] + ko_ref.shape[0]
    fill_keys(ke, kh_ref, ko_ref, km_ref)
    fill_keys(ve, vh_ref, vo_ref, vm_ref)
    ve[:, SPAN:] = jnp.ones((ve.shape[0], SPAN), bf16)
    first = lax.broadcasted_iota(jnp.int32, (BLK, SPAN), 1) < HEAD_DIM
    tri = (
        lax.broadcasted_iota(jnp.int32, (BLK, TWO), 0)
        <= lax.broadcasted_iota(jnp.int32, (BLK, TWO), 1) % BLK
    )
    lane = lax.broadcasted_iota(jnp.int32, (TWO, SPAN), 1)
    row = lax.broadcasted_iota(jnp.int32, (TWO, SPAN), 0) % BLK
    for b in range(nb):
        rows, cols = slice(b * BLK, (b + 1) * BLK), slice(b * TWO, (b + 1) * TWO)
        band = slice(b * BLK, (b + FAR + 1) * BLK)
        q2 = by_head(q_ref[rows, :] * jnp.asarray(HEAD_DIM**-0.5, bf16), first)
        s = dot(ke[band, :], q2, NT)
        sm = dot(ke[ext:, :], q2, NT) + jnp.concatenate([mb_ref[b], mb_ref[b]], 1)
        lo = info_ref[0, b]
        off = [jnp.where(e + b >= lo, 0.0, NEG).astype(f32) for e in range(FAR)]
        ends = jnp.where(tri, s[FAR * BLK :, :], s[:BLK, :] + off[0])
        mid = [s[e * BLK : (e + 1) * BLK, :] for e in range(1, FAR)]
        m = jnp.maximum(jnp.max(ends, 0, keepdims=True), jnp.max(sm, 0, keepdims=True))
        for e in range(1, FAR):
            m = jnp.maximum(m, jnp.max(mid[e - 1], 0, keepdims=True) + off[e])
        p = jnp.exp(ends - m).astype(bf16)
        zero = jnp.zeros_like(p)
        pt[0, b * BLK : (b + 1) * BLK, cols] = jnp.where(tri, zero, p)
        pt[0, (b + FAR) * BLK : (b + FAR + 1) * BLK, cols] = jnp.where(tri, p, zero)
        for e in range(1, FAR):
            pt[0, (b + e) * BLK : (b + e + 1) * BLK, cols] = jnp.exp(
                mid[e - 1] - (m - off[e])
            ).astype(bf16)
        pt[0, ext:, cols] = jnp.exp(sm - m).astype(bf16)
        o = dot(pt[0, band, cols], ve[band, :], TN) + dot(pt[0, ext:, cols], ve[ext:, :], TN)
        scale = jnp.where(row < info_ref[1, b], 1.0 / o[:, SPAN:], 0.0)
        o = o[:, :SPAN] * scale
        at_ref[rows, :] = join_heads(o, first).astype(bf16)
        g2 = (by_head(g_ref[rows, :].astype(f32), first) * scale).astype(bf16)
        d = -jnp.sum(g2.astype(f32) * o, 1, keepdims=True)
        high = d.astype(bf16).astype(f32)
        ga_ref[0, cols, :SPAN] = g2
        ga_ref[0, cols, SPAN:] = jnp.where(
            lane == 0, high, jnp.where(lane == 1, d - high, 0.0)
        ).astype(bf16)


def backward_kernel(
    q_ref, pt_ref, ga_ref, ko_ref, vo_ref, kh_ref, vh_ref, km_ref, vm_ref, *rest, nb
):
    dq_ref, dko_ref, dvo_ref, dm_ref, dh_ref, ke, ve, q2, ds = rest[-9:]
    hrows, slots = kh_ref.shape[0], km_ref.shape[0]
    ext = hrows + ko_ref.shape[0]
    fill_keys(ke, kh_ref, ko_ref, km_ref)
    fill_keys(ve, vh_ref, vo_ref, vm_ref)
    ve[:, SPAN:] = jnp.ones((ve.shape[0], SPAN), bf16)
    first = lax.broadcasted_iota(jnp.int32, (BLK, SPAN), 1) < HEAD_DIM
    unit = HEAD_DIM**-0.5
    for b in range(nb):
        rows, cols = slice(b * BLK, (b + 1) * BLK), slice(b * TWO, (b + 1) * TWO)
        band = slice(b * BLK, (b + FAR + 1) * BLK)
        q2[cols, :] = by_head(q_ref[rows, :] * jnp.asarray(unit, bf16), first)
        ga = ga_ref[0, cols, :]
        dp = dot(ve[band, :], ga, NT)
        ds[band, cols] = (pt_ref[0, band, cols].astype(f32) * dp).astype(bf16)
        dp = dot(ve[ext:, :], ga, NT)
        ds[ext:, cols] = (pt_ref[0, ext:, cols].astype(f32) * dp).astype(bf16)
        dq = dot(ds[band, cols], ke[band, :], TN) + dot(ds[ext:, cols], ke[ext:, :], TN)
        dq_ref[rows, :] = (join_heads(dq, first) * unit).astype(bf16)
    for e in range(ext // BLK):
        cols = slice(max(0, e - FAR) * TWO, (min(nb - 1, e) + 1) * TWO)
        rows = slice(e * BLK, (e + 1) * BLK)
        dv = dot(pt_ref[0, rows, cols], ga_ref[0, cols, :SPAN], NN)
        dk = dot(ds[rows, cols], q2[cols, :], NN)
        if e * BLK < hrows:
            dh_ref[rows, :] = dk.astype(bf16)
            dh_ref[hrows + e * BLK : hrows + (e + 1) * BLK, :] = dv.astype(bf16)
        else:
            own = slice(e * BLK - hrows, (e + 1) * BLK - hrows)
            dko_ref[own, :] = dk
            dvo_ref[own, :] = dv
    dm_ref[:slots, :] = dot(ds[ext:, :], q2[...], NN).astype(bf16)
    dm_ref[slots:, :] = dot(pt_ref[0, ext:, :], ga_ref[0, :, :SPAN], NN).astype(bf16)


def columns(rows, start):
    return pl.BlockSpec((rows, SPAN), lambda p, *_: (0, p + start))


ANY = pl.BlockSpec(memory_space=pl.ANY)


def forward(info, q, g, ko, vo, kh, vh, km, vm, bias, start, count, base, halo_at, carry):
    tokens, width = q.shape
    slots, hrows, nb = km.shape[0], kh.shape[0], tokens // BLK
    keys = hrows + tokens + slots
    kc, vc = halo_at
    mk, mv = base
    args = [info, q, g, ko, vo, kh, vh, km, vm, bias]
    specs = [
        columns(tokens, start), columns(tokens, start), columns(tokens, start), columns(tokens, start),
        columns(hrows, kc), columns(hrows, vc), columns(slots, mk + start), columns(slots, mv + start),
        pl.BlockSpec(bias.shape, lambda p, *_: (0, 0, 0)),
    ]
    alias = {}
    if carry is not None:
        alias = {len(args): 0}
        args.append(carry)
        specs.append(ANY)
    return pl.pallas_call(
        functools.partial(forward_kernel, nb=nb),
        grid_spec=pltpu.PrefetchScalarGridSpec(
            num_scalar_prefetch=1,
            grid=(count,),
            in_specs=specs,
            out_specs=[
                columns(tokens, start),
                pl.BlockSpec((1, keys, nb * TWO), lambda p, *_: (p, 0, 0)),
                pl.BlockSpec((1, nb * TWO, 2 * SPAN), lambda p, *_: (p, 0, 0)),
            ],
            scratch_shapes=[pltpu.VMEM((keys, SPAN), bf16), pltpu.VMEM((keys, 2 * SPAN), bf16)],
        ),
        out_shape=[
            jax.ShapeDtypeStruct((tokens, width), bf16),
            jax.ShapeDtypeStruct((count, keys, nb * TWO), bf16),
            jax.ShapeDtypeStruct((count, nb * TWO, 2 * SPAN), bf16),
        ],
        input_output_aliases=alias,
        compiler_params=pltpu.CompilerParams(vmem_limit_bytes=40 << 20),
        cost_estimate=pl.CostEstimate(
            flops=count * nb * 12 * TWO * BLK * 1024, bytes_accessed=count * (4 << 20), transcendentals=count << 20
        ),
        name="band_forward",
    )(*args)


def backward(q, pt, ga, ko, vo, kh, vh, km, vm, start, count, base, halo_at, at, carry):
    tokens, width = q.shape
    slots, hrows, nb = km.shape[0], kh.shape[0], tokens // BLK
    keys = hrows + tokens + slots
    kc, vc = halo_at
    mk, mv = base
    args = [q, pt, ga, ko, vo, kh, vh, km, vm]
    specs = [
        columns(tokens, start),
        pl.BlockSpec((1, keys, nb * TWO), lambda p, *_: (p + at, 0, 0)),
        pl.BlockSpec((1, nb * TWO, 2 * SPAN), lambda p, *_: (p + at, 0, 0)),
        columns(tokens, start), columns(tokens, start),
        columns(hrows, kc), columns(hrows, vc), columns(slots, mk + start), columns(slots, mv + start),
    ]
    alias = {}
    if carry is not None:
        alias = {len(args) + i: i for i in range(len(carry))}
        args += carry
        specs += [ANY] * len(carry)
    return pl.pallas_call(
        functools.partial(backward_kernel, nb=nb),
        grid=(count,),
        in_specs=specs,
        out_specs=[
            columns(tokens, start), columns(tokens, start), columns(tokens, start),
            columns(2 * slots, start), columns(2 * hrows, 0),
        ],
        scratch_shapes=[
            pltpu.VMEM((keys, SPAN), bf16), pltpu.VMEM((keys, 2 * SPAN), bf16),
            pltpu.VMEM((nb * TWO, SPAN), bf16), pltpu.VMEM((keys, nb * TWO), bf16),
        ],
        out_shape=[
            jax.ShapeDtypeStruct((tokens, width), bf16),
            jax.ShapeDtypeStruct((tokens, width), f32),
            jax.ShapeDtypeStruct((tokens, width), f32),
            jax.ShapeDtypeStruct((2 * slots, width), bf16),
            jax.ShapeDtypeStruct((2 * hrows, count * SPAN), bf16),
        ],
        input_output_aliases=alias,
        compiler_params=pltpu.CompilerParams(vmem_limit_bytes=40 << 20),
        cost_estimate=pl.CostEstimate(
            flops=count * nb * 20 * TWO * BLK * 1024, bytes_accessed=count * (6 << 20), transcendentals=0
        ),
        name="band_backward",
    )(*args)


def finish_kernel(slot_ref, dk_in, dv_in, mk_ref, mv_ref, *rest):
    backs, (dk_ref, dv_ref) = rest[:-2], rest[-2:]
    tokens = dk_in.shape[0]
    mine = slot_ref.shape[1]
    pick = (lax.broadcasted_iota(jnp.int32, (tokens, mine), 0) == slot_ref[...]).astype(f32).astype(bf16)
    dk = dk_in[...] + dot(pick, mk_ref[...], NN)
    dv = dv_in[...] + dot(pick, mv_ref[...], NN)
    edge = tokens - W
    for i, back in enumerate(backs):

        @pl.when(pl.program_id(0) == i)
        def _():
            dk_ref[edge:, :] = (dk[edge:] + back[:W, :].astype(f32)).astype(bf16)
            dv_ref[edge:, :] = (dv[edge:] + back[W:, :].astype(f32)).astype(bf16)


def finish(slots, dko, dvo, dmem, backs):
    tokens, width = dko.shape
    mine, n = slots.shape[0], len(backs)
    step = width // n
    col = lambda r, j: pl.BlockSpec((r, step), lambda i: (j, i))
    return pl.pallas_call(
        finish_kernel,
        grid=(n,),
        in_specs=[pl.BlockSpec((1, mine), lambda i: (0, 0)), col(tokens, 0), col(tokens, 0), col(mine, 0), col(mine, 1)]
        + [pl.BlockSpec((2 * W, step), lambda i: (0, 0))] * n,
        out_specs=[col(tokens, 0), col(tokens, 0)],
        out_shape=[jax.ShapeDtypeStruct((tokens, width), bf16)] * 2,
        compiler_params=pltpu.CompilerParams(vmem_limit_bytes=40 << 20),
        cost_estimate=pl.CostEstimate(flops=1 << 26, bytes_accessed=8 << 20, transcendentals=0),
        name="finish_rows",
    )(slots[None, :], dko, dvo, dmem, dmem, *backs)


def protein_tables(prot_blocks, last_fill):
    prot_ends = jnp.cumsum(prot_blocks)
    starts = prot_ends - prot_blocks
    valid_len = (prot_blocks - 1) * BLK + last_fill
    return prot_ends, starts, valid_len


def token_info(positions, tables):
    prot_ends, starts, valid_len = tables
    count = prot_ends.shape[0]
    blocks = jnp.floor_divide(positions, BLK)
    protein = jnp.sum((blocks[:, None] >= prot_ends[None, :]).astype(jnp.int32), axis=1)
    onehot = protein[:, None] == jnp.arange(count, dtype=jnp.int32)[None, :]
    first = jnp.sum(jnp.where(onehot, starts[None, :], 0), axis=1)
    length = jnp.sum(jnp.where(onehot, valid_len[None, :], 0), axis=1)
    return protein, first, length - (positions - first * BLK)


def swap(x, axis, bits):
    n = lax.axis_size(axis)
    return lax.ppermute(x, axis, [(i, i ^ bits) for i in range(n)])


def bits_of(n):
    out, b = [], 1
    while b < n:
        out.append(b)
        b *= 2
    return out


def gather_rows(x, axis, me):
    for bit in bits_of(lax.axis_size(axis)):
        other = swap(x, axis, bit)
        upper = (me & bit) != 0
        x = jnp.where(upper, jnp.concatenate([other, x], 0), jnp.concatenate([x, other], 0))
    return x


def halve(x, axis, me):
    for bit in bits_of(lax.axis_size(axis)):
        lead, n = x.shape[0], x.shape[1]
        x = x.reshape(lead, n // 2, 2, *x.shape[2:])
        upper = (me & bit) != 0
        keep = jnp.where(upper, x[:, :, 1], x[:, :, 0])
        send = jnp.where(upper, x[:, :, 0], x[:, :, 1])
        x = keep.astype(f32) + swap(send.astype(bf16), axis, bit).astype(f32)
    return x


def exchange(parts, axis, shift, me, n):
    rows = parts.shape[0] // n
    part = lambda j: lax.dynamic_slice_in_dim(parts, j * rows, rows)
    got = [swap(part(me ^ k).astype(bf16), axis, k << shift) for k in range(1, n)]
    return sum([g.astype(f32) for g in got], part(me).astype(f32))


def spread(x, axis, shift, me, n):
    parts = [x] + [swap(x, axis, k << shift) for k in range(1, n)]
    for bit in bits_of(n):
        upper = (me & bit) != 0
        parts = [jnp.where(upper, parts[j ^ bit], parts[j]) for j in range(n)]
    return jnp.concatenate(parts, 0)


def per_device(queries, key_rows, value_rows, cotangent, out_weight, prot_blocks, last_fill, memory_slots):
    q, k, v, cot = queries[0], key_rows[0], value_rows[0], cotangent[0]
    tables = protein_tables(prot_blocks[0], last_fill[0])
    slots = memory_slots[0]
    tokens, width = q.shape
    nctx, nfam = lax.axis_size("ctx"), lax.axis_size("fam")
    me, fam = lax.axis_index("ctx"), lax.axis_index("fam")
    total = slots.shape[0]
    mine = total // nctx
    nb = tokens // BLK
    pairs = width // SPAN
    fgroups, bgroups = math.gcd(pairs, 2), math.gcd(pairs, 4)
    fcount, bcount = pairs // fgroups, pairs // bgroups
    step = fcount * SPAN
    shift = [(i, i + 1) for i in range(nctx - 1)]
    back = [(i + 1, i) for i in range(nctx - 1)]
    edge = tokens - W
    halos = []
    for i in range(fgroups):
        cols = slice(i * step, (i + 1) * step)
        halos.append(lax.ppermute(jnp.concatenate([k[edge:, cols], v[edge:, cols]], 1), "ctx", shift))
    own_slots = lax.dynamic_slice_in_dim(slots, me * mine, mine)
    pick = (own_slots[:, None] == jnp.arange(tokens, dtype=jnp.int32)[None, :]).astype(bf16)
    rows = jnp.concatenate([dot(pick, k, NN).astype(bf16), dot(pick, v, NN).astype(bf16)], 1)
    mem = gather_rows(rows, "ctx", me)
    grad_attn = dot(cot, out_weight, NT).astype(bf16)
    heads = me * tokens + jnp.arange(nb, dtype=jnp.int32) * BLK
    source = jnp.arange(total, dtype=jnp.int32) // mine * tokens + slots
    prot, first, left = token_info(jnp.concatenate([heads, source]), tables)
    lo = jnp.clip(first[:nb] - (me * tokens - W) // BLK, 0, nb + FAR)
    info = jnp.stack([lo, jnp.clip(left[:nb], 0, BLK)])
    seen = (left[nb:] > 0)[None, :] & (prot[None, nb:] < prot[:nb, None])
    bias = jnp.broadcast_to(jnp.where(seen, 0.0, NEG).astype(f32)[:, :, None], (nb, total, BLK))
    base = (0, pairs)
    att, saved = None, []
    for i in range(fgroups):
        att, pt, ga = forward(
            info, q, grad_attn, k, v, halos[i], halos[i], mem, mem, bias,
            i * fcount, fcount, base, (0, fcount), att)
        saved.append((pt, ga))
    core = me & 1
    half = width // 2
    mine_att = lax.dynamic_slice_in_dim(att, core * half, half, 1)
    your_att = lax.dynamic_slice_in_dim(att, (1 - core) * half, half, 1)
    sent = swap(dot(your_att, cot, TN).astype(bf16), "ctx", 1)
    kept = dot(mine_att, cot, TN)

    carry, dhs = None, []

    def run(i, carry):
        at = i * bcount
        j = at // fcount
        r = at - j * fcount
        pt, ga = saved[j]
        out = backward(
            q, pt, ga, k, v, halos[j], halos[j], mem, mem,
            at, bcount, base, (r, fcount + r), r, carry)
        return list(out[:4]), out[4]

    backs = []
    for i in range(bgroups):
        carry, dh = run(i, carry)
        backs.append(lax.ppermute(dh, "ctx", back))
    plane = nctx // 2
    total_w = kept + sent.astype(f32)
    total_w = exchange(total_w, "ctx", 1, me >> 1, plane)
    total_w = exchange(total_w, "fam", 0, fam, nfam)
    w = spread(total_w.astype(bf16), "fam", 0, fam, nfam)
    w = spread(w, "ctx", 1, me >> 1, plane)
    other = swap(w, "ctx", 1)
    scale = (nfam * nctx * tokens) ** -0.5
    upper = core != 0
    weight = jnp.concatenate([jnp.where(upper, other, w), jnp.where(upper, w, other)], 0).astype(f32) * scale
    dq, dko, dvo, dm = carry
    dmem = halve(dm.reshape(2, nctx, mine, width), "ctx", me).reshape(2 * mine, width).astype(bf16)
    dk, dv = finish(own_slots, dko, dvo, dmem, backs)
    return dq[None], dk[None], dv[None], weight


def solution(mesh):
    row = P("fam", "ctx", None)
    small = P("fam", None)
    return jax.shard_map(
        per_device,
        mesh=mesh,
        in_specs=(row, row, row, row, P(), small, small, small),
        out_specs=(row, row, row, P()),
        check_vma=False,
    )
```

```python
import functools
import math

import jax
import jax.numpy as jnp
from jax import lax
from jax.experimental import pallas as pl
from jax.experimental.pallas import tpu as pltpu
from jax.sharding import PartitionSpec as P


HEAD_DIM = 64
W = 512
BLK = 128
SPAN = 2 * HEAD_DIM
TWO = 2 * BLK
FAR = W // BLK
NEG = -1e30
NT = (((1,), (1,)), ((), ()))
NN = (((1,), (0,)), ((), ()))
TN = (((0,), (0,)), ((), ()))
f32 = jnp.float32
bf16 = jnp.bfloat16


def dot(a, b, dims):
    return lax.dot_general(a, b, dims, preferred_element_type=f32)


def by_head(x, first):
    zero = jnp.zeros_like(x)
    return jnp.concatenate([jnp.where(first, x, zero), jnp.where(first, zero, x)], 0)


def join_heads(x, first):
    return jnp.where(first, x[:BLK], x[BLK:])


def fill_keys(dst, halo, own, memory):
    h, o = halo.shape[0], own.shape[0]
    dst[0:h, :SPAN] = halo[...]
    dst[h : h + o, :SPAN] = own[...]
    dst[h + o :, :SPAN] = memory[...]


def forward_kernel(
    info_ref, q_ref, g_ref, ko_ref, vo_ref, kh_ref, vh_ref, km_ref, vm_ref, mb_ref, *rest, nb
):
    at_ref, pt, ga_ref, ke, ve = rest[-5:]
    ext = kh_ref.shape[0] + ko_ref.shape[0]
    fill_keys(ke, kh_ref, ko_ref, km_ref)
    fill_keys(ve, vh_ref, vo_ref, vm_ref)
    ve[:, SPAN:] = jnp.ones((ve.shape[0], SPAN), bf16)
    first = lax.broadcasted_iota(jnp.int32, (BLK, SPAN), 1) < HEAD_DIM
    tri = (
        lax.broadcasted_iota(jnp.int32, (BLK, TWO), 0)
        <= lax.broadcasted_iota(jnp.int32, (BLK, TWO), 1) % BLK
    )
    lane = lax.broadcasted_iota(jnp.int32, (TWO, SPAN), 1)
    row = lax.broadcasted_iota(jnp.int32, (TWO, SPAN), 0) % BLK
    for b in range(nb):
        rows, cols = slice(b * BLK, (b + 1) * BLK), slice(b * TWO, (b + 1) * TWO)
        band = slice(b * BLK, (b + FAR + 1) * BLK)
        q2 = by_head(q_ref[rows, :] * jnp.asarray(HEAD_DIM**-0.5, bf16), first)
        s = dot(ke[band, :], q2, NT)
        sm = dot(ke[ext:, :], q2, NT) + jnp.concatenate([mb_ref[b], mb_ref[b]], 1)
        lo = info_ref[0, b]
        off = [jnp.where(e + b >= lo, 0.0, NEG).astype(f32) for e in range(FAR)]
        ends = jnp.where(tri, s[FAR * BLK :, :], s[:BLK, :] + off[0])
        mid = [s[e * BLK : (e + 1) * BLK, :] for e in range(1, FAR)]
        m = jnp.maximum(jnp.max(ends, 0, keepdims=True), jnp.max(sm, 0, keepdims=True))
        for e in range(1, FAR):
            m = jnp.maximum(m, jnp.max(mid[e - 1], 0, keepdims=True) + off[e])
        p = jnp.exp(ends - m).astype(bf16)
        zero = jnp.zeros_like(p)
        pt[0, b * BLK : (b + 1) * BLK, cols] = jnp.where(tri, zero, p)
        pt[0, (b + FAR) * BLK : (b + FAR + 1) * BLK, cols] = jnp.where(tri, p, zero)
        for e in range(1, FAR):
            pt[0, (b + e) * BLK : (b + e + 1) * BLK, cols] = jnp.exp(
                mid[e - 1] - (m - off[e])
            ).astype(bf16)
        pt[0, ext:, cols] = jnp.exp(sm - m).astype(bf16)
        o = dot(pt[0, band, cols], ve[band, :], TN) + dot(pt[0, ext:, cols], ve[ext:, :], TN)
        scale = jnp.where(row < info_ref[1, b], 1.0 / o[:, SPAN:], 0.0)
        o = o[:, :SPAN] * scale
        at_ref[rows, :] = join_heads(o, first).astype(bf16)
        g2 = (by_head(g_ref[rows, :].astype(f32), first) * scale).astype(bf16)
        d = -jnp.sum(g2.astype(f32) * o, 1, keepdims=True)
        high = d.astype(bf16).astype(f32)
        ga_ref[0, cols, :SPAN] = g2
        ga_ref[0, cols, SPAN:] = jnp.where(
            lane == 0, high, jnp.where(lane == 1, d - high, 0.0)
        ).astype(bf16)


def backward_kernel(
    q_ref, pt_ref, ga_ref, ko_ref, vo_ref, kh_ref, vh_ref, km_ref, vm_ref, *rest, nb
):
    dq_ref, dko_ref, dvo_ref, dm_ref, dh_ref, ke, ve, q2, ds = rest[-9:]
    hrows, slots = kh_ref.shape[0], km_ref.shape[0]
    ext = hrows + ko_ref.shape[0]
    fill_keys(ke, kh_ref, ko_ref, km_ref)
    fill_keys(ve, vh_ref, vo_ref, vm_ref)
    ve[:, SPAN:] = jnp.ones((ve.shape[0], SPAN), bf16)
    first = lax.broadcasted_iota(jnp.int32, (BLK, SPAN), 1) < HEAD_DIM
    unit = HEAD_DIM**-0.5
    for b in range(nb):
        rows, cols = slice(b * BLK, (b + 1) * BLK), slice(b * TWO, (b + 1) * TWO)
        band = slice(b * BLK, (b + FAR + 1) * BLK)
        q2[cols, :] = by_head(q_ref[rows, :] * jnp.asarray(unit, bf16), first)
        ga = ga_ref[0, cols, :]
        dp = dot(ve[band, :], ga, NT)
        ds[band, cols] = (pt_ref[0, band, cols].astype(f32) * dp).astype(bf16)
        dp = dot(ve[ext:, :], ga, NT)
        ds[ext:, cols] = (pt_ref[0, ext:, cols].astype(f32) * dp).astype(bf16)
        dq = dot(ds[band, cols], ke[band, :], TN) + dot(ds[ext:, cols], ke[ext:, :], TN)
        dq_ref[rows, :] = (join_heads(dq, first) * unit).astype(bf16)
    for e in range(ext // BLK):
        cols = slice(max(0, e - FAR) * TWO, (min(nb - 1, e) + 1) * TWO)
        rows = slice(e * BLK, (e + 1) * BLK)
        dv = dot(pt_ref[0, rows, cols], ga_ref[0, cols, :SPAN], NN)
        dk = dot(ds[rows, cols], q2[cols, :], NN)
        if e * BLK < hrows:
            dh_ref[rows, :] = dk.astype(bf16)
            dh_ref[hrows + e * BLK : hrows + (e + 1) * BLK, :] = dv.astype(bf16)
        else:
            own = slice(e * BLK - hrows, (e + 1) * BLK - hrows)
            dko_ref[own, :] = dk
            dvo_ref[own, :] = dv
    dm_ref[:slots, :] = dot(ds[ext:, :], q2[...], NN).astype(bf16)
    dm_ref[slots:, :] = dot(pt_ref[0, ext:, :], ga_ref[0, :, :SPAN], NN).astype(bf16)


def columns(rows, start):
    return pl.BlockSpec((rows, SPAN), lambda p, *_: (0, p + start))


ANY = pl.BlockSpec(memory_space=pl.ANY)


def forward(info, q, g, ko, vo, kh, vh, km, vm, bias, start, count, base, halo_at, carry):
    tokens, width = q.shape
    slots, hrows, nb = km.shape[0], kh.shape[0], tokens // BLK
    keys = hrows + tokens + slots
    kc, vc = halo_at
    mk, mv = base
    args = [info, q, g, ko, vo, kh, vh, km, vm, bias]
    specs = [
        columns(tokens, start), columns(tokens, start), columns(tokens, start), columns(tokens, start),
        columns(hrows, kc), columns(hrows, vc), columns(slots, mk + start), columns(slots, mv + start),
        pl.BlockSpec(bias.shape, lambda p, *_: (0, 0, 0)),
    ]
    alias = {}
    if carry is not None:
        alias = {len(args): 0}
        args.append(carry)
        specs.append(ANY)
    return pl.pallas_call(
        functools.partial(forward_kernel, nb=nb),
        grid_spec=pltpu.PrefetchScalarGridSpec(
            num_scalar_prefetch=1,
            grid=(count,),
            in_specs=specs,
            out_specs=[
                columns(tokens, start),
                pl.BlockSpec((1, keys, nb * TWO), lambda p, *_: (p, 0, 0)),
                pl.BlockSpec((1, nb * TWO, 2 * SPAN), lambda p, *_: (p, 0, 0)),
            ],
            scratch_shapes=[pltpu.VMEM((keys, SPAN), bf16), pltpu.VMEM((keys, 2 * SPAN), bf16)],
        ),
        out_shape=[
            jax.ShapeDtypeStruct((tokens, width), bf16),
            jax.ShapeDtypeStruct((count, keys, nb * TWO), bf16),
            jax.ShapeDtypeStruct((count, nb * TWO, 2 * SPAN), bf16),
        ],
        input_output_aliases=alias,
        compiler_params=pltpu.CompilerParams(vmem_limit_bytes=60 << 20),
        cost_estimate=pl.CostEstimate(
            flops=count * nb * 12 * TWO * BLK * 1024, bytes_accessed=count * (4 << 20), transcendentals=count << 20
        ),
        name="band_forward",
    )(*args)


def backward(q, pt, ga, ko, vo, kh, vh, km, vm, start, count, base, halo_at, at, carry):
    tokens, width = q.shape
    slots, hrows, nb = km.shape[0], kh.shape[0], tokens // BLK
    keys = hrows + tokens + slots
    kc, vc = halo_at
    mk, mv = base
    args = [q, pt, ga, ko, vo, kh, vh, km, vm]
    specs = [
        columns(tokens, start),
        pl.BlockSpec((1, keys, nb * TWO), lambda p, *_: (p + at, 0, 0)),
        pl.BlockSpec((1, nb * TWO, 2 * SPAN), lambda p, *_: (p + at, 0, 0)),
        columns(tokens, start), columns(tokens, start),
        columns(hrows, kc), columns(hrows, vc), columns(slots, mk + start), columns(slots, mv + start),
    ]
    alias = {}
    if carry is not None:
        alias = {len(args) + i: i for i in range(len(carry))}
        args += carry
        specs += [ANY] * len(carry)
    return pl.pallas_call(
        functools.partial(backward_kernel, nb=nb),
        grid=(count,),
        in_specs=specs,
        out_specs=[
            columns(tokens, start), columns(tokens, start), columns(tokens, start),
            columns(2 * slots, start), columns(2 * hrows, 0),
        ],
        scratch_shapes=[
            pltpu.VMEM((keys, SPAN), bf16), pltpu.VMEM((keys, 2 * SPAN), bf16),
            pltpu.VMEM((nb * TWO, SPAN), bf16), pltpu.VMEM((keys, nb * TWO), bf16),
        ],
        out_shape=[
            jax.ShapeDtypeStruct((tokens, width), bf16),
            jax.ShapeDtypeStruct((tokens, width), f32),
            jax.ShapeDtypeStruct((tokens, width), f32),
            jax.ShapeDtypeStruct((2 * slots, width), bf16),
            jax.ShapeDtypeStruct((2 * hrows, count * SPAN), bf16),
        ],
        input_output_aliases=alias,
        compiler_params=pltpu.CompilerParams(vmem_limit_bytes=60 << 20),
        cost_estimate=pl.CostEstimate(
            flops=count * nb * 20 * TWO * BLK * 1024, bytes_accessed=count * (6 << 20), transcendentals=0
        ),
        name="band_backward",
    )(*args)


def finish_kernel(slot_ref, dk_in, dv_in, mk_ref, mv_ref, *rest):
    backs, (dk_ref, dv_ref) = rest[:-2], rest[-2:]
    tokens = dk_in.shape[0]
    mine = slot_ref.shape[1]
    pick = (lax.broadcasted_iota(jnp.int32, (tokens, mine), 0) == slot_ref[...]).astype(f32).astype(bf16)
    dk = dk_in[...] + dot(pick, mk_ref[...], NN)
    dv = dv_in[...] + dot(pick, mv_ref[...], NN)
    edge = tokens - W
    for i, back in enumerate(backs):

        @pl.when(pl.program_id(0) == i)
        def _():
            dk_ref[edge:, :] = (dk[edge:] + back[:W, :].astype(f32)).astype(bf16)
            dv_ref[edge:, :] = (dv[edge:] + back[W:, :].astype(f32)).astype(bf16)


def finish(slots, dko, dvo, dmem, backs):
    tokens, width = dko.shape
    mine, n = slots.shape[0], len(backs)
    step = width // n
    col = lambda r, j: pl.BlockSpec((r, step), lambda i: (j, i))
    return pl.pallas_call(
        finish_kernel,
        grid=(n,),
        in_specs=[pl.BlockSpec((1, mine), lambda i: (0, 0)), col(tokens, 0), col(tokens, 0), col(mine, 0), col(mine, 1)]
        + [pl.BlockSpec((2 * W, step), lambda i: (0, 0))] * n,
        out_specs=[col(tokens, 0), col(tokens, 0)],
        out_shape=[jax.ShapeDtypeStruct((tokens, width), bf16)] * 2,
        compiler_params=pltpu.CompilerParams(vmem_limit_bytes=60 << 20),
        cost_estimate=pl.CostEstimate(flops=1 << 26, bytes_accessed=8 << 20, transcendentals=0),
        name="finish_rows",
    )(slots[None, :], dko, dvo, dmem, dmem, *backs)


def protein_tables(prot_blocks, last_fill):
    prot_ends = jnp.cumsum(prot_blocks)
    starts = prot_ends - prot_blocks
    valid_len = (prot_blocks - 1) * BLK + last_fill
    return prot_ends, starts, valid_len


def token_info(positions, tables):
    prot_ends, starts, valid_len = tables
    count = prot_ends.shape[0]
    blocks = jnp.floor_divide(positions, BLK)
    protein = jnp.sum((blocks[:, None] >= prot_ends[None, :]).astype(jnp.int32), axis=1)
    onehot = protein[:, None] == jnp.arange(count, dtype=jnp.int32)[None, :]
    first = jnp.sum(jnp.where(onehot, starts[None, :], 0), axis=1)
    length = jnp.sum(jnp.where(onehot, valid_len[None, :], 0), axis=1)
    return protein, first, length - (positions - first * BLK)


def swap(x, axis, bits):
    return lax.ppermute(x, axis, [(i, i ^ bits) for i in range(lax.axis_size(axis))])


def bits_of(n):
    out, b = [], 1
    while b < n:
        out.append(b)
        b *= 2
    return out


def gather_rows(x, axis, me):
    for bit in bits_of(lax.axis_size(axis)):
        other = swap(x, axis, bit)
        upper = (me & bit) != 0
        x = jnp.where(upper, jnp.concatenate([other, x], 0), jnp.concatenate([x, other], 0))
    return x


def halve(x, axis, me):
    for bit in bits_of(lax.axis_size(axis)):
        lead, n = x.shape[0], x.shape[1]
        x = x.reshape(lead, n // 2, 2, *x.shape[2:])
        upper = (me & bit) != 0
        keep = jnp.where(upper, x[:, :, 1], x[:, :, 0])
        send = jnp.where(upper, x[:, :, 0], x[:, :, 1])
        x = keep.astype(f32) + swap(send.astype(bf16), axis, bit).astype(f32)
    return x


def exchange(parts, axis, shift, me, n):
    rows = parts.shape[0] // n
    part = lambda j: lax.dynamic_slice_in_dim(parts, j * rows, rows)
    got = [swap(part(me ^ k).astype(bf16), axis, k << shift) for k in range(1, n)]
    return sum([g.astype(f32) for g in got], part(me).astype(f32))


def spread(x, axis, shift, me, n):
    parts = [x] + [swap(x, axis, k << shift) for k in range(1, n)]
    for bit in bits_of(n):
        upper = (me & bit) != 0
        parts = [jnp.where(upper, parts[j ^ bit], parts[j]) for j in range(n)]
    return jnp.concatenate(parts, 0)


def per_device(queries, key_rows, value_rows, cotangent, out_weight, prot_blocks, last_fill, memory_slots):
    q, k, v, cot = queries[0], key_rows[0], value_rows[0], cotangent[0]
    tables = protein_tables(prot_blocks[0], last_fill[0])
    slots = memory_slots[0]
    tokens, width = q.shape
    nctx, nfam = lax.axis_size("ctx"), lax.axis_size("fam")
    me, fam = lax.axis_index("ctx"), lax.axis_index("fam")
    total = slots.shape[0]
    mine = total // nctx
    nb = tokens // BLK
    pairs = width // SPAN
    fgroups, bgroups = math.gcd(pairs, 2), math.gcd(pairs, 4)
    fcount, bcount = pairs // fgroups, pairs // bgroups
    step = fcount * SPAN
    shift = [(i, i + 1) for i in range(nctx - 1)]
    back = [(i + 1, i) for i in range(nctx - 1)]
    edge = tokens - W
    halos = []
    for i in range(fgroups):
        cols = slice(i * step, (i + 1) * step)
        halos.append(lax.ppermute(jnp.concatenate([k[edge:, cols], v[edge:, cols]], 1), "ctx", shift))
    own_slots = lax.dynamic_slice_in_dim(slots, me * mine, mine)
    pick = (own_slots[:, None] == jnp.arange(tokens, dtype=jnp.int32)[None, :]).astype(bf16)
    rows = jnp.concatenate([dot(pick, k, NN).astype(bf16), dot(pick, v, NN).astype(bf16)], 1)
    mem = gather_rows(rows, "ctx", me)
    grad_attn = dot(cot, out_weight, NT).astype(bf16)
    heads = me * tokens + jnp.arange(nb, dtype=jnp.int32) * BLK
    source = jnp.arange(total, dtype=jnp.int32) // mine * tokens + slots
    prot, first, left = token_info(jnp.concatenate([heads, source]), tables)
    lo = jnp.clip(first[:nb] - (me * tokens - W) // BLK, 0, nb + FAR)
    info = jnp.stack([lo, jnp.clip(left[:nb], 0, BLK)])
    seen = (left[nb:] > 0)[None, :] & (prot[None, nb:] < prot[:nb, None])
    bias = jnp.broadcast_to(jnp.where(seen, 0.0, NEG).astype(f32)[:, :, None], (nb, total, BLK))
    base = (0, pairs)
    att, saved = None, []
    for i in range(fgroups):
        att, pt, ga = forward(
            info, q, grad_attn, k, v, halos[i], halos[i], mem, mem, bias,
            i * fcount, fcount, base, (0, fcount), att)
        saved.append((pt, ga))
    core = me & 1
    half = width // 2
    mine_att = lax.dynamic_slice_in_dim(att, core * half, half, 1)
    your_att = lax.dynamic_slice_in_dim(att, (1 - core) * half, half, 1)
    sent = swap(dot(your_att, cot, TN).astype(bf16), "ctx", 1)
    kept = dot(mine_att, cot, TN)

    carry = None

    def run(i, carry):
        at = i * bcount
        j = at // fcount
        r = at - j * fcount
        pt, ga = saved[j]
        out = backward(
            q, pt, ga, k, v, halos[j], halos[j], mem, mem,
            at, bcount, base, (r, fcount + r), r, carry)
        return list(out[:4]), out[4]

    backs = []
    for i in range(bgroups):
        carry, dh = run(i, carry)
        backs.append(lax.ppermute(dh, "ctx", back))
    plane = nctx // 2
    total_w = kept + sent.astype(f32)
    total_w = exchange(total_w, "ctx", 1, me >> 1, plane)
    total_w = exchange(total_w, "fam", 0, fam, nfam)
    w = spread(total_w.astype(bf16), "fam", 0, fam, nfam)
    w = spread(w, "ctx", 1, me >> 1, plane)
    other = swap(w, "ctx", 1)
    scale = (nfam * nctx * tokens) ** -0.5
    upper = core != 0
    weight = jnp.concatenate([jnp.where(upper, other, w), jnp.where(upper, w, other)], 0).astype(f32) * scale
    dq, dko, dvo, dm = carry
    dmem = halve(dm.reshape(2, nctx, mine, width), "ctx", me).reshape(2 * mine, width).astype(bf16)
    dk, dv = finish(own_slots, dko, dvo, dmem, backs)
    return dq[None], dk[None], dv[None], weight


def solution(mesh):
    row = P("fam", "ctx", None)
    small = P("fam", None)

    return jax.shard_map(
        per_device,
        mesh=mesh,
        in_specs=(row, row, row, row, P(), small, small, small),
        out_specs=(row, row, row, P()),
        check_vma=False,
    )
```

```python
import functools

import jax
import jax.numpy as jnp
from jax import lax
from jax.experimental import pallas as pl
from jax.experimental.pallas import tpu as pltpu
from jax.sharding import PartitionSpec as P


HEAD_DIM = 64
W = 512
BLK = 128
SPAN = 2 * HEAD_DIM
TWO = 2 * BLK
FAR = W // BLK
NEG = -1e30
NT = (((1,), (1,)), ((), ()))
NN = (((1,), (0,)), ((), ()))
TN = (((0,), (0,)), ((), ()))
f32 = jnp.float32
bf16 = jnp.bfloat16


def dot(a, b, dims):
    return lax.dot_general(a, b, dims, preferred_element_type=f32)


def by_head(x, first):
    zero = jnp.zeros_like(x)
    return jnp.concatenate([jnp.where(first, x, zero), jnp.where(first, zero, x)], 0)


def join_heads(x, first):
    return jnp.where(first, x[:BLK], x[BLK:])


def fill_keys(dst, halo, own, memory):
    h, o = halo.shape[0], own.shape[0]
    dst[0:h, :SPAN] = halo[...]
    dst[h : h + o, :SPAN] = own[...]
    dst[h + o :, :SPAN] = memory[...]


def forward_kernel(
    info_ref, q_ref, g_ref, ko_ref, vo_ref, kh_ref, vh_ref, km_ref, vm_ref, mb_ref, *rest, nb
):
    at_ref, pt, ga_ref, ke, ve = rest[-5:]
    ext = kh_ref.shape[0] + ko_ref.shape[0]
    fill_keys(ke, kh_ref, ko_ref, km_ref)
    fill_keys(ve, vh_ref, vo_ref, vm_ref)
    ve[:, SPAN:] = jnp.ones((ve.shape[0], SPAN), bf16)
    first = lax.broadcasted_iota(jnp.int32, (BLK, SPAN), 1) < HEAD_DIM
    tri = (
        lax.broadcasted_iota(jnp.int32, (BLK, TWO), 0)
        <= lax.broadcasted_iota(jnp.int32, (BLK, TWO), 1) % BLK
    )
    lane = lax.broadcasted_iota(jnp.int32, (TWO, SPAN), 1)
    row = lax.broadcasted_iota(jnp.int32, (TWO, SPAN), 0) % BLK
    for b in range(nb):
        rows, cols = slice(b * BLK, (b + 1) * BLK), slice(b * TWO, (b + 1) * TWO)
        band = slice(b * BLK, (b + FAR + 1) * BLK)
        q2 = by_head(q_ref[rows, :] * jnp.asarray(HEAD_DIM**-0.5, bf16), first)
        s = dot(ke[band, :], q2, NT)
        sm = dot(ke[ext:, :], q2, NT) + jnp.concatenate([mb_ref[b], mb_ref[b]], 1)
        lo = info_ref[0, b]
        off = [jnp.where(e + b >= lo, 0.0, NEG).astype(f32) for e in range(FAR)]
        ends = jnp.where(tri, s[FAR * BLK :, :], s[:BLK, :] + off[0])
        mid = [s[e * BLK : (e + 1) * BLK, :] for e in range(1, FAR)]
        m = jnp.maximum(jnp.max(ends, 0, keepdims=True), jnp.max(sm, 0, keepdims=True))
        for e in range(1, FAR):
            m = jnp.maximum(m, jnp.max(mid[e - 1], 0, keepdims=True) + off[e])
        p = jnp.exp(ends - m).astype(bf16)
        zero = jnp.zeros_like(p)
        pt[0, b * BLK : (b + 1) * BLK, cols] = jnp.where(tri, zero, p)
        pt[0, (b + FAR) * BLK : (b + FAR + 1) * BLK, cols] = jnp.where(tri, p, zero)
        for e in range(1, FAR):
            pt[0, (b + e) * BLK : (b + e + 1) * BLK, cols] = jnp.exp(
                mid[e - 1] - (m - off[e])
            ).astype(bf16)
        pt[0, ext:, cols] = jnp.exp(sm - m).astype(bf16)
        o = dot(pt[0, band, cols], ve[band, :], TN) + dot(pt[0, ext:, cols], ve[ext:, :], TN)
        scale = jnp.where(row < info_ref[1, b], 1.0 / o[:, SPAN:], 0.0)
        o = o[:, :SPAN] * scale
        at_ref[rows, :] = join_heads(o, first).astype(bf16)
        g2 = (by_head(g_ref[rows, :].astype(f32), first) * scale).astype(bf16)
        d = -jnp.sum(g2.astype(f32) * o, 1, keepdims=True)
        high = d.astype(bf16).astype(f32)
        ga_ref[0, cols, :SPAN] = g2
        ga_ref[0, cols, SPAN:] = jnp.where(
            lane == 0, high, jnp.where(lane == 1, d - high, 0.0)
        ).astype(bf16)


def backward_kernel(
    q_ref, pt_ref, ga_ref, ko_ref, vo_ref, kh_ref, vh_ref, km_ref, vm_ref, *rest, nb
):
    dq_ref, dko_ref, dvo_ref, dm_ref, dh_ref, ke, ve, q2, ds = rest[-9:]
    hrows, slots = kh_ref.shape[0], km_ref.shape[0]
    ext = hrows + ko_ref.shape[0]
    fill_keys(ke, kh_ref, ko_ref, km_ref)
    fill_keys(ve, vh_ref, vo_ref, vm_ref)
    ve[:, SPAN:] = jnp.ones((ve.shape[0], SPAN), bf16)
    first = lax.broadcasted_iota(jnp.int32, (BLK, SPAN), 1) < HEAD_DIM
    unit = HEAD_DIM**-0.5
    for b in range(nb):
        rows, cols = slice(b * BLK, (b + 1) * BLK), slice(b * TWO, (b + 1) * TWO)
        band = slice(b * BLK, (b + FAR + 1) * BLK)
        q2[cols, :] = by_head(q_ref[rows, :] * jnp.asarray(unit, bf16), first)
        ga = ga_ref[0, cols, :]
        dp = dot(ve[band, :], ga, NT)
        ds[band, cols] = (pt_ref[0, band, cols].astype(f32) * dp).astype(bf16)
        dp = dot(ve[ext:, :], ga, NT)
        ds[ext:, cols] = (pt_ref[0, ext:, cols].astype(f32) * dp).astype(bf16)
        dq = dot(ds[band, cols], ke[band, :], TN) + dot(ds[ext:, cols], ke[ext:, :], TN)
        dq_ref[rows, :] = (join_heads(dq, first) * unit).astype(bf16)
    for e in range(ext // BLK):
        cols = slice(max(0, e - FAR) * TWO, (min(nb - 1, e) + 1) * TWO)
        rows = slice(e * BLK, (e + 1) * BLK)
        dv = dot(pt_ref[0, rows, cols], ga_ref[0, cols, :SPAN], NN)
        dk = dot(ds[rows, cols], q2[cols, :], NN)
        if e * BLK < hrows:
            dh_ref[rows, :] = dk.astype(bf16)
            dh_ref[hrows + e * BLK : hrows + (e + 1) * BLK, :] = dv.astype(bf16)
        else:
            own = slice(e * BLK - hrows, (e + 1) * BLK - hrows)
            dko_ref[own, :] = dk
            dvo_ref[own, :] = dv
    dm_ref[:slots, :] = dot(ds[ext:, :], q2[...], NN).astype(bf16)
    dm_ref[slots:, :] = dot(pt_ref[0, ext:, :], ga_ref[0, :, :SPAN], NN).astype(bf16)


def columns(rows, start):
    return pl.BlockSpec((rows, SPAN), lambda p, *_: (0, p + start))


ANY = pl.BlockSpec(memory_space=pl.ANY)


def forward(info, q, g, ko, vo, kh, vh, km, vm, bias, start, count, base, halo_at, carry):
    tokens, width = q.shape
    slots, hrows, nb = km.shape[0], kh.shape[0], tokens // BLK
    keys = hrows + tokens + slots
    kc, vc = halo_at
    mk, mv = base
    args = [info, q, g, ko, vo, kh, vh, km, vm, bias]
    specs = [
        columns(tokens, start), columns(tokens, start), columns(tokens, start), columns(tokens, start),
        columns(hrows, kc), columns(hrows, vc), columns(slots, mk + start), columns(slots, mv + start),
        pl.BlockSpec(bias.shape, lambda p, *_: (0, 0, 0)),
    ]
    alias = {}
    if carry is not None:
        alias = {len(args): 0}
        args.append(carry)
        specs.append(ANY)
    return pl.pallas_call(
        functools.partial(forward_kernel, nb=nb),
        grid_spec=pltpu.PrefetchScalarGridSpec(
            num_scalar_prefetch=1,
            grid=(count,),
            in_specs=specs,
            out_specs=[
                columns(tokens, start),
                pl.BlockSpec((1, keys, nb * TWO), lambda p, *_: (p, 0, 0)),
                pl.BlockSpec((1, nb * TWO, 2 * SPAN), lambda p, *_: (p, 0, 0)),
            ],
            scratch_shapes=[pltpu.VMEM((keys, SPAN), bf16), pltpu.VMEM((keys, 2 * SPAN), bf16)],
        ),
        out_shape=[
            jax.ShapeDtypeStruct((tokens, width), bf16),
            jax.ShapeDtypeStruct((count, keys, nb * TWO), bf16),
            jax.ShapeDtypeStruct((count, nb * TWO, 2 * SPAN), bf16),
        ],
        input_output_aliases=alias,
        compiler_params=pltpu.CompilerParams(vmem_limit_bytes=67_000_000),
        cost_estimate=pl.CostEstimate(
            flops=count * nb * 12 * TWO * BLK * 1024, bytes_accessed=count * (4 << 20), transcendentals=count << 20
        ),
        name="band_forward",
    )(*args)


def backward(q, pt, ga, ko, vo, kh, vh, km, vm, start, count, base, halo_at, at, carry, dh_total, dh_at):
    tokens, width = q.shape
    slots, hrows, nb = km.shape[0], kh.shape[0], tokens // BLK
    keys = hrows + tokens + slots
    kc, vc = halo_at
    mk, mv = base
    args = [q, pt, ga, ko, vo, kh, vh, km, vm]
    specs = [
        columns(tokens, start),
        pl.BlockSpec((1, keys, nb * TWO), lambda p, *_: (p + at, 0, 0)),
        pl.BlockSpec((1, nb * TWO, 2 * SPAN), lambda p, *_: (p + at, 0, 0)),
        columns(tokens, start), columns(tokens, start),
        columns(hrows, kc), columns(hrows, vc), columns(slots, mk + start), columns(slots, mv + start),
    ]
    alias = {}
    if carry is not None:
        alias = {len(args) + i: i for i in range(len(carry))}
        args += carry
        specs += [ANY] * len(carry)
    return pl.pallas_call(
        functools.partial(backward_kernel, nb=nb),
        grid=(count,),
        in_specs=specs,
        out_specs=[
            columns(tokens, start), columns(tokens, start), columns(tokens, start),
            columns(2 * slots, start), columns(2 * hrows, dh_at),
        ],
        scratch_shapes=[
            pltpu.VMEM((keys, SPAN), bf16), pltpu.VMEM((keys, 2 * SPAN), bf16),
            pltpu.VMEM((nb * TWO, SPAN), bf16), pltpu.VMEM((keys, nb * TWO), bf16),
        ],
        out_shape=[
            jax.ShapeDtypeStruct((tokens, width), bf16),
            jax.ShapeDtypeStruct((tokens, width), f32),
            jax.ShapeDtypeStruct((tokens, width), f32),
            jax.ShapeDtypeStruct((2 * slots, width), bf16),
            jax.ShapeDtypeStruct((2 * hrows, dh_total * SPAN), bf16),
        ],
        input_output_aliases=alias,
        compiler_params=pltpu.CompilerParams(vmem_limit_bytes=67_000_000),
        cost_estimate=pl.CostEstimate(
            flops=count * nb * 20 * TWO * BLK * 1024, bytes_accessed=count * (6 << 20), transcendentals=0
        ),
        name="band_backward",
    )(*args)


def finish_kernel(slot_ref, dk_in, dv_in, mk_ref, mv_ref, *rest, groups):
    backs, (dk_ref, dv_ref) = rest[:-2], rest[-2:]
    tokens = dk_in.shape[0]
    mine = slot_ref.shape[1]
    pick = (lax.broadcasted_iota(jnp.int32, (tokens, mine), 0) == slot_ref[...]).astype(f32).astype(bf16)
    dk = dk_in[...] + dot(pick, mk_ref[...], NN)
    dv = dv_in[...] + dot(pick, mv_ref[...], NN)
    edge = tokens - W
    if edge:
        dk_ref[:edge, :] = dk[:edge].astype(bf16)
        dv_ref[:edge, :] = dv[:edge].astype(bf16)
    pair = pl.program_id(0)
    for back, (at, count) in zip(backs, groups):

        @pl.when((pair >= at) & (pair < at + count))
        def _():
            dk_ref[edge:, :] = (dk[edge:] + back[:W, :].astype(f32)).astype(bf16)
            dv_ref[edge:, :] = (dv[edge:] + back[W:, :].astype(f32)).astype(bf16)


def finish(slots, dko, dvo, dmem, backs, groups):
    tokens, width = dko.shape
    mine = slots.shape[0]

    def back_columns(at, count):
        return pl.BlockSpec((2 * W, SPAN), lambda p: (0, jnp.clip(p - at, 0, count - 1)))

    col = lambda rows, j: pl.BlockSpec((rows, SPAN), lambda p: (j, p))
    return pl.pallas_call(
        functools.partial(finish_kernel, groups=groups),
        grid=(width // SPAN,),
        in_specs=[pl.BlockSpec((1, mine), lambda p: (0, 0)), col(tokens, 0), col(tokens, 0), col(mine, 0), col(mine, 1)]
        + [back_columns(*g) for g in groups],
        out_specs=[col(tokens, 0), col(tokens, 0)],
        out_shape=[jax.ShapeDtypeStruct((tokens, width), bf16)] * 2,
        compiler_params=pltpu.CompilerParams(vmem_limit_bytes=67_000_000),
        cost_estimate=pl.CostEstimate(flops=1 << 26, bytes_accessed=8 << 20, transcendentals=0),
        name="finish_rows",
    )(slots[None, :], dko, dvo, dmem, dmem, *backs)


def protein_tables(prot_blocks, last_fill):
    prot_ends = jnp.cumsum(prot_blocks)
    starts = prot_ends - prot_blocks
    valid_len = (prot_blocks - 1) * BLK + last_fill
    return prot_ends, starts, valid_len


def token_info(positions, tables):
    prot_ends, starts, valid_len = tables
    count = prot_ends.shape[0]
    blocks = jnp.floor_divide(positions, BLK)
    protein = jnp.sum((blocks[:, None] >= prot_ends[None, :]).astype(jnp.int32), axis=1)
    onehot = protein[:, None] == jnp.arange(count, dtype=jnp.int32)[None, :]
    first = jnp.sum(jnp.where(onehot, starts[None, :], 0), axis=1)
    length = jnp.sum(jnp.where(onehot, valid_len[None, :], 0), axis=1)
    return protein, first, length - (positions - first * BLK)


def swap(x, axis, bits):
    return lax.ppermute(x, axis, [(i, i ^ bits) for i in range(lax.axis_size(axis))])


def bits_of(n):
    out, b = [], 1
    while b < n:
        out.append(b)
        b *= 2
    return out


def gather_rows(x, axis, me):
    for bit in bits_of(lax.axis_size(axis)):
        other = swap(x, axis, bit)
        upper = (me & bit) != 0
        x = jnp.where(upper, jnp.concatenate([other, x], 0), jnp.concatenate([x, other], 0))
    return x


def halve(x, axis, me):
    for bit in bits_of(lax.axis_size(axis)):
        lead, n = x.shape[0], x.shape[1]
        x = x.reshape(lead, n // 2, 2, *x.shape[2:])
        upper = (me & bit) != 0
        keep = jnp.where(upper, x[:, :, 1], x[:, :, 0])
        send = jnp.where(upper, x[:, :, 0], x[:, :, 1])
        x = keep.astype(f32) + swap(send.astype(bf16), axis, bit).astype(f32)
    return x


def exchange(parts, axis, shift, me, n):
    rows = parts.shape[0] // n
    part = lambda j: lax.dynamic_slice_in_dim(parts, j * rows, rows)
    got = [swap(part(me ^ k).astype(bf16), axis, k << shift) for k in range(1, n)]
    return sum([g.astype(f32) for g in got], part(me).astype(f32))


def spread(x, axis, shift, me, n):
    parts = [x] + [swap(x, axis, k << shift) for k in range(1, n)]
    for bit in bits_of(n):
        upper = (me & bit) != 0
        parts = [jnp.where(upper, parts[j ^ bit], parts[j]) for j in range(n)]
    return jnp.concatenate(parts, 0)


def groups_of(pairs):
    if pairs % 8:
        return [pairs], [(0, 0, pairs)], [pairs]
    u = pairs // 8
    return [u, 3 * u, 4 * u], [(0, 0, u), (1, 0, 3 * u), (2, 0, 2 * u), (2, 2 * u, 2 * u)], [4 * u, 2 * u, 2 * u]


def per_device(queries, key_rows, value_rows, cotangent, out_weight, prot_blocks, last_fill, memory_slots):
    q, k, v, cot = queries[0], key_rows[0], value_rows[0], cotangent[0]
    tables = protein_tables(prot_blocks[0], last_fill[0])
    slots = memory_slots[0]
    tokens, width = q.shape
    nctx, nfam = lax.axis_size("ctx"), lax.axis_size("fam")
    me, fam = lax.axis_index("ctx"), lax.axis_index("fam")
    total = slots.shape[0]
    mine = total // nctx
    nb = tokens // BLK
    pairs = width // SPAN
    fsizes, bplan, dhs = groups_of(pairs)
    fstarts = [sum(fsizes[:i]) for i in range(len(fsizes))]
    shift = [(i, i + 1) for i in range(nctx - 1)]
    back = [(i + 1, i) for i in range(nctx - 1)]
    edge = tokens - W
    halos = []
    for i, (at, count) in enumerate(zip(fstarts, fsizes)):
        cols = slice(at * SPAN, (at + count) * SPAN)
        halos.append(lax.ppermute(jnp.concatenate([k[edge:, cols], v[edge:, cols]], 1), "ctx", shift))
    own_slots = lax.dynamic_slice_in_dim(slots, me * mine, mine)
    pick = (own_slots[:, None] == jnp.arange(tokens, dtype=jnp.int32)[None, :]).astype(bf16)
    rows = jnp.concatenate([dot(pick, k, NN).astype(bf16), dot(pick, v, NN).astype(bf16)], 1)
    mem = gather_rows(rows, "ctx", me)
    grad_attn = dot(cot, out_weight, NT).astype(bf16)
    heads = me * tokens + jnp.arange(nb, dtype=jnp.int32) * BLK
    source = jnp.arange(total, dtype=jnp.int32) // mine * tokens + slots
    prot, first, left = token_info(jnp.concatenate([heads, source]), tables)
    lo = jnp.clip(first[:nb] - (me * tokens - W) // BLK, 0, nb + FAR)
    info = jnp.stack([lo, jnp.clip(left[:nb], 0, BLK)])
    seen = (left[nb:] > 0)[None, :] & (prot[None, nb:] < prot[:nb, None])
    bias = jnp.broadcast_to(jnp.where(seen, 0.0, NEG).astype(f32)[:, :, None], (nb, total, BLK))
    base = (0, pairs)
    att, saved = None, []
    for i, (at, count) in enumerate(zip(fstarts, fsizes)):
        att, pt, ga = forward(
            info, q, grad_attn, k, v, halos[i], halos[i], mem, mem, bias,
            at, count, base, (0, count), att)
        saved.append((pt, ga))
    core = me & 1
    half = width // 2
    mine_att = lax.dynamic_slice_in_dim(att, core * half, half, 1)
    your_att = lax.dynamic_slice_in_dim(att, (1 - core) * half, half, 1)
    sent = swap(dot(your_att, cot, TN).astype(bf16), "ctx", 1)
    kept = dot(mine_att, cot, TN)

    carry, backs, i = [], [], 0
    for total_dh in dhs:
        done = 0
        while done < total_dh:
            j, r, count = bplan[i]
            pt, ga = saved[j]
            out = backward(
                q, pt, ga, k, v, halos[j], halos[j], mem, mem, fstarts[j] + r, count,
                base, (r, fsizes[j] + r), r, carry, total_dh, done)
            carry = list(out)
            done, i = done + count, i + 1
        backs.append(lax.ppermute(carry.pop(), "ctx", back))
    plane = nctx // 2
    total_w = kept + sent.astype(f32)
    total_w = exchange(total_w, "ctx", 1, me >> 1, plane)
    total_w = exchange(total_w, "fam", 0, fam, nfam)
    w = spread(total_w.astype(bf16), "fam", 0, fam, nfam)
    w = spread(w, "ctx", 1, me >> 1, plane)
    other = swap(w, "ctx", 1)
    scale = (nfam * nctx * tokens) ** -0.5
    upper = core != 0
    weight = jnp.concatenate([jnp.where(upper, other, w), jnp.where(upper, w, other)], 0).astype(f32) * scale
    dq, dko, dvo, dm = carry
    dmem = halve(dm.reshape(2, nctx, mine, width), "ctx", me).reshape(2 * mine, width).astype(bf16)
    dk, dv = finish(
        own_slots, dko, dvo, dmem, backs, [(sum(dhs[:i]), n) for i, n in enumerate(dhs)])
    return dq[None], dk[None], dv[None], weight


def solution(mesh):
    row = P("fam", "ctx", None)
    small = P("fam", None)

    return jax.shard_map(
        per_device,
        mesh=mesh,
        in_specs=(row, row, row, row, P(), small, small, small),
        out_specs=(row, row, row, P()),
        check_vma=False,
    )
```

```python
import functools

import jax
import jax.numpy as jnp
from jax import lax
from jax.experimental import pallas as pl
from jax.experimental.pallas import tpu as pltpu
from jax.sharding import PartitionSpec as P


HEAD_DIM = 64
W = 512
BLK = 128
SPAN = 2 * HEAD_DIM
TWO = 2 * BLK
FAR = W // BLK
NEG = -1e30
NT = (((1,), (1,)), ((), ()))
NN = (((1,), (0,)), ((), ()))
TN = (((0,), (0,)), ((), ()))
f32 = jnp.float32
bf16 = jnp.bfloat16


def dot(a, b, dims):
    return lax.dot_general(a, b, dims, preferred_element_type=f32)


def by_head(x, first):
    zero = jnp.zeros_like(x)
    return jnp.concatenate([jnp.where(first, x, zero), jnp.where(first, zero, x)], 0)


def join_heads(x, first):
    return jnp.where(first, x[:BLK], x[BLK:])


def fill_keys(dst, halo, own, memory):
    h, o = halo.shape[0], own.shape[0]
    dst[0:h, :SPAN] = halo[...]
    dst[h : h + o, :SPAN] = own[...]
    dst[h + o :, :SPAN] = memory[...]


def forward_kernel(
    info_ref, q_ref, g_ref, ko_ref, vo_ref, kh_ref, vh_ref, km_ref, vm_ref, mb_ref, *rest, nb, members
):
    at_ref, dm_ref, pt, ga_ref, ke, ve, q2s, pm = rest[-8:]
    slots = km_ref.shape[0]
    mine = slots // members
    ext = kh_ref.shape[0] + ko_ref.shape[0]
    fill_keys(ke, kh_ref, ko_ref, km_ref)
    fill_keys(ve, vh_ref, vo_ref, vm_ref)
    ve[:, SPAN:] = jnp.ones((ve.shape[0], SPAN), bf16)
    first = lax.broadcasted_iota(jnp.int32, (BLK, SPAN), 1) < HEAD_DIM
    tri = (
        lax.broadcasted_iota(jnp.int32, (BLK, TWO), 0)
        <= lax.broadcasted_iota(jnp.int32, (BLK, TWO), 1) % BLK
    )
    lane = lax.broadcasted_iota(jnp.int32, (TWO, SPAN), 1)
    row = lax.broadcasted_iota(jnp.int32, (TWO, SPAN), 0) % BLK
    for b in range(nb):
        rows, cols = slice(b * BLK, (b + 1) * BLK), slice(b * TWO, (b + 1) * TWO)
        band = slice(b * BLK, (b + FAR + 1) * BLK)
        q2 = by_head(q_ref[rows, :] * jnp.asarray(HEAD_DIM**-0.5, bf16), first)
        q2s[cols, :] = q2
        s = dot(ke[band, :], q2, NT)
        sm = dot(ke[ext:, :], q2, NT) + jnp.concatenate([mb_ref[b], mb_ref[b]], 1)
        lo = info_ref[0, b]
        off = [jnp.where(e + b >= lo, 0.0, NEG).astype(f32) for e in range(FAR)]
        ends = jnp.where(tri, s[FAR * BLK :, :], s[:BLK, :] + off[0])
        mid = [s[e * BLK : (e + 1) * BLK, :] for e in range(1, FAR)]
        m = jnp.maximum(jnp.max(ends, 0, keepdims=True), jnp.max(sm, 0, keepdims=True))
        for e in range(1, FAR):
            m = jnp.maximum(m, jnp.max(mid[e - 1], 0, keepdims=True) + off[e])
        p = jnp.exp(ends - m).astype(bf16)
        zero = jnp.zeros_like(p)
        pt[0, b * BLK : (b + 1) * BLK, cols] = jnp.where(tri, zero, p)
        pt[0, (b + FAR) * BLK : (b + FAR + 1) * BLK, cols] = jnp.where(tri, p, zero)
        for e in range(1, FAR):
            pt[0, (b + e) * BLK : (b + e + 1) * BLK, cols] = jnp.exp(
                mid[e - 1] - (m - off[e])
            ).astype(bf16)
        pm[:, cols] = jnp.exp(sm - m).astype(bf16)
        o = dot(pt[0, band, cols], ve[band, :], TN) + dot(pm[:, cols], ve[ext:, :], TN)
        scale = jnp.where(row < info_ref[1, b], 1.0 / o[:, SPAN:], 0.0)
        o = o[:, :SPAN] * scale
        at_ref[rows, :] = join_heads(o, first).astype(bf16)
        g2 = (by_head(g_ref[rows, :].astype(f32), first) * scale).astype(bf16)
        d = -jnp.sum(g2.astype(f32) * o, 1, keepdims=True)
        high = d.astype(bf16).astype(f32)
        ga_ref[0, cols, :SPAN] = g2
        ga_ref[0, cols, SPAN:] = jnp.where(
            lane == 0, high, jnp.where(lane == 1, d - high, 0.0)
        ).astype(bf16)
        dp = dot(ve[ext:, :], ga_ref[0, cols, :], NT)
        pt[0, ext:, cols] = (pm[:, cols].astype(f32) * dp).astype(bf16)
    dk = dot(pt[0, ext:, :], q2s[...], NN).astype(bf16)
    dv = dot(pm[...], ga_ref[0, :, :SPAN], NN).astype(bf16)
    for j in range(members):
        part = slice(j * mine, (j + 1) * mine)
        dm_ref[2 * j * mine : (2 * j + 1) * mine, :] = dk[part]
        dm_ref[(2 * j + 1) * mine : (2 * j + 2) * mine, :] = dv[part]


def backward_kernel(
    q_ref, pt_ref, ga_ref, ko_ref, vo_ref, kh_ref, vh_ref, km_ref, *rest, nb
):
    dq_ref, dko_ref, dvo_ref, dh_ref, ke, ve, q2, ds = rest[-8:]
    hrows = kh_ref.shape[0]
    ext = hrows + ko_ref.shape[0]
    fill_keys(ke, kh_ref, ko_ref, km_ref)
    ve[0:hrows, :SPAN] = vh_ref[...]
    ve[hrows:, :SPAN] = vo_ref[...]
    ve[:, SPAN:] = jnp.ones((ve.shape[0], SPAN), bf16)
    first = lax.broadcasted_iota(jnp.int32, (BLK, SPAN), 1) < HEAD_DIM
    unit = HEAD_DIM**-0.5
    for b in range(nb):
        rows, cols = slice(b * BLK, (b + 1) * BLK), slice(b * TWO, (b + 1) * TWO)
        band = slice(b * BLK, (b + FAR + 1) * BLK)
        q2[cols, :] = by_head(q_ref[rows, :] * jnp.asarray(unit, bf16), first)
        ga = ga_ref[0, cols, :]
        dp = dot(ve[band, :], ga, NT)
        ds[band, cols] = (pt_ref[0, band, cols].astype(f32) * dp).astype(bf16)
        dq = dot(ds[band, cols], ke[band, :], TN) + dot(pt_ref[0, ext:, cols], ke[ext:, :], TN)
        dq_ref[rows, :] = (join_heads(dq, first) * unit).astype(bf16)
    for e in range(ext // BLK):
        cols = slice(max(0, e - FAR) * TWO, (min(nb - 1, e) + 1) * TWO)
        rows = slice(e * BLK, (e + 1) * BLK)
        dv = dot(pt_ref[0, rows, cols], ga_ref[0, cols, :SPAN], NN)
        dk = dot(ds[rows, cols], q2[cols, :], NN)
        if e * BLK < hrows:
            dh_ref[rows, :] = dk.astype(bf16)
            dh_ref[hrows + e * BLK : hrows + (e + 1) * BLK, :] = dv.astype(bf16)
        else:
            own = slice(e * BLK - hrows, (e + 1) * BLK - hrows)
            dko_ref[own, :] = dk.astype(bf16)
            dvo_ref[own, :] = dv.astype(bf16)


def columns(rows, start):
    return pl.BlockSpec((rows, SPAN), lambda p, *_: (0, p + start))


ANY = pl.BlockSpec(memory_space=pl.ANY)


def forward(info, q, g, ko, vo, kh, vh, km, vm, bias, members, start, count, base, halo_at, carry):
    tokens, width = q.shape
    slots, hrows, nb = km.shape[0], kh.shape[0], tokens // BLK
    keys = hrows + tokens + slots
    kc, vc = halo_at
    mk, mv = base
    args = [info, q, g, ko, vo, kh, vh, km, vm, bias]
    specs = [
        columns(tokens, start), columns(tokens, start), columns(tokens, start), columns(tokens, start),
        columns(hrows, kc), columns(hrows, vc), columns(slots, mk + start), columns(slots, mv + start),
        pl.BlockSpec(bias.shape, lambda p, *_: (0, 0, 0)),
    ]
    alias = {}
    if carry:
        alias = {len(args) + i: i for i in range(len(carry))}
        args += carry
        specs += [ANY] * len(carry)
    return pl.pallas_call(
        functools.partial(forward_kernel, nb=nb, members=members),
        grid_spec=pltpu.PrefetchScalarGridSpec(
            num_scalar_prefetch=1,
            grid=(count,),
            in_specs=specs,
            out_specs=[
                columns(tokens, start), columns(2 * slots, start),
                pl.BlockSpec((1, keys, nb * TWO), lambda p, *_: (p, 0, 0)),
                pl.BlockSpec((1, nb * TWO, 2 * SPAN), lambda p, *_: (p, 0, 0)),
            ],
            scratch_shapes=[
                pltpu.VMEM((keys, SPAN), bf16), pltpu.VMEM((keys, 2 * SPAN), bf16),
                pltpu.VMEM((nb * TWO, SPAN), bf16), pltpu.VMEM((slots, nb * TWO), bf16),
            ],
        ),
        out_shape=[
            jax.ShapeDtypeStruct((tokens, width), bf16),
            jax.ShapeDtypeStruct((2 * slots, width), bf16),
            jax.ShapeDtypeStruct((count, keys, nb * TWO), bf16),
            jax.ShapeDtypeStruct((count, nb * TWO, 2 * SPAN), bf16),
        ],
        input_output_aliases=alias,
        compiler_params=pltpu.CompilerParams(vmem_limit_bytes=67_000_000),
        cost_estimate=pl.CostEstimate(
            flops=count * nb * 12 * TWO * BLK * 1024, bytes_accessed=count * (4 << 20), transcendentals=count << 20
        ),
        name="band_forward",
    )(*args)


def backward(q, pt, ga, ko, vo, kh, vh, km, start, count, base, halo_at, at, carry, dh_total, dh_at):
    tokens, width = q.shape
    slots, hrows, nb = km.shape[0], kh.shape[0], tokens // BLK
    keys = hrows + tokens + slots
    kc, vc = halo_at
    args = [q, pt, ga, ko, vo, kh, vh, km]
    specs = [
        columns(tokens, start),
        pl.BlockSpec((1, keys, nb * TWO), lambda p, *_: (p + at, 0, 0)),
        pl.BlockSpec((1, nb * TWO, 2 * SPAN), lambda p, *_: (p + at, 0, 0)),
        columns(tokens, start), columns(tokens, start),
        columns(hrows, kc), columns(hrows, vc), columns(slots, base + start),
    ]
    alias = {}
    if carry:
        alias = {len(args) + i: i for i in range(len(carry))}
        args += carry
        specs += [ANY] * len(carry)
    return pl.pallas_call(
        functools.partial(backward_kernel, nb=nb),
        grid=(count,),
        in_specs=specs,
        out_specs=[
            columns(tokens, start), columns(tokens, start), columns(tokens, start),
            columns(2 * hrows, dh_at),
        ],
        scratch_shapes=[
            pltpu.VMEM((keys, SPAN), bf16), pltpu.VMEM((keys - slots, 2 * SPAN), bf16),
            pltpu.VMEM((nb * TWO, SPAN), bf16), pltpu.VMEM((keys - slots, nb * TWO), bf16),
        ],
        out_shape=[
            jax.ShapeDtypeStruct((tokens, width), bf16),
            jax.ShapeDtypeStruct((tokens, width), bf16),
            jax.ShapeDtypeStruct((tokens, width), bf16),
            jax.ShapeDtypeStruct((2 * hrows, dh_total * SPAN), bf16),
        ],
        input_output_aliases=alias,
        compiler_params=pltpu.CompilerParams(vmem_limit_bytes=67_000_000),
        cost_estimate=pl.CostEstimate(
            flops=count * nb * 20 * TWO * BLK * 1024, bytes_accessed=count * (6 << 20), transcendentals=0
        ),
        name="band_backward",
    )(*args)


def finish_kernel(slot_ref, dk_in, dv_in, dm_ref, *rest, segments):
    backs, (dk_ref, dv_ref) = rest[:-2], rest[-2:]
    rows = dk_in.shape[0]
    mine = slot_ref.shape[1]
    at = lax.broadcasted_iota(jnp.int32, (rows, mine), 0) + pl.program_id(0) * rows
    pick = (at == slot_ref[...]).astype(f32).astype(bf16)
    for g, pair, pos, count in segments:
        to, of = slice(pair * SPAN, (pair + count) * SPAN), slice(pos * SPAN, (pos + count) * SPAN)
        back = backs[g]
        dk = dk_in[:, to].astype(f32) + dot(pick, dm_ref[:mine, to], NN)
        dv = dv_in[:, to].astype(f32) + dot(pick, dm_ref[mine:, to], NN)
        dk_ref[:, to] = (dk + back[0, :, of].astype(f32)).astype(bf16)
        dv_ref[:, to] = (dv + back[1, :, of].astype(f32)).astype(bf16)


def finish(slots, dko, dvo, dmem, backs, segments):
    tokens, width = dko.shape
    mine = slots.shape[0]
    row = pl.BlockSpec((BLK, width), lambda r: (r, 0))
    return pl.pallas_call(
        functools.partial(finish_kernel, segments=segments),
        grid=(tokens // BLK,),
        in_specs=[pl.BlockSpec((1, mine), lambda r: (0, 0)), row, row, pl.BlockSpec((2 * mine, width), lambda r: (0, 0))]
        + [pl.BlockSpec((2, BLK, b.shape[-1]), lambda r: (0, r, 0)) for b in backs],
        out_specs=[row, row],
        out_shape=[jax.ShapeDtypeStruct((tokens, width), bf16)] * 2,
        compiler_params=pltpu.CompilerParams(vmem_limit_bytes=67_000_000),
        cost_estimate=pl.CostEstimate(flops=1 << 26, bytes_accessed=6 << 20, transcendentals=0),
        name="finish_rows",
    )(slots[None, :], dko, dvo, dmem, *backs)


def place_kernel(where_ref, w_ref, *rest, nfam, scale):
    out_ref = rest[-1]
    piece = w_ref.shape[0] // nfam
    fam = where_ref[2]
    for k in range(nfam):
        row = pl.multiple_of((fam ^ k) * piece, piece)
        out_ref[pl.ds(row, piece), :] = w_ref[k * piece : (k + 1) * piece, :].astype(f32) * scale


def place(where, w, plane, nfam, scale, carry):
    half, width = w.shape
    rows = half // plane
    args, specs, alias = [w], [pl.BlockSpec((rows, width), lambda k, s: (k, 0))], {}
    if carry is not None:
        args, specs, alias = args + [carry], specs + [ANY], {2: 0}
    return pl.pallas_call(
        functools.partial(place_kernel, nfam=nfam, scale=scale),
        grid_spec=pltpu.PrefetchScalarGridSpec(
            num_scalar_prefetch=1,
            grid=(plane,),
            in_specs=specs,
            out_specs=pl.BlockSpec((rows, width), lambda k, s: (s[0] * plane + (s[1] ^ k), 0)),
        ),
        out_shape=jax.ShapeDtypeStruct((2 * half, width), f32),
        input_output_aliases=alias,
        compiler_params=pltpu.CompilerParams(vmem_limit_bytes=67_000_000),
        cost_estimate=pl.CostEstimate(flops=1 << 20, bytes_accessed=3 << 20, transcendentals=0),
        name="place_rows",
    )(where, *args)


def protein_tables(prot_blocks, last_fill):
    prot_ends = jnp.cumsum(prot_blocks)
    starts = prot_ends - prot_blocks
    valid_len = (prot_blocks - 1) * BLK + last_fill
    return prot_ends, starts, valid_len


def token_info(positions, tables):
    prot_ends, starts, valid_len = tables
    count = prot_ends.shape[0]
    blocks = jnp.floor_divide(positions, BLK)
    protein = jnp.sum((blocks[:, None] >= prot_ends[None, :]).astype(jnp.int32), axis=1)
    onehot = protein[:, None] == jnp.arange(count, dtype=jnp.int32)[None, :]
    first = jnp.sum(jnp.where(onehot, starts[None, :], 0), axis=1)
    length = jnp.sum(jnp.where(onehot, valid_len[None, :], 0), axis=1)
    return protein, first, length - (positions - first * BLK)


def swap(x, axis, bits):
    return lax.ppermute(x, axis, [(i, i ^ bits) for i in range(lax.axis_size(axis))])


def bits_of(n):
    out, b = [], 1
    while b < n:
        out.append(b)
        b *= 2
    return out


def gather_rows(x, axis, me):
    for bit in bits_of(lax.axis_size(axis)):
        other = swap(x, axis, bit)
        upper = (me & bit) != 0
        x = jnp.where(upper, jnp.concatenate([other, x], 0), jnp.concatenate([x, other], 0))
    return x


def exchange(part, axis, shift, me, n):
    got = [swap(part(me ^ k).astype(bf16), axis, k << shift) for k in range(1, n)]
    return sum([g.astype(f32) for g in got], part(me))


def spread(x, axis, shift, n):
    return jnp.concatenate([x] + [swap(x, axis, k << shift) for k in range(1, n)], 0)


def groups_of(pairs):
    if pairs % 8:
        return [pairs], [(0, 0, pairs)], [pairs]
    u = pairs // 8
    return [3 * u, 3 * u, 2 * u], [(0, 0, u), (1, 0, 3 * u), (0, u, 2 * u), (2, 0, 2 * u)], [4 * u, 2 * u, 2 * u]


def per_device(queries, key_rows, value_rows, cotangent, out_weight, prot_blocks, last_fill, memory_slots):
    q, k, v, cot = queries[0], key_rows[0], value_rows[0], cotangent[0]
    tables = protein_tables(prot_blocks[0], last_fill[0])
    slots = memory_slots[0]
    tokens, width = q.shape
    nctx, nfam = lax.axis_size("ctx"), lax.axis_size("fam")
    me, fam = lax.axis_index("ctx"), lax.axis_index("fam")
    total = slots.shape[0]
    mine = total // nctx
    nb = tokens // BLK
    pairs = width // SPAN
    fsizes, bplan, dhs = groups_of(pairs)
    fstarts = [sum(fsizes[:i]) for i in range(len(fsizes))]
    shift = [(i, i + 1) for i in range(nctx - 1)]
    back = [(i + 1, i) for i in range(nctx - 1)]
    edge = tokens - W
    halos = []
    for i, (at, count) in enumerate(zip(fstarts, fsizes)):
        cols = slice(at * SPAN, (at + count) * SPAN)
        halos.append(lax.ppermute(jnp.concatenate([k[edge:, cols], v[edge:, cols]], 1), "ctx", shift))
    own_slots = lax.dynamic_slice_in_dim(slots, me * mine, mine)
    pick = (own_slots[:, None] == jnp.arange(tokens, dtype=jnp.int32)[None, :]).astype(bf16)
    rows = jnp.concatenate([dot(pick, k, NN).astype(bf16), dot(pick, v, NN).astype(bf16)], 1)
    mem = gather_rows(rows, "ctx", me)
    grad_attn = dot(cot, out_weight, NT).astype(bf16)
    heads = me * tokens + jnp.arange(nb, dtype=jnp.int32) * BLK
    source = jnp.arange(total, dtype=jnp.int32) // mine * tokens + slots
    prot, first, left = token_info(jnp.concatenate([heads, source]), tables)
    lo = jnp.clip(first[:nb] - (me * tokens - W) // BLK, 0, nb + FAR)
    info = jnp.stack([lo, jnp.clip(left[:nb], 0, BLK)])
    seen = (left[nb:] > 0)[None, :] & (prot[None, nb:] < prot[:nb, None])
    bias = jnp.broadcast_to(jnp.where(seen, 0.0, NEG).astype(f32)[:, :, None], (nb, total, BLK))
    base = (0, pairs)
    carry, saved = [], []
    for i, (at, count) in enumerate(zip(fstarts, fsizes)):
        att, dm, pt, ga = forward(
            info, q, grad_attn, k, v, halos[i], halos[i], mem, mem, bias, nctx,
            at, count, base, (0, count), carry)
        carry = [att, dm]
        saved.append((pt, ga))
    core, spot, plane = me & 1, me >> 1, nctx // 2
    w = dot(att, cot, TN).astype(bf16).reshape(2, plane, width // nctx, width)
    dm = dm.reshape(plane, 2, 2 * mine, width)
    at = lambda x, j, axis: lax.dynamic_index_in_dim(x, j, axis, keepdims=False)
    side = lambda c: jnp.concatenate([at(w, c, 0), at(dm, c, 1)], 1)
    sent = swap(side(1 - core), "ctx", 1)
    kept = side(core)
    carry, backs, segments, i = [], [], [], 0
    for total_dh in dhs:
        done = 0
        while done < total_dh:
            j, r, count = bplan[i]
            pt, ga = saved[j]
            out = backward(
                q, pt, ga, k, v, halos[j], halos[j], mem, fstarts[j] + r, count,
                0, (r, fsizes[j] + r), r, carry, total_dh, done)
            carry = list(out)
            segments.append((len(backs), fstarts[j] + r, done, count))
            done, i = done + count, i + 1
        backs.append(lax.ppermute(carry.pop(), "ctx", back))
    total_w = exchange(
        lambda j: at(sent, j, 0).astype(f32) + at(kept, j, 0).astype(f32), "ctx", 1, spot, plane)
    mem_grad, total_w = total_w[width // nctx :].astype(bf16), total_w[: width // nctx].reshape(nfam, -1, width)
    total_w = exchange(lambda j: at(total_w, j, 0), "fam", 0, fam, nfam)
    w = spread(total_w.astype(bf16), "fam", 0, nfam)
    w = spread(w, "ctx", 1, plane)
    other = swap(w, "ctx", 1)
    scale = (nfam * nctx * tokens) ** -0.5
    where = lambda c: jnp.stack([c, spot, fam]).astype(jnp.int32)
    weight = place(where(core), w, plane, nfam, scale, None)
    weight = place(where(1 - core), other, plane, nfam, scale, weight)
    dq, dko, dvo = carry
    backs = [x.reshape(2, W, -1) for x in backs]
    dk, dv = finish(own_slots, dko, dvo, mem_grad, backs, segments)
    return dq[None], dk[None], dv[None], weight


def solution(mesh):
    row = P("fam", "ctx", None)
    small = P("fam", None)

    return jax.shard_map(
        per_device,
        mesh=mesh,
        in_specs=(row, row, row, row, P(), small, small, small),
        out_specs=(row, row, row, P()),
        check_vma=False,
    )
```

```python
import functools

import jax
import jax.numpy as jnp
from jax import lax
from jax.experimental import pallas as pl
from jax.experimental.pallas import tpu as pltpu
from jax.sharding import PartitionSpec as P


HEAD_DIM = 64
W = 512
BLK = 128
SPAN = 2 * HEAD_DIM
TWO = 2 * BLK
FAR = W // BLK
NEG = -1e30
NT = (((1,), (1,)), ((), ()))
NN = (((1,), (0,)), ((), ()))
TN = (((0,), (0,)), ((), ()))
f32 = jnp.float32
bf16 = jnp.bfloat16


def dot(a, b, dims):
    return lax.dot_general(a, b, dims, preferred_element_type=f32)


def by_head(x, first):
    zero = jnp.zeros_like(x)
    return jnp.concatenate([jnp.where(first, x, zero), jnp.where(first, zero, x)], 0)


def join_heads(x, first):
    return jnp.where(first, x[:BLK], x[BLK:])


def fill_keys(dst, halo, own, memory):
    h, o = halo.shape[0], own.shape[0]
    dst[0:h, :SPAN] = halo[...]
    dst[h : h + o, :SPAN] = own[...]
    dst[h + o :, :SPAN] = memory[...]


def forward_kernel(
    info_ref, q_ref, g_ref, ko_ref, vo_ref, kh_ref, vh_ref, km_ref, vm_ref, mb_ref, *rest, nb, order
):
    at_ref, dm_ref, pt, ga_ref, ke, ve, q2s, pm = rest[-8:]
    slots = km_ref.shape[0]
    mine = slots // len(order)
    ext = kh_ref.shape[0] + ko_ref.shape[0]
    fill_keys(ke, kh_ref, ko_ref, km_ref)
    fill_keys(ve, vh_ref, vo_ref, vm_ref)
    ve[:, SPAN:] = jnp.ones((ve.shape[0], SPAN), bf16)
    first = lax.broadcasted_iota(jnp.int32, (BLK, SPAN), 1) < HEAD_DIM
    tri = (
        lax.broadcasted_iota(jnp.int32, (BLK, TWO), 0)
        <= lax.broadcasted_iota(jnp.int32, (BLK, TWO), 1) % BLK
    )
    lane = lax.broadcasted_iota(jnp.int32, (TWO, SPAN), 1)
    row = lax.broadcasted_iota(jnp.int32, (TWO, SPAN), 0) % BLK
    unit = jnp.asarray(HEAD_DIM**-0.5, bf16)
    at = lambda b: (slice(b * BLK, (b + 1) * BLK), slice(b * TWO, (b + 1) * TWO), slice(b * BLK, (b + FAR + 1) * BLK))
    scores, outs = {}, {}

    def score(b):
        rows, cols, band = at(b)
        q2 = by_head(q_ref[rows, :] * unit, first)
        q2s[cols, :] = q2
        scores[b] = (dot(ke[band, :], q2, NT), dot(ke[ext:, :], q2, NT))

    def exponentials(b):
        _, cols, _ = at(b)
        s, sm = scores.pop(b)
        sm = sm + jnp.concatenate([mb_ref[b], mb_ref[b]], 1)
        off = [jnp.where(e + b >= info_ref[0, b], 0.0, NEG).astype(f32) for e in range(FAR)]
        ends = jnp.where(tri, s[FAR * BLK :, :], s[:BLK, :] + off[0])
        mid = [s[e * BLK : (e + 1) * BLK, :] for e in range(1, FAR)]
        m = jnp.maximum(jnp.max(ends, 0, keepdims=True), jnp.max(sm, 0, keepdims=True))
        for e in range(1, FAR):
            m = jnp.maximum(m, jnp.max(mid[e - 1], 0, keepdims=True) + off[e])
        for e in range(1, FAR):
            pt[0, (b + e) * BLK : (b + e + 1) * BLK, cols] = jnp.exp(
                mid[e - 1] - (m - off[e])
            ).astype(bf16)
        pm[:, cols] = jnp.exp(sm - m).astype(bf16)
        p = jnp.exp(ends - m).astype(bf16)
        zero = jnp.zeros_like(p)
        pt[0, b * BLK : (b + 1) * BLK, cols] = jnp.where(tri, zero, p)
        pt[0, (b + FAR) * BLK : (b + FAR + 1) * BLK, cols] = jnp.where(tri, p, zero)

    def attend(b):
        _, cols, band = at(b)
        outs[b] = dot(pt[0, band, cols], ve[band, :], TN) + dot(pm[:, cols], ve[ext:, :], TN)

    def gradients(b):
        rows, cols, _ = at(b)
        o = outs.pop(b)
        scale = jnp.where(row < info_ref[1, b], 1.0 / o[:, SPAN:], 0.0)
        o = o[:, :SPAN] * scale
        at_ref[rows, :] = join_heads(o, first).astype(bf16)
        g2 = (by_head(g_ref[rows, :].astype(f32), first) * scale).astype(bf16)
        d = -jnp.sum(g2.astype(f32) * o, 1, keepdims=True)
        high = d.astype(bf16).astype(f32)
        ga_ref[0, cols, :SPAN] = g2
        ga_ref[0, cols, SPAN:] = jnp.where(
            lane == 0, high, jnp.where(lane == 1, d - high, 0.0)
        ).astype(bf16)

    def memory(b):
        _, cols, _ = at(b)
        dp = dot(ve[ext:, :], ga_ref[0, cols, :], NT)
        pt[0, ext:, cols] = (pm[:, cols].astype(f32) * dp).astype(bf16)

    for t in range(nb + 4):
        for stage, lag in ((score, 0), (attend, 2), (exponentials, 1), (memory, 4), (gradients, 3)):
            if 0 <= t - lag < nb:
                stage(t - lag)
    dk = dot(pt[0, ext:, :], q2s[...], NN).astype(bf16)
    dv = dot(pm[...], ga_ref[0, :, :SPAN], NN).astype(bf16)
    for i, j in enumerate(order):
        part = slice(i * mine, (i + 1) * mine)
        dm_ref[2 * j * mine : (2 * j + 1) * mine, :] = dk[part]
        dm_ref[(2 * j + 1) * mine : (2 * j + 2) * mine, :] = dv[part]


def backward_kernel(
    q_ref, pt_ref, ga_ref, ko_ref, vo_ref, kh_ref, vh_ref, km_ref, *rest, nb
):
    dq_ref, dko_ref, dvo_ref, dh_ref, ke, ve, q2, ds = rest[-8:]
    hrows = kh_ref.shape[0]
    ext = hrows + ko_ref.shape[0]
    fill_keys(ke, kh_ref, ko_ref, km_ref)
    ve[0:hrows, :SPAN] = vh_ref[...]
    ve[hrows:, :SPAN] = vo_ref[...]
    ve[:, SPAN:] = jnp.ones((ve.shape[0], SPAN), bf16)
    first = lax.broadcasted_iota(jnp.int32, (BLK, SPAN), 1) < HEAD_DIM
    unit = HEAD_DIM**-0.5
    for b in range(nb):
        rows, cols = slice(b * BLK, (b + 1) * BLK), slice(b * TWO, (b + 1) * TWO)
        band = slice(b * BLK, (b + FAR + 1) * BLK)
        q2[cols, :] = by_head(q_ref[rows, :] * jnp.asarray(unit, bf16), first)
        ga = ga_ref[0, cols, :]
        dp = dot(ve[band, :], ga, NT)
        ds[band, cols] = (pt_ref[0, band, cols].astype(f32) * dp).astype(bf16)
        dq = dot(ds[band, cols], ke[band, :], TN) + dot(pt_ref[0, ext:, cols], ke[ext:, :], TN)
        dq_ref[rows, :] = (join_heads(dq, first) * unit).astype(bf16)
    for e in range(ext // BLK):
        cols = slice(max(0, e - FAR) * TWO, (min(nb - 1, e) + 1) * TWO)
        rows = slice(e * BLK, (e + 1) * BLK)
        dv = dot(pt_ref[0, rows, cols], ga_ref[0, cols, :SPAN], NN)
        dk = dot(ds[rows, cols], q2[cols, :], NN)
        if e * BLK < hrows:
            dh_ref[rows, :] = dk.astype(bf16)
            dh_ref[hrows + e * BLK : hrows + (e + 1) * BLK, :] = dv.astype(bf16)
        else:
            own = slice(e * BLK - hrows, (e + 1) * BLK - hrows)
            dko_ref[own, :] = dk.astype(bf16)
            dvo_ref[own, :] = dv.astype(bf16)


def columns(rows, start):
    return pl.BlockSpec((rows, SPAN), lambda p, *_: (0, p + start))


ANY = pl.BlockSpec(memory_space=pl.ANY)


def forward(info, q, g, ko, vo, kh, vh, km, vm, bias, order, start, count, base, halo_at, carry):
    tokens, width = q.shape
    slots, hrows, nb = km.shape[0], kh.shape[0], tokens // BLK
    keys = hrows + tokens + slots
    kc, vc = halo_at
    mk, mv = base
    args = [info, q, g, ko, vo, kh, vh, km, vm, bias]
    specs = [
        columns(tokens, start), columns(tokens, start), columns(tokens, start), columns(tokens, start),
        columns(hrows, kc), columns(hrows, vc), columns(slots, mk + start), columns(slots, mv + start),
        pl.BlockSpec(bias.shape, lambda p, *_: (0, 0, 0)),
    ]
    alias = {}
    if carry:
        alias = {len(args) + i: i for i in range(len(carry))}
        args += carry
        specs += [ANY] * len(carry)
    return pl.pallas_call(
        functools.partial(forward_kernel, nb=nb, order=order),
        grid_spec=pltpu.PrefetchScalarGridSpec(
            num_scalar_prefetch=1,
            grid=(count,),
            in_specs=specs,
            out_specs=[
                columns(tokens, start), columns(2 * slots, start),
                pl.BlockSpec((1, keys, nb * TWO), lambda p, *_: (p, 0, 0)),
                pl.BlockSpec((1, nb * TWO, 2 * SPAN), lambda p, *_: (p, 0, 0)),
            ],
            scratch_shapes=[
                pltpu.VMEM((keys, SPAN), bf16), pltpu.VMEM((keys, 2 * SPAN), bf16),
                pltpu.VMEM((nb * TWO, SPAN), bf16), pltpu.VMEM((slots, nb * TWO), bf16),
            ],
        ),
        out_shape=[
            jax.ShapeDtypeStruct((tokens, width), bf16),
            jax.ShapeDtypeStruct((2 * slots, width), bf16),
            jax.ShapeDtypeStruct((count, keys, nb * TWO), bf16),
            jax.ShapeDtypeStruct((count, nb * TWO, 2 * SPAN), bf16),
        ],
        input_output_aliases=alias,
        compiler_params=pltpu.CompilerParams(vmem_limit_bytes=67_000_000),
        cost_estimate=pl.CostEstimate(
            flops=count * nb * 12 * TWO * BLK * 1024, bytes_accessed=count * (4 << 20), transcendentals=count << 20
        ),
        name="band_forward",
    )(*args)


def backward(q, pt, ga, ko, vo, kh, vh, km, start, count, base, halo_at, at, carry, dh_total, dh_at):
    tokens, width = q.shape
    slots, hrows, nb = km.shape[0], kh.shape[0], tokens // BLK
    keys = hrows + tokens + slots
    kc, vc = halo_at
    args = [q, pt, ga, ko, vo, kh, vh, km]
    specs = [
        columns(tokens, start),
        pl.BlockSpec((1, keys, nb * TWO), lambda p, *_: (p + at, 0, 0)),
        pl.BlockSpec((1, nb * TWO, 2 * SPAN), lambda p, *_: (p + at, 0, 0)),
        columns(tokens, start), columns(tokens, start),
        columns(hrows, kc), columns(hrows, vc), columns(slots, base + start),
    ]
    alias = {}
    if carry:
        alias = {len(args) + i: i for i in range(len(carry))}
        args += carry
        specs += [ANY] * len(carry)
    return pl.pallas_call(
        functools.partial(backward_kernel, nb=nb),
        grid=(count,),
        in_specs=specs,
        out_specs=[
            columns(tokens, start), columns(tokens, start), columns(tokens, start),
            columns(2 * hrows, dh_at),
        ],
        scratch_shapes=[
            pltpu.VMEM((keys, SPAN), bf16), pltpu.VMEM((keys - slots, 2 * SPAN), bf16),
            pltpu.VMEM((nb * TWO, SPAN), bf16), pltpu.VMEM((keys - slots, nb * TWO), bf16),
        ],
        out_shape=[
            jax.ShapeDtypeStruct((tokens, width), bf16),
            jax.ShapeDtypeStruct((tokens, width), bf16),
            jax.ShapeDtypeStruct((tokens, width), bf16),
            jax.ShapeDtypeStruct((2 * hrows, dh_total * SPAN), bf16),
        ],
        input_output_aliases=alias,
        compiler_params=pltpu.CompilerParams(vmem_limit_bytes=67_000_000),
        cost_estimate=pl.CostEstimate(
            flops=count * nb * 20 * TWO * BLK * 1024, bytes_accessed=count * (6 << 20), transcendentals=0
        ),
        name="band_backward",
    )(*args)


def finish_kernel(slot_ref, dk_in, dv_in, dm_ref, *rest, segments):
    backs, (dk_ref, dv_ref) = rest[:-2], rest[-2:]
    rows = dk_in.shape[0]
    mine = slot_ref.shape[1]
    at = lax.broadcasted_iota(jnp.int32, (rows, mine), 0) + pl.program_id(0) * rows
    pick = (at == slot_ref[...]).astype(f32).astype(bf16)
    for g, pair, pos, count in segments:
        to, of = slice(pair * SPAN, (pair + count) * SPAN), slice(pos * SPAN, (pos + count) * SPAN)
        back = backs[g]
        dk = dk_in[:, to].astype(f32) + dot(pick, dm_ref[:mine, to], NN)
        dv = dv_in[:, to].astype(f32) + dot(pick, dm_ref[mine:, to], NN)
        dk_ref[:, to] = (dk + back[0, :, of].astype(f32)).astype(bf16)
        dv_ref[:, to] = (dv + back[1, :, of].astype(f32)).astype(bf16)


def finish(slots, dko, dvo, dmem, backs, segments):
    tokens, width = dko.shape
    mine = slots.shape[0]
    row = pl.BlockSpec((BLK, width), lambda r: (r, 0))
    return pl.pallas_call(
        functools.partial(finish_kernel, segments=segments),
        grid=(tokens // BLK,),
        in_specs=[pl.BlockSpec((1, mine), lambda r: (0, 0)), row, row, pl.BlockSpec((2 * mine, width), lambda r: (0, 0))]
        + [pl.BlockSpec((2, BLK, b.shape[-1]), lambda r: (0, r, 0)) for b in backs],
        out_specs=[row, row],
        out_shape=[jax.ShapeDtypeStruct((tokens, width), bf16)] * 2,
        compiler_params=pltpu.CompilerParams(vmem_limit_bytes=67_000_000),
        cost_estimate=pl.CostEstimate(flops=1 << 26, bytes_accessed=6 << 20, transcendentals=0),
        name="finish_rows",
    )(slots[None, :], dko, dvo, dmem, *backs)


def place_kernel(where_ref, *rest, plane, nfam, scale):
    n = 2 * plane
    parts, out_ref, buf, sems = rest[:n], rest[n], rest[n + 1], rest[n + 2]
    rows = parts[0].shape[0]
    piece = rows // nfam
    core, spot, fam = where_ref[0], where_ref[1], where_ref[2]
    copies = []
    for i, part in enumerate(parts):
        side = jnp.where(i < plane, core, 1 - core)
        at = pl.multiple_of((side * plane + (spot ^ (i % plane))) * rows, rows)
        for k in range(nfam):
            row = pl.multiple_of((fam ^ k) * piece, piece)
            buf[i, pl.ds(row, piece), :] = part[k * piece : (k + 1) * piece, :].astype(f32) * scale
        copies.append(pltpu.make_async_copy(buf.at[i], out_ref.at[pl.ds(at, rows), :], sems.at[i]))
        copies[-1].start()
    for copy in copies:
        copy.wait()


def place(where, parts, nfam, scale):
    rows, width = parts[0].shape
    n = len(parts)
    return pl.pallas_call(
        functools.partial(place_kernel, plane=n // 2, nfam=nfam, scale=scale),
        in_specs=[pl.BlockSpec(memory_space=pltpu.SMEM)] + [pl.BlockSpec(memory_space=pltpu.VMEM)] * n,
        out_specs=pl.BlockSpec(memory_space=pl.ANY),
        out_shape=jax.ShapeDtypeStruct((n * rows, width), f32),
        scratch_shapes=[pltpu.VMEM((n, rows, width), f32), pltpu.SemaphoreType.DMA((n,))],
        compiler_params=pltpu.CompilerParams(vmem_limit_bytes=67_000_000),
        cost_estimate=pl.CostEstimate(flops=1 << 20, bytes_accessed=6 << 20, transcendentals=0),
        name="place_rows",
    )(where, *parts)


def protein_tables(prot_blocks, last_fill):
    prot_ends = jnp.cumsum(prot_blocks)
    starts = prot_ends - prot_blocks
    valid_len = (prot_blocks - 1) * BLK + last_fill
    return prot_ends, starts, valid_len


def token_info(positions, tables):
    prot_ends, starts, valid_len = tables
    count = prot_ends.shape[0]
    blocks = jnp.floor_divide(positions, BLK)
    protein = jnp.sum((blocks[:, None] >= prot_ends[None, :]).astype(jnp.int32), axis=1)
    onehot = protein[:, None] == jnp.arange(count, dtype=jnp.int32)[None, :]
    first = jnp.sum(jnp.where(onehot, starts[None, :], 0), axis=1)
    length = jnp.sum(jnp.where(onehot, valid_len[None, :], 0), axis=1)
    return protein, first, length - (positions - first * BLK)


def swap(x, axis, bits):
    return lax.ppermute(x, axis, [(i, i ^ bits) for i in range(lax.axis_size(axis))])


def bits_of(n):
    out, b = [], 1
    while b < n:
        out.append(b)
        b *= 2
    return out


def mirrored(n):
    order = [0]
    for bit in reversed(bits_of(n)):
        order = order + [i + bit for i in order]
    return order


def gather_rows(x, axis, me):
    for bit in reversed(bits_of(lax.axis_size(axis))):
        other = swap(x, axis, bit)
        upper = (me & bit) != 0
        x = jnp.where(upper, jnp.concatenate([other, x], 0), jnp.concatenate([x, other], 0))
    return x


def exchange(part, axis, shift, me, n):
    return [part(me)] + [swap(part(me ^ k).astype(bf16), axis, k << shift) for k in range(1, n)]


def spread(x, axis, shift, n):
    return [x] + [swap(x, axis, k << shift) for k in range(1, n)]


def total_of(parts):
    return sum([x.astype(f32) for x in parts[1:]], parts[0].astype(f32))


def groups_of(pairs):
    if pairs % 8:
        return [pairs], [(0, 0, pairs)], [pairs]
    u = pairs // 8
    return [2 * u, 3 * u, 3 * u], [(0, 0, 2 * u), (1, 0, 3 * u), (2, 0, u), (2, u, 2 * u)], [6 * u, 2 * u]


def per_device(queries, key_rows, value_rows, cotangent, out_weight, prot_blocks, last_fill, memory_slots):
    q, k, v, cot = queries[0], key_rows[0], value_rows[0], cotangent[0]
    tables = protein_tables(prot_blocks[0], last_fill[0])
    slots = memory_slots[0]
    tokens, width = q.shape
    nctx, nfam = lax.axis_size("ctx"), lax.axis_size("fam")
    me, fam = lax.axis_index("ctx"), lax.axis_index("fam")
    total = slots.shape[0]
    mine = total // nctx
    nb = tokens // BLK
    pairs = width // SPAN
    fsizes, bplan, dhs = groups_of(pairs)
    fstarts = [sum(fsizes[:i]) for i in range(len(fsizes))]
    shift = [(i, i + 1) for i in range(nctx - 1)]
    back = [(i + 1, i) for i in range(nctx - 1)]
    edge = tokens - W
    halos = []
    for i, (at, count) in enumerate(zip(fstarts, fsizes)):
        cols = slice(at * SPAN, (at + count) * SPAN)
        halos.append(lax.ppermute(jnp.concatenate([k[edge:, cols], v[edge:, cols]], 1), "ctx", shift))
    own_slots = lax.dynamic_slice_in_dim(slots, me * mine, mine)
    pick = (own_slots[:, None] == jnp.arange(tokens, dtype=jnp.int32)[None, :]).astype(bf16)
    rows = jnp.concatenate([dot(pick, k, NN).astype(bf16), dot(pick, v, NN).astype(bf16)], 1)
    mem = gather_rows(rows, "ctx", me)
    grad_attn = dot(cot, out_weight, NT).astype(bf16)
    heads = me * tokens + jnp.arange(nb, dtype=jnp.int32) * BLK
    order = mirrored(nctx)
    source = (jnp.asarray(order, jnp.int32)[:, None] * tokens + slots.reshape(nctx, mine)[jnp.asarray(order)]).reshape(-1)
    prot, first, left = token_info(jnp.concatenate([heads, source]), tables)
    lo = jnp.clip(first[:nb] - (me * tokens - W) // BLK, 0, nb + FAR)
    info = jnp.stack([lo, jnp.clip(left[:nb], 0, BLK)])
    seen = (left[nb:] > 0)[None, :] & (prot[None, nb:] < prot[:nb, None])
    bias = jnp.broadcast_to(jnp.where(seen, 0.0, NEG).astype(f32)[:, :, None], (nb, total, BLK))
    base = (0, pairs)
    carry, saved = [], []
    for i, (at, count) in enumerate(zip(fstarts, fsizes)):
        att, dm, pt, ga = forward(
            info, q, grad_attn, k, v, halos[i], halos[i], mem, mem, bias, order,
            at, count, base, (0, count), carry)
        carry = [att, dm]
        saved.append((pt, ga))
    core, spot, plane = me & 1, me >> 1, nctx // 2
    w = dot(att, cot, TN).astype(bf16).reshape(2, plane, width // nctx, width)
    dm = dm.reshape(plane, 2, 2 * mine, width)
    at = lambda x, j, axis: lax.dynamic_index_in_dim(x, j, axis, keepdims=False)
    side = lambda c: jnp.concatenate([at(w, c, 0), at(dm, c, 1)], 1)
    sent = swap(side(1 - core), "ctx", 1)
    kept = side(core)
    carry, backs, segments, i = [], [], [], 0
    for total_dh in dhs:
        done = 0
        while done < total_dh:
            j, r, count = bplan[i]
            pt, ga = saved[j]
            out = backward(
                q, pt, ga, k, v, halos[j], halos[j], mem, fstarts[j] + r, count,
                0, (r, fsizes[j] + r), r, carry, total_dh, done)
            carry = list(out)
            segments.append((len(backs), fstarts[j] + r, done, count))
            done, i = done + count, i + 1
        backs.append(lax.ppermute(carry.pop(), "ctx", back))
    got = exchange(lambda j: at(sent, j, 0).astype(f32) + at(kept, j, 0).astype(f32), "ctx", 1, spot, plane)
    rows = width // nctx
    mem_grad = total_of([x[rows:] for x in got]).astype(bf16)
    piece = lambda j: total_of([lax.dynamic_slice_in_dim(x, j * (rows // nfam), rows // nfam) for x in got])
    w = total_of(exchange(piece, "fam", 0, fam, nfam)).astype(bf16)
    w = jnp.concatenate(spread(w, "fam", 0, nfam), 0)
    parts = spread(w, "ctx", 1, plane)
    parts = parts + [swap(x, "ctx", 1) for x in parts]
    scale = (nfam * nctx * tokens) ** -0.5
    weight = place(jnp.stack([core, spot, fam]).astype(jnp.int32), parts, nfam, scale)
    dq, dko, dvo = carry
    backs = [x.reshape(2, W, -1) for x in backs]
    dk, dv = finish(own_slots, dko, dvo, mem_grad, backs, segments)
    return dq[None], dk[None], dv[None], weight


def solution(mesh):
    row = P("fam", "ctx", None)
    small = P("fam", None)

    return jax.shard_map(
        per_device,
        mesh=mesh,
        in_specs=(row, row, row, row, P(), small, small, small),
        out_specs=(row, row, row, P()),
        check_vma=False,
    )
```

```python
import functools

import jax
import jax.numpy as jnp
from jax import lax
from jax.experimental import pallas as pl
from jax.experimental.pallas import tpu as pltpu
from jax.sharding import PartitionSpec as P


HEAD_DIM = 64
W = 512
BLK = 128
SPAN = 2 * HEAD_DIM
TWO = 2 * BLK
FAR = W // BLK
NEG = -1e30
NT = (((1,), (1,)), ((), ()))
NN = (((1,), (0,)), ((), ()))
TN = (((0,), (0,)), ((), ()))
f32 = jnp.float32
bf16 = jnp.bfloat16


def dot(a, b, dims):
    return lax.dot_general(a, b, dims, preferred_element_type=f32)


def by_head(x, first):
    zero = jnp.zeros_like(x)
    return jnp.concatenate([jnp.where(first, x, zero), jnp.where(first, zero, x)], 0)


def join_heads(x, first):
    return jnp.where(first, x[:BLK], x[BLK:])


def fill_keys(dst, halo, own, memory):
    h, o = halo.shape[0], own.shape[0]
    dst[0:h, :SPAN] = halo[...]
    dst[h : h + o, :SPAN] = own[...]
    dst[h + o :, :SPAN] = memory[...]


def tables(me, blocks_ref, fill_ref, slots_ref, info, bias, nb, tokens, order):
    nprot, slots = blocks_ref.shape[1], slots_ref.shape[1]
    mine = slots // len(order)
    begin = jnp.int32(0)
    first, left, pads = [0] * nb, [0] * nb, []
    for p in range(nprot):
        end = begin + blocks_ref[0, p]
        real = (end - 1) * BLK + fill_ref[0, p]
        pads.append((real, end * BLK))
        for b in range(nb):
            block = me * nb + b
            inside = (block >= begin) & (block < end)
            first[b] = jnp.where(inside, begin, first[b])
            left[b] = jnp.where(inside, real - block * BLK, left[b])
        begin = end
    for b in range(nb):
        info[0, b] = first[b] - (me * nb - FAR)
        info[1, b] = left[b]
    row = lax.broadcasted_iota(jnp.int32, (BLK, BLK), 0)
    for g in range(slots // BLK):
        lanes = jnp.broadcast_to(slots_ref[:, g * BLK : (g + 1) * BLK], (BLK, BLK))
        source = lanes.T + (row + g * BLK) // mine * tokens
        bad = jnp.zeros((BLK, BLK), f32)
        for lo, hi in pads:
            bad = jnp.where((source >= lo) & (source < hi), 1.0, bad)
        for b in range(nb):
            seen = jnp.where((source < first[b] * BLK) & (bad == 0.0), 0.0, NEG)
            for j in range(g * BLK // mine, (g + 1) * BLK // mine):
                i = order.index(j)
                bias[b, i * mine : (i + 1) * mine, :] = seen[j * mine - g * BLK : (j + 1) * mine - g * BLK]


def forward_kernel(
    me_ref, blocks_ref, fill_ref, q_ref, cot_ref, w_ref, ko_ref, vo_ref, kh_ref, vh_ref, km_ref, vm_ref, slots_ref,
    *rest, nb, order
):
    at_ref, dm_ref, pt, ga_ref, ke, ve, q2s, pm, mb_ref, g_ref, info_ref = rest[-11:]
    slots = km_ref.shape[0]
    mine = slots // len(order)
    ext = kh_ref.shape[0] + ko_ref.shape[0]

    @pl.when(pl.program_id(0) == 0)
    def _():
        tables(me_ref[0], blocks_ref, fill_ref, slots_ref, info_ref, mb_ref, nb, ko_ref.shape[0], order)

    g_ref[...] = dot(cot_ref[...], w_ref[...], NT).astype(bf16)
    fill_keys(ke, kh_ref, ko_ref, km_ref)
    fill_keys(ve, vh_ref, vo_ref, vm_ref)
    ve[:, SPAN:] = jnp.ones((ve.shape[0], SPAN), bf16)
    first = lax.broadcasted_iota(jnp.int32, (BLK, SPAN), 1) < HEAD_DIM
    tri = (
        lax.broadcasted_iota(jnp.int32, (BLK, TWO), 0)
        <= lax.broadcasted_iota(jnp.int32, (BLK, TWO), 1) % BLK
    )
    lane = lax.broadcasted_iota(jnp.int32, (TWO, SPAN), 1)
    row = lax.broadcasted_iota(jnp.int32, (TWO, SPAN), 0) % BLK
    unit = jnp.asarray(HEAD_DIM**-0.5, bf16)
    at = lambda b: (slice(b * BLK, (b + 1) * BLK), slice(b * TWO, (b + 1) * TWO), slice(b * BLK, (b + FAR + 1) * BLK))
    scores, outs = {}, {}

    def score(b):
        rows, cols, band = at(b)
        q2 = by_head(q_ref[rows, :] * unit, first)
        q2s[cols, :] = q2
        scores[b] = (dot(ke[band, :], q2, NT), dot(ke[ext:, :], q2, NT))

    def exponentials(b):
        _, cols, _ = at(b)
        s, sm = scores.pop(b)
        sm = sm + jnp.concatenate([mb_ref[b], mb_ref[b]], 1)
        off = [jnp.where(e + b >= info_ref[0, b], 0.0, NEG).astype(f32) for e in range(FAR)]
        ends = jnp.where(tri, s[FAR * BLK :, :], s[:BLK, :] + off[0])
        mid = [s[e * BLK : (e + 1) * BLK, :] for e in range(1, FAR)]
        m = jnp.maximum(jnp.max(ends, 0, keepdims=True), jnp.max(sm, 0, keepdims=True))
        for e in range(1, FAR):
            m = jnp.maximum(m, jnp.max(mid[e - 1], 0, keepdims=True) + off[e])
        for e in range(1, FAR):
            pt[0, (b + e) * BLK : (b + e + 1) * BLK, cols] = jnp.exp(
                mid[e - 1] - (m - off[e])
            ).astype(bf16)
        pm[:, cols] = jnp.exp(sm - m).astype(bf16)
        p = jnp.exp(ends - m).astype(bf16)
        zero = jnp.zeros_like(p)
        pt[0, b * BLK : (b + 1) * BLK, cols] = jnp.where(tri, zero, p)
        pt[0, (b + FAR) * BLK : (b + FAR + 1) * BLK, cols] = jnp.where(tri, p, zero)

    def attend(b):
        _, cols, band = at(b)
        outs[b] = dot(pt[0, band, cols], ve[band, :], TN) + dot(pm[:, cols], ve[ext:, :], TN)

    def gradients(b):
        rows, cols, _ = at(b)
        o = outs.pop(b)
        scale = jnp.where(row < info_ref[1, b], 1.0 / o[:, SPAN:], 0.0)
        o = o[:, :SPAN] * scale
        at_ref[rows, :] = join_heads(o, first).astype(bf16)
        g2 = (by_head(g_ref[rows, :].astype(f32), first) * scale).astype(bf16)
        d = -jnp.sum(g2.astype(f32) * o, 1, keepdims=True)
        high = d.astype(bf16).astype(f32)
        ga_ref[0, cols, :SPAN] = g2
        ga_ref[0, cols, SPAN:] = jnp.where(
            lane == 0, high, jnp.where(lane == 1, d - high, 0.0)
        ).astype(bf16)

    def memory(b):
        _, cols, _ = at(b)
        dp = dot(ve[ext:, :], ga_ref[0, cols, :], NT)
        pt[0, ext:, cols] = (pm[:, cols].astype(f32) * dp).astype(bf16)

    for t in range(nb + 4):
        for stage, lag in ((score, 0), (attend, 2), (exponentials, 1), (memory, 4), (gradients, 3)):
            if 0 <= t - lag < nb:
                stage(t - lag)
    dk = dot(pt[0, ext:, :], q2s[...], NN).astype(bf16)
    dv = dot(pm[...], ga_ref[0, :, :SPAN], NN).astype(bf16)
    for i, j in enumerate(order):
        part = slice(i * mine, (i + 1) * mine)
        dm_ref[2 * j * mine : (2 * j + 1) * mine, :] = dk[part]
        dm_ref[(2 * j + 1) * mine : (2 * j + 2) * mine, :] = dv[part]


def backward_kernel(
    q_ref, pt_ref, ga_ref, ko_ref, vo_ref, kh_ref, vh_ref, km_ref, *rest, nb
):
    dq_ref, dko_ref, dvo_ref, dh_ref, ke, ve, q2, ds = rest[-8:]
    hrows = kh_ref.shape[0]
    ext = hrows + ko_ref.shape[0]
    fill_keys(ke, kh_ref, ko_ref, km_ref)
    ve[0:hrows, :SPAN] = vh_ref[...]
    ve[hrows:, :SPAN] = vo_ref[...]
    ve[:, SPAN:] = jnp.ones((ve.shape[0], SPAN), bf16)
    first = lax.broadcasted_iota(jnp.int32, (BLK, SPAN), 1) < HEAD_DIM
    unit = HEAD_DIM**-0.5
    for b in range(nb):
        rows, cols = slice(b * BLK, (b + 1) * BLK), slice(b * TWO, (b + 1) * TWO)
        band = slice(b * BLK, (b + FAR + 1) * BLK)
        q2[cols, :] = by_head(q_ref[rows, :] * jnp.asarray(unit, bf16), first)
        ga = ga_ref[0, cols, :]
        dp = dot(ve[band, :], ga, NT)
        ds[band, cols] = (pt_ref[0, band, cols].astype(f32) * dp).astype(bf16)
        dq = dot(ds[band, cols], ke[band, :], TN) + dot(pt_ref[0, ext:, cols], ke[ext:, :], TN)
        dq_ref[rows, :] = (join_heads(dq, first) * unit).astype(bf16)
    for e in range(ext // BLK):
        cols = slice(max(0, e - FAR) * TWO, (min(nb - 1, e) + 1) * TWO)
        rows = slice(e * BLK, (e + 1) * BLK)
        dv = dot(pt_ref[0, rows, cols], ga_ref[0, cols, :SPAN], NN)
        dk = dot(ds[rows, cols], q2[cols, :], NN)
        if e * BLK < hrows:
            dh_ref[rows, :] = dk.astype(bf16)
            dh_ref[hrows + e * BLK : hrows + (e + 1) * BLK, :] = dv.astype(bf16)
        else:
            own = slice(e * BLK - hrows, (e + 1) * BLK - hrows)
            dko_ref[own, :] = dk.astype(bf16)
            dvo_ref[own, :] = dv.astype(bf16)


def columns(rows, start):
    return pl.BlockSpec((rows, SPAN), lambda p, *_: (0, p + start))


ANY = pl.BlockSpec(memory_space=pl.ANY)


def forward(me, blocks, fill, slot_row, q, cot, weight, ko, vo, halo, mem, order, start, count, carry):
    tokens, width = q.shape
    slots, hrows, nb, pairs = mem.shape[0], halo.shape[0], tokens // BLK, width // SPAN
    keys = hrows + tokens + slots
    smem = pl.BlockSpec(memory_space=pltpu.SMEM)
    args = [me, blocks, fill, q, cot, weight, ko, vo, halo, halo, mem, mem, slot_row]
    specs = [
        smem, smem, smem, columns(tokens, start), pl.BlockSpec((tokens, width), lambda p: (0, 0)),
        pl.BlockSpec((SPAN, width), lambda p: (p + start, 0)), columns(tokens, start), columns(tokens, start),
        columns(hrows, 0), columns(hrows, count), columns(slots, start), columns(slots, pairs + start),
        pl.BlockSpec((1, slots), lambda p: (0, 0)),
    ]
    alias = {}
    if carry:
        alias = {len(args) + i: i for i in range(len(carry))}
        args += carry
        specs += [ANY] * len(carry)
    return pl.pallas_call(
        functools.partial(forward_kernel, nb=nb, order=order),
        grid=(count,),
        in_specs=specs,
        out_specs=[
            columns(tokens, start), columns(2 * slots, start),
            pl.BlockSpec((1, keys, nb * TWO), lambda p: (p, 0, 0)),
            pl.BlockSpec((1, nb * TWO, 2 * SPAN), lambda p: (p, 0, 0)),
        ],
        scratch_shapes=[
            pltpu.VMEM((keys, SPAN), bf16), pltpu.VMEM((keys, 2 * SPAN), bf16),
            pltpu.VMEM((nb * TWO, SPAN), bf16), pltpu.VMEM((slots, nb * TWO), bf16),
            pltpu.VMEM((nb, slots, BLK), f32), pltpu.VMEM((tokens, SPAN), bf16), pltpu.SMEM((2, nb), jnp.int32),
        ],
        out_shape=[
            jax.ShapeDtypeStruct((tokens, width), bf16),
            jax.ShapeDtypeStruct((2 * slots, width), bf16),
            jax.ShapeDtypeStruct((count, keys, nb * TWO), bf16),
            jax.ShapeDtypeStruct((count, nb * TWO, 2 * SPAN), bf16),
        ],
        input_output_aliases=alias,
        compiler_params=pltpu.CompilerParams(vmem_limit_bytes=67_000_000),
        cost_estimate=pl.CostEstimate(
            flops=count * nb * 12 * TWO * BLK * 1024, bytes_accessed=count * (4 << 20), transcendentals=count << 20
        ),
        name="band_forward",
    )(*args)


def prepare_kernel(me_ref, slots_ref, k_ref, v_ref, rows_ref, *halos, sizes):
    tokens, width = k_ref.shape
    mine = rows_ref.shape[0]
    row = lax.broadcasted_iota(jnp.int32, (mine, tokens), 0)
    slot = jnp.zeros((mine, tokens), jnp.int32)
    for r in range(mine):
        slot = jnp.where(row == r, slots_ref[0, me_ref[0] * mine + r], slot)
    pick = (slot == lax.broadcasted_iota(jnp.int32, (mine, tokens), 1)).astype(f32).astype(bf16)
    rows_ref[:, :width] = dot(pick, k_ref[...], NN).astype(bf16)
    rows_ref[:, width:] = dot(pick, v_ref[...], NN).astype(bf16)
    at = 0
    for halo, size in zip(halos, sizes):
        halo[:, :size] = k_ref[tokens - W :, at : at + size]
        halo[:, size:] = v_ref[tokens - W :, at : at + size]
        at += size


def prepare(me, slots, k, v, mine, sizes):
    smem, vmem = pl.BlockSpec(memory_space=pltpu.SMEM), pl.BlockSpec(memory_space=pltpu.VMEM)
    return pl.pallas_call(
        functools.partial(prepare_kernel, sizes=sizes),
        in_specs=[smem, smem, vmem, vmem],
        out_specs=[vmem] * (1 + len(sizes)),
        out_shape=[jax.ShapeDtypeStruct((mine, 2 * k.shape[1]), bf16)]
        + [jax.ShapeDtypeStruct((W, 2 * size), bf16) for size in sizes],
        compiler_params=pltpu.CompilerParams(vmem_limit_bytes=67_000_000),
        name="prepare_rows",
    )(me, slots, k, v)


def partial_kernel(core_ref, att_ref, cot_ref, dm_ref, send_ref, keep_ref, *, plane):
    half = att_ref.shape[1] // 2
    rows = half // plane
    for out, c in ((send_ref, 1 - core_ref[0]), (keep_ref, core_ref[0])):
        w = dot(att_ref[:, pl.ds(pl.multiple_of(c * half, half), half)], cot_ref[...], TN).astype(bf16)
        for j in range(plane):
            out[j, :rows, :] = w[j * rows : (j + 1) * rows]
            out[j, rows:, :] = dm_ref[j, c]


def weight_partial(core, att, cot, dm, plane):
    width, extra = att.shape[1], dm.shape[2]
    smem, vmem = pl.BlockSpec(memory_space=pltpu.SMEM), pl.BlockSpec(memory_space=pltpu.VMEM)
    shape = jax.ShapeDtypeStruct((plane, width // 2 // plane + extra, width), bf16)
    return pl.pallas_call(
        functools.partial(partial_kernel, plane=plane),
        in_specs=[smem, vmem, vmem, vmem],
        out_specs=[vmem, vmem],
        out_shape=[shape, shape],
        compiler_params=pltpu.CompilerParams(vmem_limit_bytes=67_000_000),
        cost_estimate=pl.CostEstimate(flops=1 << 30, bytes_accessed=5 << 20, transcendentals=0),
        name="weight_partial",
    )(core, att, cot, dm)


def backward(q, pt, ga, ko, vo, kh, vh, km, start, count, base, halo_at, at, carry, dh_total, dh_at):
    tokens, width = q.shape
    slots, hrows, nb = km.shape[0], kh.shape[0], tokens // BLK
    keys = hrows + tokens + slots
    kc, vc = halo_at
    args = [q, pt, ga, ko, vo, kh, vh, km]
    specs = [
        columns(tokens, start),
        pl.BlockSpec((1, keys, nb * TWO), lambda p, *_: (p + at, 0, 0)),
        pl.BlockSpec((1, nb * TWO, 2 * SPAN), lambda p, *_: (p + at, 0, 0)),
        columns(tokens, start), columns(tokens, start),
        columns(hrows, kc), columns(hrows, vc), columns(slots, base + start),
    ]
    alias = {}
    if carry:
        alias = {len(args) + i: i for i in range(len(carry))}
        args += carry
        specs += [ANY] * len(carry)
    return pl.pallas_call(
        functools.partial(backward_kernel, nb=nb),
        grid=(count,),
        in_specs=specs,
        out_specs=[
            columns(tokens, start), columns(tokens, start), columns(tokens, start),
            columns(2 * hrows, dh_at),
        ],
        scratch_shapes=[
            pltpu.VMEM((keys, SPAN), bf16), pltpu.VMEM((keys - slots, 2 * SPAN), bf16),
            pltpu.VMEM((nb * TWO, SPAN), bf16), pltpu.VMEM((keys - slots, nb * TWO), bf16),
        ],
        out_shape=[
            jax.ShapeDtypeStruct((tokens, width), bf16),
            jax.ShapeDtypeStruct((tokens, width), bf16),
            jax.ShapeDtypeStruct((tokens, width), bf16),
            jax.ShapeDtypeStruct((2 * hrows, dh_total * SPAN), bf16),
        ],
        input_output_aliases=alias,
        compiler_params=pltpu.CompilerParams(vmem_limit_bytes=67_000_000),
        cost_estimate=pl.CostEstimate(
            flops=count * nb * 20 * TWO * BLK * 1024, bytes_accessed=count * (6 << 20), transcendentals=0
        ),
        name="band_backward",
    )(*args)


def finish_kernel(slot_ref, dk_in, dv_in, dm_ref, *rest, segments):
    backs, (dk_ref, dv_ref) = rest[:-2], rest[-2:]
    rows = dk_in.shape[0]
    mine = slot_ref.shape[1]
    at = lax.broadcasted_iota(jnp.int32, (rows, mine), 0) + pl.program_id(0) * rows
    pick = (at == slot_ref[...]).astype(f32).astype(bf16)
    for g, pair, pos, count in segments:
        to, of = slice(pair * SPAN, (pair + count) * SPAN), slice(pos * SPAN, (pos + count) * SPAN)
        back = backs[g]
        dk = dk_in[:, to].astype(f32) + dot(pick, dm_ref[:mine, to], NN)
        dv = dv_in[:, to].astype(f32) + dot(pick, dm_ref[mine:, to], NN)
        dk_ref[:, to] = (dk + back[0, :, of].astype(f32)).astype(bf16)
        dv_ref[:, to] = (dv + back[1, :, of].astype(f32)).astype(bf16)


def finish(slots, dko, dvo, dmem, backs, segments):
    tokens, width = dko.shape
    mine = slots.shape[0]
    row = pl.BlockSpec((BLK, width), lambda r: (r, 0))
    return pl.pallas_call(
        functools.partial(finish_kernel, segments=segments),
        grid=(tokens // BLK,),
        in_specs=[pl.BlockSpec((1, mine), lambda r: (0, 0)), row, row, pl.BlockSpec((2 * mine, width), lambda r: (0, 0))]
        + [pl.BlockSpec((2, BLK, b.shape[-1]), lambda r: (0, r, 0)) for b in backs],
        out_specs=[row, row],
        out_shape=[jax.ShapeDtypeStruct((tokens, width), bf16)] * 2,
        compiler_params=pltpu.CompilerParams(vmem_limit_bytes=67_000_000),
        cost_estimate=pl.CostEstimate(flops=1 << 26, bytes_accessed=6 << 20, transcendentals=0),
        name="finish_rows",
    )(slots[None, :], dko, dvo, dmem, *backs)


def place_kernel(where_ref, *rest, plane, nfam, scale):
    n = 2 * plane
    parts, out_ref, buf, sems = rest[:n], rest[n], rest[n + 1], rest[n + 2]
    rows = parts[0].shape[0]
    piece = rows // nfam
    core, spot, fam = where_ref[0], where_ref[1], where_ref[2]
    copies = []
    for i, part in enumerate(parts):
        side = jnp.where(i < plane, core, 1 - core)
        at = pl.multiple_of((side * plane + (spot ^ (i % plane))) * rows, rows)
        for k in range(nfam):
            row = pl.multiple_of((fam ^ k) * piece, piece)
            buf[i, pl.ds(row, piece), :] = part[k * piece : (k + 1) * piece, :].astype(f32) * scale
        copies.append(pltpu.make_async_copy(buf.at[i], out_ref.at[pl.ds(at, rows), :], sems.at[i]))
        copies[-1].start()
    for copy in copies:
        copy.wait()


def place(where, parts, nfam, scale):
    rows, width = parts[0].shape
    n = len(parts)
    return pl.pallas_call(
        functools.partial(place_kernel, plane=n // 2, nfam=nfam, scale=scale),
        in_specs=[pl.BlockSpec(memory_space=pltpu.SMEM)] + [pl.BlockSpec(memory_space=pltpu.VMEM)] * n,
        out_specs=pl.BlockSpec(memory_space=pl.ANY),
        out_shape=jax.ShapeDtypeStruct((n * rows, width), f32),
        scratch_shapes=[pltpu.VMEM((n, rows, width), f32), pltpu.SemaphoreType.DMA((n,))],
        compiler_params=pltpu.CompilerParams(vmem_limit_bytes=67_000_000),
        cost_estimate=pl.CostEstimate(flops=1 << 20, bytes_accessed=6 << 20, transcendentals=0),
        name="place_rows",
    )(where, *parts)


def swap(x, axis, bits):
    return lax.ppermute(x, axis, [(i, i ^ bits) for i in range(lax.axis_size(axis))])


def bits_of(n):
    out, b = [], 1
    while b < n:
        out.append(b)
        b *= 2
    return out


def mirrored(n):
    order = [0]
    for bit in reversed(bits_of(n)):
        order = order + [i + bit for i in order]
    return order


def gather_rows(x, axis, me):
    for bit in reversed(bits_of(lax.axis_size(axis))):
        other = swap(x, axis, bit)
        upper = (me & bit) != 0
        x = jnp.where(upper, jnp.concatenate([other, x], 0), jnp.concatenate([x, other], 0))
    return x


def exchange(part, axis, shift, me, n):
    return [part(me)] + [swap(part(me ^ k).astype(bf16), axis, k << shift) for k in range(1, n)]


def spread(x, axis, shift, n):
    return [x] + [swap(x, axis, k << shift) for k in range(1, n)]


def total_of(parts):
    return sum([x.astype(f32) for x in parts[1:]], parts[0].astype(f32))


def groups_of(pairs):
    if pairs % 8:
        return [pairs], [(0, 0, pairs)], [pairs]
    u = pairs // 8
    return [3 * u, 5 * u], [(0, 0, u), (1, 0, 5 * u), (0, u, 2 * u)], [6 * u, 2 * u]


def per_device(queries, key_rows, value_rows, cotangent, out_weight, prot_blocks, last_fill, memory_slots):
    q, k, v, cot = queries[0], key_rows[0], value_rows[0], cotangent[0]
    slots = memory_slots[0]
    tokens, width = q.shape
    nctx, nfam = lax.axis_size("ctx"), lax.axis_size("fam")
    me, fam = lax.axis_index("ctx"), lax.axis_index("fam")
    total = slots.shape[0]
    mine = total // nctx
    pairs = width // SPAN
    fsizes, bplan, dhs = groups_of(pairs)
    fstarts = [sum(fsizes[:i]) for i in range(len(fsizes))]
    shift = [(i, i + 1) for i in range(nctx - 1)]
    back = [(i + 1, i) for i in range(nctx - 1)]
    where = jnp.stack([me]).astype(jnp.int32)
    rows, *halos = prepare(where, memory_slots, k, v, mine, [n * SPAN for n in fsizes])
    mem = gather_rows(rows, "ctx", me)
    halos = [lax.ppermute(x, "ctx", shift) for x in halos]
    order = mirrored(nctx)
    carry, saved = [], []
    for i, (at, count) in enumerate(zip(fstarts, fsizes)):
        att, dm, pt, ga = forward(
            where, prot_blocks, last_fill, memory_slots, q, cot, out_weight, k, v, halos[i], mem, order,
            at, count, carry)
        carry = [att, dm]
        saved.append((pt, ga))
    core, spot, plane = me & 1, me >> 1, nctx // 2
    at = lambda x, j, axis: lax.dynamic_index_in_dim(x, j, axis, keepdims=False)
    send, kept = weight_partial(
        jnp.stack([core]).astype(jnp.int32), att, cot, dm.reshape(plane, 2, 2 * mine, width), plane)
    sent = swap(send, "ctx", 1)
    carry, backs, segments, i = [], [], [], 0
    for total_dh in dhs:
        done = 0
        while done < total_dh:
            j, r, count = bplan[i]
            pt, ga = saved[j]
            out = backward(
                q, pt, ga, k, v, halos[j], halos[j], mem, fstarts[j] + r, count,
                0, (r, fsizes[j] + r), r, carry, total_dh, done)
            carry = list(out)
            segments.append((len(backs), fstarts[j] + r, done, count))
            done, i = done + count, i + 1
        backs.append(lax.ppermute(carry.pop(), "ctx", back))
    got = exchange(lambda j: at(sent, j, 0).astype(f32) + at(kept, j, 0).astype(f32), "ctx", 1, spot, plane)
    rows = width // nctx
    mem_grad = total_of([x[rows:] for x in got]).astype(bf16)
    piece = lambda j: total_of([lax.dynamic_slice_in_dim(x, j * (rows // nfam), rows // nfam) for x in got])
    w = total_of(exchange(piece, "fam", 0, fam, nfam)).astype(bf16)
    w = jnp.concatenate(spread(w, "fam", 0, nfam), 0)
    parts = spread(w, "ctx", 1, plane)
    parts = parts + [swap(x, "ctx", 1) for x in parts]
    scale = (nfam * nctx * tokens) ** -0.5
    weight = place(jnp.stack([core, spot, fam]).astype(jnp.int32), parts, nfam, scale)
    dq, dko, dvo = carry
    backs = [x.reshape(2, W, -1) for x in backs]
    dk, dv = finish(lax.dynamic_slice_in_dim(slots, me * mine, mine), dko, dvo, mem_grad, backs, segments)
    return dq[None], dk[None], dv[None], weight


def solution(mesh):
    row = P("fam", "ctx", None)
    small = P("fam", None)

    return jax.shard_map(
        per_device,
        mesh=mesh,
        in_specs=(row, row, row, row, P(), small, small, small),
        out_specs=(row, row, row, P()),
        check_vma=False,
    )
```

```python
import functools

import jax
import jax.numpy as jnp
from jax import lax
from jax.experimental import pallas as pl
from jax.experimental.pallas import tpu as pltpu
from jax.sharding import PartitionSpec as P


HEAD_DIM = 64
W = 512
BLK = 128
SPAN = 2 * HEAD_DIM
TWO = 2 * BLK
FAR = W // BLK
NEG = -1e30
NT = (((1,), (1,)), ((), ()))
NN = (((1,), (0,)), ((), ()))
TN = (((0,), (0,)), ((), ()))
f32 = jnp.float32
bf16 = jnp.bfloat16


def dot(a, b, dims):
    return lax.dot_general(a, b, dims, preferred_element_type=f32)


def by_head(x, first):
    zero = jnp.zeros_like(x)
    return jnp.concatenate([jnp.where(first, x, zero), jnp.where(first, zero, x)], 0)


def join_heads(x, first):
    return jnp.where(first, x[:BLK], x[BLK:])


def fill_keys(dst, halo, own, memory):
    h, o = halo.shape[0], own.shape[0]
    dst[0:h, :SPAN] = halo[...]
    dst[h : h + o, :SPAN] = own[...]
    dst[h + o :, :SPAN] = memory[...]


def tables(me, blocks_ref, fill_ref, slots_ref, info, bias, nb, tokens, order):
    nprot, slots = blocks_ref.shape[1], slots_ref.shape[1]
    mine = slots // len(order)
    begin = jnp.int32(0)
    first, left, pads = [0] * nb, [0] * nb, []
    for p in range(nprot):
        end = begin + blocks_ref[0, p]
        real = (end - 1) * BLK + fill_ref[0, p]
        pads.append((real, end * BLK))
        for b in range(nb):
            block = me * nb + b
            inside = (block >= begin) & (block < end)
            first[b] = jnp.where(inside, begin, first[b])
            left[b] = jnp.where(inside, real - block * BLK, left[b])
        begin = end
    for b in range(nb):
        info[0, b] = first[b] - (me * nb - FAR)
        info[1, b] = left[b]
    row = lax.broadcasted_iota(jnp.int32, (BLK, BLK), 0)
    for g in range(slots // BLK):
        lanes = jnp.broadcast_to(slots_ref[:, g * BLK : (g + 1) * BLK], (BLK, BLK))
        source = lanes.T + (row + g * BLK) // mine * tokens
        bad = jnp.zeros((BLK, BLK), f32)
        for lo, hi in pads:
            bad = jnp.where((source >= lo) & (source < hi), 1.0, bad)
        for b in range(nb):
            seen = jnp.where((source < first[b] * BLK) & (bad == 0.0), 0.0, NEG)
            for j in range(g * BLK // mine, (g + 1) * BLK // mine):
                i = order.index(j)
                bias[b, i * mine : (i + 1) * mine, :] = seen[j * mine - g * BLK : (j + 1) * mine - g * BLK]


def forward_kernel(
    me_ref, blocks_ref, fill_ref, q_ref, cot_ref, w_ref, ko_ref, vo_ref, kh_ref, vh_ref, km_ref, vm_ref, slots_ref,
    *rest, nb, order, start
):
    send_ref, keep_ref, pt, ga_ref, ke, ve, q2s, pm, mb_ref, g_ref, at_ref, w_buf, dm_buf, sems, info_ref = rest[-15:]
    slots = km_ref.shape[0]
    mine = slots // len(order)
    ext = kh_ref.shape[0] + ko_ref.shape[0]

    @pl.when(pl.program_id(0) == 0)
    def _():
        tables(me_ref[0], blocks_ref, fill_ref, slots_ref, info_ref, mb_ref, nb, ko_ref.shape[0], order)

    g_ref[...] = dot(cot_ref[...], w_ref[...], NT).astype(bf16)
    fill_keys(ke, kh_ref, ko_ref, km_ref)
    fill_keys(ve, vh_ref, vo_ref, vm_ref)
    ve[:, SPAN:] = jnp.ones((ve.shape[0], SPAN), bf16)
    first = lax.broadcasted_iota(jnp.int32, (BLK, SPAN), 1) < HEAD_DIM
    tri = (
        lax.broadcasted_iota(jnp.int32, (BLK, TWO), 0)
        <= lax.broadcasted_iota(jnp.int32, (BLK, TWO), 1) % BLK
    )
    lane = lax.broadcasted_iota(jnp.int32, (TWO, SPAN), 1)
    row = lax.broadcasted_iota(jnp.int32, (TWO, SPAN), 0) % BLK
    unit = jnp.asarray(HEAD_DIM**-0.5, bf16)
    at = lambda b: (slice(b * BLK, (b + 1) * BLK), slice(b * TWO, (b + 1) * TWO), slice(b * BLK, (b + FAR + 1) * BLK))
    scores, outs = {}, {}

    def score(b):
        rows, cols, band = at(b)
        q2 = by_head(q_ref[rows, :] * unit, first)
        q2s[cols, :] = q2
        scores[b] = (dot(ke[band, :], q2, NT), dot(ke[ext:, :], q2, NT))

    def exponentials(b):
        _, cols, _ = at(b)
        s, sm = scores.pop(b)
        sm = sm + jnp.concatenate([mb_ref[b], mb_ref[b]], 1)
        off = [jnp.where(e + b >= info_ref[0, b], 0.0, NEG).astype(f32) for e in range(FAR)]
        ends = jnp.where(tri, s[FAR * BLK :, :], s[:BLK, :] + off[0])
        mid = [s[e * BLK : (e + 1) * BLK, :] for e in range(1, FAR)]
        m = jnp.maximum(jnp.max(ends, 0, keepdims=True), jnp.max(sm, 0, keepdims=True))
        for e in range(1, FAR):
            m = jnp.maximum(m, jnp.max(mid[e - 1], 0, keepdims=True) + off[e])
        for e in range(1, FAR):
            pt[0, (b + e) * BLK : (b + e + 1) * BLK, cols] = jnp.exp(
                mid[e - 1] - (m - off[e])
            ).astype(bf16)
        pm[:, cols] = jnp.exp(sm - m).astype(bf16)
        p = jnp.exp(ends - m).astype(bf16)
        zero = jnp.zeros_like(p)
        pt[0, b * BLK : (b + 1) * BLK, cols] = jnp.where(tri, zero, p)
        pt[0, (b + FAR) * BLK : (b + FAR + 1) * BLK, cols] = jnp.where(tri, p, zero)

    def attend(b):
        _, cols, band = at(b)
        outs[b] = dot(pt[0, band, cols], ve[band, :], TN) + dot(pm[:, cols], ve[ext:, :], TN)

    def gradients(b):
        rows, cols, _ = at(b)
        o = outs.pop(b)
        scale = jnp.where(row < info_ref[1, b], 1.0 / o[:, SPAN:], 0.0)
        o = o[:, :SPAN] * scale
        at_ref[rows, :] = join_heads(o, first).astype(bf16)
        g2 = (by_head(g_ref[rows, :].astype(f32), first) * scale).astype(bf16)
        d = -jnp.sum(g2.astype(f32) * o, 1, keepdims=True)
        high = d.astype(bf16).astype(f32)
        ga_ref[0, cols, :SPAN] = g2
        ga_ref[0, cols, SPAN:] = jnp.where(
            lane == 0, high, jnp.where(lane == 1, d - high, 0.0)
        ).astype(bf16)

    def memory(b):
        _, cols, _ = at(b)
        dp = dot(ve[ext:, :], ga_ref[0, cols, :], NT)
        pt[0, ext:, cols] = (pm[:, cols].astype(f32) * dp).astype(bf16)

    for t in range(nb + 4):
        for stage, lag in ((score, 0), (attend, 2), (exponentials, 1), (memory, 4), (gradients, 3)):
            if 0 <= t - lag < nb:
                stage(t - lag)
    step, plane, width = pl.program_id(0), len(order) // 2, cot_ref.shape[1]
    core, slot, rows = me_ref[0] & 1, lax.rem(step, 2), width // len(order)
    dk = dot(pt[0, ext:, :], q2s[...], NN).astype(bf16)
    dv = dot(pm[...], ga_ref[0, :, :SPAN], NN).astype(bf16)
    for i, j in enumerate(order):
        part = slice(i * mine, (i + 1) * mine)
        dm_buf[slot, j % 2, j // 2, :mine, :] = dk[part]
        dm_buf[slot, j % 2, j // 2, mine:, :] = dv[part]
    w_buf[slot] = dot(at_ref[...], cot_ref[...], TN).astype(bf16)

    def copies(at, slot):
        pair = start + at
        out = []
        for t in range(max(1, SPAN // rows)):
            block = pair * (SPAN // rows) + t
            out.append((block // plane == core, lambda ref, t=t, block=block: pltpu.make_async_copy(
                w_buf.at[slot, pl.ds(t * rows, rows), :], ref.at[lax.rem(block, plane), pl.ds(0, rows), :],
                sems.at[slot, 2 + t])))
        for side in range(2):
            out.append((core == side, lambda ref, side=side: pltpu.make_async_copy(
                dm_buf.at[slot, side],
                ref.at[:, pl.ds(rows, 2 * mine), pl.ds(pl.multiple_of(pair * SPAN, SPAN), SPAN)],
                sems.at[slot, side])))
        return out

    for stays, copy in copies(step, slot):

        @pl.when(stays)
        def _():
            copy(keep_ref).start()

        @pl.when(jnp.logical_not(stays))
        def _():
            copy(send_ref).start()

    @pl.when(step > 0)
    def _():
        for _, copy in copies(step - 1, 1 - slot):
            copy(keep_ref).wait()

    @pl.when(step == pl.num_programs(0) - 1)
    def _():
        for _, copy in copies(step, slot):
            copy(keep_ref).wait()


def backward_kernel(
    q_ref, pt_ref, ga_ref, ko_ref, vo_ref, kh_ref, vh_ref, km_ref, *rest, nb
):
    dq_ref, dko_ref, dvo_ref, dh_ref, ke, ve, q2, ds = rest[-8:]
    hrows = kh_ref.shape[0]
    ext = hrows + ko_ref.shape[0]
    fill_keys(ke, kh_ref, ko_ref, km_ref)
    ve[0:hrows, :SPAN] = vh_ref[...]
    ve[hrows:, :SPAN] = vo_ref[...]
    ve[:, SPAN:] = jnp.ones((ve.shape[0], SPAN), bf16)
    first = lax.broadcasted_iota(jnp.int32, (BLK, SPAN), 1) < HEAD_DIM
    unit = HEAD_DIM**-0.5
    for b in range(nb):
        rows, cols = slice(b * BLK, (b + 1) * BLK), slice(b * TWO, (b + 1) * TWO)
        band = slice(b * BLK, (b + FAR + 1) * BLK)
        q2[cols, :] = by_head(q_ref[rows, :] * jnp.asarray(unit, bf16), first)
        ga = ga_ref[0, cols, :]
        dp = dot(ve[band, :], ga, NT)
        ds[band, cols] = (pt_ref[0, band, cols].astype(f32) * dp).astype(bf16)
        dq = dot(ds[band, cols], ke[band, :], TN) + dot(pt_ref[0, ext:, cols], ke[ext:, :], TN)
        dq_ref[rows, :] = (join_heads(dq, first) * unit).astype(bf16)
    for e in range(ext // BLK):
        cols = slice(max(0, e - FAR) * TWO, (min(nb - 1, e) + 1) * TWO)
        rows = slice(e * BLK, (e + 1) * BLK)
        dv = dot(pt_ref[0, rows, cols], ga_ref[0, cols, :SPAN], NN)
        dk = dot(ds[rows, cols], q2[cols, :], NN)
        if e * BLK < hrows:
            dh_ref[rows, :] = dk.astype(bf16)
            dh_ref[hrows + e * BLK : hrows + (e + 1) * BLK, :] = dv.astype(bf16)
        else:
            own = slice(e * BLK - hrows, (e + 1) * BLK - hrows)
            dko_ref[own, :] = dk.astype(bf16)
            dvo_ref[own, :] = dv.astype(bf16)


def columns(rows, start):
    return pl.BlockSpec((rows, SPAN), lambda p, *_: (0, p + start))


ANY = pl.BlockSpec(memory_space=pl.ANY)


def forward(me, blocks, fill, slot_row, q, cot, weight, ko, vo, halo, mem, order, start, count, carry):
    tokens, width = q.shape
    slots, hrows, nb, pairs = mem.shape[0], halo.shape[0], tokens // BLK, width // SPAN
    keys = hrows + tokens + slots
    smem = pl.BlockSpec(memory_space=pltpu.SMEM)
    members, plane = len(order), len(order) // 2
    rows, extra = width // members, 2 * slots // members
    out = jax.ShapeDtypeStruct((plane, rows + extra, width), bf16)
    args = [me, blocks, fill, q, cot, weight, ko, vo, halo, halo, mem, mem, slot_row]
    specs = [
        smem, smem, smem, columns(tokens, start), pl.BlockSpec((tokens, width), lambda p: (0, 0)),
        pl.BlockSpec((SPAN, width), lambda p: (p + start, 0)), columns(tokens, start), columns(tokens, start),
        columns(hrows, 0), columns(hrows, count), columns(slots, start), columns(slots, pairs + start),
        pl.BlockSpec((1, slots), lambda p: (0, 0)),
    ]
    alias = {}
    if carry:
        alias = {len(args) + i: i for i in range(len(carry))}
        args += carry
        specs += [ANY] * len(carry)
    return pl.pallas_call(
        functools.partial(forward_kernel, nb=nb, order=order, start=start),
        grid=(count,),
        in_specs=specs,
        out_specs=[
            ANY, ANY,
            pl.BlockSpec((1, keys, nb * TWO), lambda p: (p, 0, 0)),
            pl.BlockSpec((1, nb * TWO, 2 * SPAN), lambda p: (p, 0, 0)),
        ],
        scratch_shapes=[
            pltpu.VMEM((keys, SPAN), bf16), pltpu.VMEM((keys, 2 * SPAN), bf16),
            pltpu.VMEM((nb * TWO, SPAN), bf16), pltpu.VMEM((slots, nb * TWO), bf16),
            pltpu.VMEM((nb, slots, BLK), f32), pltpu.VMEM((tokens, SPAN), bf16),
            pltpu.VMEM((tokens, SPAN), bf16), pltpu.VMEM((2, SPAN, width), bf16),
            pltpu.VMEM((2, 2, plane, extra, SPAN), bf16), pltpu.SemaphoreType.DMA((2, 2 + SPAN // rows)),
            pltpu.SMEM((2, nb), jnp.int32),
        ],
        out_shape=[
            out, out,
            jax.ShapeDtypeStruct((count, keys, nb * TWO), bf16),
            jax.ShapeDtypeStruct((count, nb * TWO, 2 * SPAN), bf16),
        ],
        input_output_aliases=alias,
        compiler_params=pltpu.CompilerParams(vmem_limit_bytes=67_000_000),
        cost_estimate=pl.CostEstimate(
            flops=count * nb * 12 * TWO * BLK * 1024, bytes_accessed=count * (4 << 20), transcendentals=count << 20
        ),
        name="band_forward",
    )(*args)


def prepare_kernel(me_ref, slots_ref, k_ref, v_ref, rows_ref, *halos, sizes):
    tokens, width = k_ref.shape
    mine = rows_ref.shape[0]
    row = lax.broadcasted_iota(jnp.int32, (mine, tokens), 0)
    slot = jnp.zeros((mine, tokens), jnp.int32)
    for r in range(mine):
        slot = jnp.where(row == r, slots_ref[0, me_ref[0] * mine + r], slot)
    pick = (slot == lax.broadcasted_iota(jnp.int32, (mine, tokens), 1)).astype(f32).astype(bf16)
    rows_ref[:, :width] = dot(pick, k_ref[...], NN).astype(bf16)
    rows_ref[:, width:] = dot(pick, v_ref[...], NN).astype(bf16)
    at = 0
    for halo, size in zip(halos, sizes):
        halo[:, :size] = k_ref[tokens - W :, at : at + size]
        halo[:, size:] = v_ref[tokens - W :, at : at + size]
        at += size


def prepare(me, slots, k, v, mine, sizes):
    smem, vmem = pl.BlockSpec(memory_space=pltpu.SMEM), pl.BlockSpec(memory_space=pltpu.VMEM)
    return pl.pallas_call(
        functools.partial(prepare_kernel, sizes=sizes),
        in_specs=[smem, smem, vmem, vmem],
        out_specs=[vmem] * (1 + len(sizes)),
        out_shape=[jax.ShapeDtypeStruct((mine, 2 * k.shape[1]), bf16)]
        + [jax.ShapeDtypeStruct((W, 2 * size), bf16) for size in sizes],
        compiler_params=pltpu.CompilerParams(vmem_limit_bytes=67_000_000),
        name="prepare_rows",
    )(me, slots, k, v)


def backward(q, pt, ga, ko, vo, kh, vh, km, start, count, base, halo_at, at, carry, dh_total, dh_at):
    tokens, width = q.shape
    slots, hrows, nb = km.shape[0], kh.shape[0], tokens // BLK
    keys = hrows + tokens + slots
    kc, vc = halo_at
    args = [q, pt, ga, ko, vo, kh, vh, km]
    specs = [
        columns(tokens, start),
        pl.BlockSpec((1, keys, nb * TWO), lambda p, *_: (p + at, 0, 0)),
        pl.BlockSpec((1, nb * TWO, 2 * SPAN), lambda p, *_: (p + at, 0, 0)),
        columns(tokens, start), columns(tokens, start),
        columns(hrows, kc), columns(hrows, vc), columns(slots, base + start),
    ]
    alias = {}
    if carry:
        alias = {len(args) + i: i for i in range(len(carry))}
        args += carry
        specs += [ANY] * len(carry)
    return pl.pallas_call(
        functools.partial(backward_kernel, nb=nb),
        grid=(count,),
        in_specs=specs,
        out_specs=[
            columns(tokens, start), columns(tokens, start), columns(tokens, start),
            columns(2 * hrows, dh_at),
        ],
        scratch_shapes=[
            pltpu.VMEM((keys, SPAN), bf16), pltpu.VMEM((keys - slots, 2 * SPAN), bf16),
            pltpu.VMEM((nb * TWO, SPAN), bf16), pltpu.VMEM((keys - slots, nb * TWO), bf16),
        ],
        out_shape=[
            jax.ShapeDtypeStruct((tokens, width), bf16),
            jax.ShapeDtypeStruct((tokens, width), bf16),
            jax.ShapeDtypeStruct((tokens, width), bf16),
            jax.ShapeDtypeStruct((2 * hrows, dh_total * SPAN), bf16),
        ],
        input_output_aliases=alias,
        compiler_params=pltpu.CompilerParams(vmem_limit_bytes=67_000_000),
        cost_estimate=pl.CostEstimate(
            flops=count * nb * 20 * TWO * BLK * 1024, bytes_accessed=count * (6 << 20), transcendentals=0
        ),
        name="band_backward",
    )(*args)


def finish_kernel(slot_ref, dk_in, dv_in, dm_ref, *rest, segments):
    backs, (dk_ref, dv_ref) = rest[:-2], rest[-2:]
    rows = dk_in.shape[0]
    mine = slot_ref.shape[1]
    at = lax.broadcasted_iota(jnp.int32, (rows, mine), 0) + pl.program_id(0) * rows
    pick = (at == slot_ref[...]).astype(f32).astype(bf16)
    for g, pair, pos, count in segments:
        to, of = slice(pair * SPAN, (pair + count) * SPAN), slice(pos * SPAN, (pos + count) * SPAN)
        back = backs[g]
        dk = dk_in[:, to].astype(f32) + dot(pick, dm_ref[:mine, to], NN)
        dv = dv_in[:, to].astype(f32) + dot(pick, dm_ref[mine:, to], NN)
        dk_ref[:, to] = (dk + back[0, :, of].astype(f32)).astype(bf16)
        dv_ref[:, to] = (dv + back[1, :, of].astype(f32)).astype(bf16)


def finish(slots, dko, dvo, dmem, backs, segments):
    tokens, width = dko.shape
    mine = slots.shape[0]
    row = pl.BlockSpec((BLK, width), lambda r: (r, 0))
    return pl.pallas_call(
        functools.partial(finish_kernel, segments=segments),
        grid=(tokens // BLK,),
        in_specs=[pl.BlockSpec((1, mine), lambda r: (0, 0)), row, row, pl.BlockSpec((2 * mine, width), lambda r: (0, 0))]
        + [pl.BlockSpec((2, BLK, b.shape[-1]), lambda r: (0, r, 0)) for b in backs],
        out_specs=[row, row],
        out_shape=[jax.ShapeDtypeStruct((tokens, width), bf16)] * 2,
        compiler_params=pltpu.CompilerParams(vmem_limit_bytes=67_000_000),
        cost_estimate=pl.CostEstimate(flops=1 << 26, bytes_accessed=6 << 20, transcendentals=0),
        name="finish_rows",
    )(slots[None, :], dko, dvo, dmem, *backs)


def place_kernel(where_ref, *rest, plane, scale):
    n = 2 * plane
    parts, out_ref, buf, sems = rest[:n], rest[n], rest[n + 1], rest[n + 2]
    rows = parts[0].shape[0]
    core, spot = where_ref[0], where_ref[1]
    copies = []
    for i, part in enumerate(parts):
        side = jnp.where(i < plane, core, 1 - core)
        at = pl.multiple_of((side * plane + (spot ^ (i % plane))) * rows, rows)
        buf[i] = part[...].astype(f32) * scale
        copies.append(pltpu.make_async_copy(buf.at[i], out_ref.at[pl.ds(at, rows), :], sems.at[i]))
        copies[-1].start()
    for copy in copies:
        copy.wait()


def place(where, parts, scale):
    rows, width = parts[0].shape
    n = len(parts)
    return pl.pallas_call(
        functools.partial(place_kernel, plane=n // 2, scale=scale),
        in_specs=[pl.BlockSpec(memory_space=pltpu.SMEM)] + [pl.BlockSpec(memory_space=pltpu.VMEM)] * n,
        out_specs=pl.BlockSpec(memory_space=pl.ANY),
        out_shape=jax.ShapeDtypeStruct((n * rows, width), f32),
        scratch_shapes=[pltpu.VMEM((n, rows, width), f32), pltpu.SemaphoreType.DMA((n,))],
        compiler_params=pltpu.CompilerParams(vmem_limit_bytes=67_000_000),
        cost_estimate=pl.CostEstimate(flops=1 << 20, bytes_accessed=6 << 20, transcendentals=0),
        name="place_rows",
    )(where, *parts)


def swap(x, axis, bits):
    return lax.ppermute(x, axis, [(i, i ^ bits) for i in range(lax.axis_size(axis))])


def bits_of(n):
    out, b = [], 1
    while b < n:
        out.append(b)
        b *= 2
    return out


def mirrored(n):
    order = [0]
    for bit in reversed(bits_of(n)):
        order = order + [i + bit for i in order]
    return order


def gather_rows(x, axis, me):
    for bit in reversed(bits_of(lax.axis_size(axis))):
        other = swap(x, axis, bit)
        upper = (me & bit) != 0
        x = jnp.where(upper, jnp.concatenate([other, x], 0), jnp.concatenate([x, other], 0))
    return x


def exchange(part, axis, shift, me, n):
    return [part(me)] + [swap(part(me ^ k).astype(bf16), axis, k << shift) for k in range(1, n)]


def spread(x, axis, shift, n):
    return [x] + [swap(x, axis, k << shift) for k in range(1, n)]


def total_of(parts):
    return sum([x.astype(f32) for x in parts[1:]], parts[0].astype(f32))


def groups_of(pairs):
    if pairs % 8:
        return [pairs], [(0, 0, pairs)], [pairs]
    u = pairs // 8
    return [2 * u, 6 * u], [(0, 0, 2 * u), (1, 0, 4 * u), (1, 4 * u, 2 * u)], [6 * u, 2 * u]


def per_device(queries, key_rows, value_rows, cotangent, out_weight, prot_blocks, last_fill, memory_slots):
    q, k, v, cot = queries[0], key_rows[0], value_rows[0], cotangent[0]
    slots = memory_slots[0]
    tokens, width = q.shape
    nctx, nfam = lax.axis_size("ctx"), lax.axis_size("fam")
    me = lax.axis_index("ctx")
    total = slots.shape[0]
    mine = total // nctx
    pairs = width // SPAN
    fsizes, bplan, dhs = groups_of(pairs)
    fstarts = [sum(fsizes[:i]) for i in range(len(fsizes))]
    shift = [(i, i + 1) for i in range(nctx - 1)]
    back = [(i + 1, i) for i in range(nctx - 1)]
    where = jnp.stack([me]).astype(jnp.int32)
    rows, *halos = prepare(where, memory_slots, k, v, mine, [n * SPAN for n in fsizes])
    mem = gather_rows(rows, "ctx", me)
    halos = [lax.ppermute(x, "ctx", shift) for x in halos]
    order = mirrored(nctx)
    carry, saved = [], []
    for i, (at, count) in enumerate(zip(fstarts, fsizes)):
        send, kept, pt, ga = forward(
            where, prot_blocks, last_fill, memory_slots, q, cot, out_weight, k, v, halos[i], mem, order,
            at, count, carry)
        carry = [send, kept]
        saved.append((pt, ga))
    core, spot, plane = me & 1, me >> 1, nctx // 2
    at = lambda x, j, axis: lax.dynamic_index_in_dim(x, j, axis, keepdims=False)
    sent = swap(send, "ctx", 1)
    carry, backs, segments, i = [], [], [], 0
    for total_dh in dhs:
        done = 0
        while done < total_dh:
            j, r, count = bplan[i]
            pt, ga = saved[j]
            out = backward(
                q, pt, ga, k, v, halos[j], halos[j], mem, fstarts[j] + r, count,
                0, (r, fsizes[j] + r), r, carry, total_dh, done)
            carry = list(out)
            segments.append((len(backs), fstarts[j] + r, done, count))
            done, i = done + count, i + 1
        backs.append(lax.ppermute(carry.pop(), "ctx", back))
    got = exchange(lambda j: at(sent, j, 0).astype(f32) + at(kept, j, 0).astype(f32), "ctx", 1, spot, plane)
    rows = width // nctx
    mem_grad = total_of([x[rows:] for x in got]).astype(bf16)
    w = total_of([x[:rows] for x in got]).astype(bf16)
    for i, bit in enumerate(bits_of(nfam)):
        w = total_of([w, swap(w, "fam", bit)]).astype(bf16)
    parts = spread(w, "ctx", 1, plane)
    parts = parts + [swap(x, "ctx", 1) for x in parts]
    scale = (nfam * nctx * tokens) ** -0.5
    weight = place(jnp.stack([core, spot]).astype(jnp.int32), parts, scale)
    dq, dko, dvo = carry
    backs = [x.reshape(2, W, -1) for x in backs]
    dk, dv = finish(lax.dynamic_slice_in_dim(slots, me * mine, mine), dko, dvo, mem_grad, backs, segments)
    return dq[None], dk[None], dv[None], weight


def solution(mesh):
    row = P("fam", "ctx", None)
    small = P("fam", None)

    return jax.shard_map(
        per_device,
        mesh=mesh,
        in_specs=(row, row, row, row, P(), small, small, small),
        out_specs=(row, row, row, P()),
        check_vma=False,
    )
```

```python
import functools

import jax
import jax.numpy as jnp
from jax import lax
from jax.experimental import pallas as pl
from jax.experimental.pallas import tpu as pltpu
from jax.sharding import PartitionSpec as P


HEAD_DIM = 64
W = 512
BLK = 128
SPAN = 2 * HEAD_DIM
TWO = 2 * BLK
FAR = W // BLK
NEG = -1e30
NT = (((1,), (1,)), ((), ()))
NN = (((1,), (0,)), ((), ()))
TN = (((0,), (0,)), ((), ()))
f32 = jnp.float32
bf16 = jnp.bfloat16


def dot(a, b, dims):
    return lax.dot_general(a, b, dims, preferred_element_type=f32)


def by_head(x, first):
    zero = jnp.zeros_like(x)
    return jnp.concatenate([jnp.where(first, x, zero), jnp.where(first, zero, x)], 0)


def join_heads(x, first):
    return jnp.where(first, x[:BLK], x[BLK:])


def fill_keys(dst, halo, own, memory):
    h, o = halo.shape[0], own.shape[0]
    dst[0:h, :SPAN] = halo[...]
    dst[h : h + o, :SPAN] = own[...]
    dst[h + o :, :SPAN] = memory[...]


def tables(me, blocks_ref, fill_ref, slots_ref, info, bias, nb, tokens, order):
    nprot, slots = blocks_ref.shape[1], slots_ref.shape[1]
    mine = slots // len(order)
    begin = jnp.int32(0)
    first, left, pads = [0] * nb, [0] * nb, []
    for p in range(nprot):
        end = begin + blocks_ref[0, p]
        real = (end - 1) * BLK + fill_ref[0, p]
        pads.append((real, end * BLK))
        for b in range(nb):
            block = me * nb + b
            inside = (block >= begin) & (block < end)
            first[b] = jnp.where(inside, begin, first[b])
            left[b] = jnp.where(inside, real - block * BLK, left[b])
        begin = end
    for b in range(nb):
        info[0, b] = first[b] - (me * nb - FAR)
        info[1, b] = left[b]
    row = lax.broadcasted_iota(jnp.int32, (BLK, BLK), 0)
    for g in range(slots // BLK):
        lanes = jnp.broadcast_to(slots_ref[:, g * BLK : (g + 1) * BLK], (BLK, BLK))
        source = lanes.T + (row + g * BLK) // mine * tokens
        bad = jnp.zeros((BLK, BLK), f32)
        for lo, hi in pads:
            bad = jnp.where((source >= lo) & (source < hi), 1.0, bad)
        for b in range(nb):
            seen = jnp.where((source < first[b] * BLK) & (bad == 0.0), 0.0, NEG)
            for j in range(g * BLK // mine, (g + 1) * BLK // mine):
                i = order.index(j)
                bias[b, i * mine : (i + 1) * mine, :] = seen[j * mine - g * BLK : (j + 1) * mine - g * BLK]


def forward_kernel(
    me_ref, blocks_ref, fill_ref, q_ref, cot_ref, g_ref, ko_ref, vo_ref, kh_ref, vh_ref, km_ref, vm_ref, slots_ref,
    *rest, nb, order, start
):
    send_ref, keep_ref, pt, ga_ref, ke, ve, q2s, pm, mb_ref, at_ref, w_buf, dm_buf, sems, info_ref = rest[-14:]
    slots = km_ref.shape[0]
    mine = slots // len(order)
    ext = kh_ref.shape[0] + ko_ref.shape[0]

    @pl.when(pl.program_id(0) == 0)
    def _():
        tables(me_ref[0], blocks_ref, fill_ref, slots_ref, info_ref, mb_ref, nb, ko_ref.shape[0], order)

    fill_keys(ke, kh_ref, ko_ref, km_ref)
    fill_keys(ve, vh_ref, vo_ref, vm_ref)
    ve[:, SPAN:] = jnp.ones((ve.shape[0], SPAN), bf16)
    first = lax.broadcasted_iota(jnp.int32, (BLK, SPAN), 1) < HEAD_DIM
    tri = (
        lax.broadcasted_iota(jnp.int32, (BLK, TWO), 0)
        <= lax.broadcasted_iota(jnp.int32, (BLK, TWO), 1) % BLK
    )
    lane = lax.broadcasted_iota(jnp.int32, (TWO, SPAN), 1)
    row = lax.broadcasted_iota(jnp.int32, (TWO, SPAN), 0) % BLK
    unit = jnp.asarray(HEAD_DIM**-0.5, bf16)
    at = lambda b: (slice(b * BLK, (b + 1) * BLK), slice(b * TWO, (b + 1) * TWO), slice(b * BLK, (b + FAR + 1) * BLK))
    scores, outs = {}, {}

    def score(b):
        rows, cols, band = at(b)
        q2 = by_head(q_ref[rows, :] * unit, first)
        q2s[cols, :] = q2
        scores[b] = (dot(ke[band, :], q2, NT), dot(ke[ext:, :], q2, NT))

    def exponentials(b):
        _, cols, _ = at(b)
        s, sm = scores.pop(b)
        sm = sm + jnp.concatenate([mb_ref[b], mb_ref[b]], 1)
        off = [jnp.where(e + b >= info_ref[0, b], 0.0, NEG).astype(f32) for e in range(FAR)]
        ends = jnp.where(tri, s[FAR * BLK :, :], s[:BLK, :] + off[0])
        mid = [s[e * BLK : (e + 1) * BLK, :] for e in range(1, FAR)]
        m = jnp.maximum(jnp.max(ends, 0, keepdims=True), jnp.max(sm, 0, keepdims=True))
        for e in range(1, FAR):
            m = jnp.maximum(m, jnp.max(mid[e - 1], 0, keepdims=True) + off[e])
        for e in range(1, FAR):
            pt[0, (b + e) * BLK : (b + e + 1) * BLK, cols] = jnp.exp(
                mid[e - 1] - (m - off[e])
            ).astype(bf16)
        pm[:, cols] = jnp.exp(sm - m).astype(bf16)
        p = jnp.exp(ends - m).astype(bf16)
        zero = jnp.zeros_like(p)
        pt[0, b * BLK : (b + 1) * BLK, cols] = jnp.where(tri, zero, p)
        pt[0, (b + FAR) * BLK : (b + FAR + 1) * BLK, cols] = jnp.where(tri, p, zero)

    def attend(b):
        _, cols, band = at(b)
        outs[b] = dot(pt[0, band, cols], ve[band, :], TN) + dot(pm[:, cols], ve[ext:, :], TN)

    def gradients(b):
        rows, cols, _ = at(b)
        o = outs.pop(b)
        scale = jnp.where(row < info_ref[1, b], 1.0 / o[:, SPAN:], 0.0)
        o = o[:, :SPAN] * scale
        at_ref[rows, :] = join_heads(o, first).astype(bf16)
        g2 = (by_head(g_ref[rows, :].astype(f32), first) * scale).astype(bf16)
        d = -jnp.sum(g2.astype(f32) * o, 1, keepdims=True)
        high = d.astype(bf16).astype(f32)
        ga_ref[0, cols, :SPAN] = g2
        ga_ref[0, cols, SPAN:] = jnp.where(
            lane == 0, high, jnp.where(lane == 1, d - high, 0.0)
        ).astype(bf16)

    def memory(b):
        _, cols, _ = at(b)
        dp = dot(ve[ext:, :], ga_ref[0, cols, :], NT)
        pt[0, ext:, cols] = (pm[:, cols].astype(f32) * dp).astype(bf16)

    for t in range(nb + 4):
        for stage, lag in ((score, 0), (attend, 2), (exponentials, 1), (memory, 4), (gradients, 3)):
            if 0 <= t - lag < nb:
                stage(t - lag)
    step, plane, width = pl.program_id(0), len(order) // 2, cot_ref.shape[1]
    core, slot, rows = me_ref[0] & 1, lax.rem(step, 2), width // len(order)
    dk = dot(pt[0, ext:, :], q2s[...], NN).astype(bf16)
    dv = dot(pm[...], ga_ref[0, :, :SPAN], NN).astype(bf16)
    for i, j in enumerate(order):
        part = slice(i * mine, (i + 1) * mine)
        dm_buf[slot, j % 2, j // 2, :mine, :] = dk[part]
        dm_buf[slot, j % 2, j // 2, mine:, :] = dv[part]
    w_buf[slot] = dot(at_ref[...], cot_ref[...], TN).astype(bf16)

    def copies(at, slot):
        pair = start + at
        out = []
        for t in range(max(1, SPAN // rows)):
            block = pair * (SPAN // rows) + t
            out.append((block // plane == core, lambda ref, t=t, block=block: pltpu.make_async_copy(
                w_buf.at[slot, pl.ds(t * rows, rows), :], ref.at[lax.rem(block, plane), pl.ds(0, rows), :],
                sems.at[slot, 2 + t])))
        for side in range(2):
            out.append((core == side, lambda ref, side=side: pltpu.make_async_copy(
                dm_buf.at[slot, side],
                ref.at[:, pl.ds(rows, 2 * mine), pl.ds(pl.multiple_of(pair * SPAN, SPAN), SPAN)],
                sems.at[slot, side])))
        return out

    for stays, copy in copies(step, slot):

        @pl.when(stays)
        def _():
            copy(keep_ref).start()

        @pl.when(jnp.logical_not(stays))
        def _():
            copy(send_ref).start()

    @pl.when(step > 0)
    def _():
        for _, copy in copies(step - 1, 1 - slot):
            copy(keep_ref).wait()

    @pl.when(step == pl.num_programs(0) - 1)
    def _():
        for _, copy in copies(step, slot):
            copy(keep_ref).wait()


def backward_kernel(
    q_ref, pt_ref, ga_ref, ko_ref, vo_ref, kh_ref, vh_ref, km_ref, *rest, nb
):
    dq_ref, dko_ref, dvo_ref, dh_ref, ke, ve, q2, ds = rest[-8:]
    hrows = kh_ref.shape[0]
    ext = hrows + ko_ref.shape[0]
    fill_keys(ke, kh_ref, ko_ref, km_ref)
    ve[0:hrows, :SPAN] = vh_ref[...]
    ve[hrows:, :SPAN] = vo_ref[...]
    ve[:, SPAN:] = jnp.ones((ve.shape[0], SPAN), bf16)
    first = lax.broadcasted_iota(jnp.int32, (BLK, SPAN), 1) < HEAD_DIM
    unit = HEAD_DIM**-0.5
    for b in range(nb):
        rows, cols = slice(b * BLK, (b + 1) * BLK), slice(b * TWO, (b + 1) * TWO)
        band = slice(b * BLK, (b + FAR + 1) * BLK)
        q2[cols, :] = by_head(q_ref[rows, :] * jnp.asarray(unit, bf16), first)
        ga = ga_ref[0, cols, :]
        dp = dot(ve[band, :], ga, NT)
        ds[band, cols] = (pt_ref[0, band, cols].astype(f32) * dp).astype(bf16)
        dq = dot(ds[band, cols], ke[band, :], TN) + dot(pt_ref[0, ext:, cols], ke[ext:, :], TN)
        dq_ref[rows, :] = (join_heads(dq, first) * unit).astype(bf16)
    for e in range(ext // BLK):
        cols = slice(max(0, e - FAR) * TWO, (min(nb - 1, e) + 1) * TWO)
        rows = slice(e * BLK, (e + 1) * BLK)
        dv = dot(pt_ref[0, rows, cols], ga_ref[0, cols, :SPAN], NN)
        dk = dot(ds[rows, cols], q2[cols, :], NN)
        if e * BLK < hrows:
            dh_ref[rows, :] = dk.astype(bf16)
            dh_ref[hrows + e * BLK : hrows + (e + 1) * BLK, :] = dv.astype(bf16)
        else:
            own = slice(e * BLK - hrows, (e + 1) * BLK - hrows)
            dko_ref[own, :] = dk.astype(bf16)
            dvo_ref[own, :] = dv.astype(bf16)


def columns(rows, start):
    return pl.BlockSpec((rows, SPAN), lambda p, *_: (0, p + start))


ANY = pl.BlockSpec(memory_space=pl.ANY)


def forward(me, blocks, fill, slot_row, q, cot, g, ko, vo, halo, mem, order, start, count, carry):
    tokens, width = q.shape
    slots, hrows, nb, pairs = mem.shape[0], halo.shape[0], tokens // BLK, width // SPAN
    keys = hrows + tokens + slots
    smem = pl.BlockSpec(memory_space=pltpu.SMEM)
    members, plane = len(order), len(order) // 2
    rows, extra = width // members, 2 * slots // members
    out = jax.ShapeDtypeStruct((plane, rows + extra, width), bf16)
    args = [me, blocks, fill, q, cot, g, ko, vo, halo, halo, mem, mem, slot_row]
    specs = [
        smem, smem, smem, columns(tokens, start), pl.BlockSpec((tokens, width), lambda p: (0, 0)),
        columns(tokens, start), columns(tokens, start), columns(tokens, start),
        columns(hrows, 0), columns(hrows, count), columns(slots, start), columns(slots, pairs + start),
        pl.BlockSpec((1, slots), lambda p: (0, 0)),
    ]
    alias = {}
    if carry:
        alias = {len(args) + i: i for i in range(len(carry))}
        args += carry
        specs += [ANY] * len(carry)
    return pl.pallas_call(
        functools.partial(forward_kernel, nb=nb, order=order, start=start),
        grid=(count,),
        in_specs=specs,
        out_specs=[
            ANY, ANY,
            pl.BlockSpec((1, keys, nb * TWO), lambda p: (p, 0, 0)),
            pl.BlockSpec((1, nb * TWO, 2 * SPAN), lambda p: (p, 0, 0)),
        ],
        scratch_shapes=[
            pltpu.VMEM((keys, SPAN), bf16), pltpu.VMEM((keys, 2 * SPAN), bf16),
            pltpu.VMEM((nb * TWO, SPAN), bf16), pltpu.VMEM((slots, nb * TWO), bf16),
            pltpu.VMEM((nb, slots, BLK), f32),
            pltpu.VMEM((tokens, SPAN), bf16), pltpu.VMEM((2, SPAN, width), bf16),
            pltpu.VMEM((2, 2, plane, extra, SPAN), bf16), pltpu.SemaphoreType.DMA((2, 2 + SPAN // rows)),
            pltpu.SMEM((2, nb), jnp.int32),
        ],
        out_shape=[
            out, out,
            jax.ShapeDtypeStruct((count, keys, nb * TWO), bf16),
            jax.ShapeDtypeStruct((count, nb * TWO, 2 * SPAN), bf16),
        ],
        input_output_aliases=alias,
        compiler_params=pltpu.CompilerParams(vmem_limit_bytes=67_000_000),
        cost_estimate=pl.CostEstimate(
            flops=count * nb * 12 * TWO * BLK * 1024, bytes_accessed=count * (4 << 20), transcendentals=count << 20
        ),
        name="band_forward",
    )(*args)


def prepare_kernel(me_ref, slots_ref, k_ref, v_ref, rows_ref, *halos, sizes):
    tokens, width = k_ref.shape
    mine = rows_ref.shape[0]
    row = lax.broadcasted_iota(jnp.int32, (mine, tokens), 0)
    slot = jnp.zeros((mine, tokens), jnp.int32)
    for r in range(mine):
        slot = jnp.where(row == r, slots_ref[0, me_ref[0] * mine + r], slot)
    pick = (slot == lax.broadcasted_iota(jnp.int32, (mine, tokens), 1)).astype(f32).astype(bf16)
    rows_ref[:, :width] = dot(pick, k_ref[...], NN).astype(bf16)
    rows_ref[:, width:] = dot(pick, v_ref[...], NN).astype(bf16)
    at = 0
    for halo, size in zip(halos, sizes):
        halo[:, :size] = k_ref[tokens - W :, at : at + size]
        halo[:, size:] = v_ref[tokens - W :, at : at + size]
        at += size


def prepare(me, slots, k, v, mine, sizes):
    smem, vmem = pl.BlockSpec(memory_space=pltpu.SMEM), pl.BlockSpec(memory_space=pltpu.VMEM)
    return pl.pallas_call(
        functools.partial(prepare_kernel, sizes=sizes),
        in_specs=[smem, smem, vmem, vmem],
        out_specs=[vmem] * (1 + len(sizes)),
        out_shape=[jax.ShapeDtypeStruct((mine, 2 * k.shape[1]), bf16)]
        + [jax.ShapeDtypeStruct((W, 2 * size), bf16) for size in sizes],
        compiler_params=pltpu.CompilerParams(vmem_limit_bytes=67_000_000),
        name="prepare_rows",
    )(me, slots, k, v)


def backward(q, pt, ga, ko, vo, kh, vh, km, start, count, base, halo_at, at, carry, dh_total, dh_at):
    tokens, width = q.shape
    slots, hrows, nb = km.shape[0], kh.shape[0], tokens // BLK
    keys = hrows + tokens + slots
    kc, vc = halo_at
    args = [q, pt, ga, ko, vo, kh, vh, km]
    specs = [
        columns(tokens, start),
        pl.BlockSpec((1, keys, nb * TWO), lambda p, *_: (p + at, 0, 0)),
        pl.BlockSpec((1, nb * TWO, 2 * SPAN), lambda p, *_: (p + at, 0, 0)),
        columns(tokens, start), columns(tokens, start),
        columns(hrows, kc), columns(hrows, vc), columns(slots, base + start),
    ]
    alias = {}
    if carry:
        alias = {len(args) + i: i for i in range(len(carry))}
        args += carry
        specs += [ANY] * len(carry)
    return pl.pallas_call(
        functools.partial(backward_kernel, nb=nb),
        grid=(count,),
        in_specs=specs,
        out_specs=[
            columns(tokens, start), columns(tokens, start), columns(tokens, start),
            columns(2 * hrows, dh_at),
        ],
        scratch_shapes=[
            pltpu.VMEM((keys, SPAN), bf16), pltpu.VMEM((keys - slots, 2 * SPAN), bf16),
            pltpu.VMEM((nb * TWO, SPAN), bf16), pltpu.VMEM((keys - slots, nb * TWO), bf16),
        ],
        out_shape=[
            jax.ShapeDtypeStruct((tokens, width), bf16),
            jax.ShapeDtypeStruct((tokens, width), bf16),
            jax.ShapeDtypeStruct((tokens, width), bf16),
            jax.ShapeDtypeStruct((2 * hrows, dh_total * SPAN), bf16),
        ],
        input_output_aliases=alias,
        compiler_params=pltpu.CompilerParams(vmem_limit_bytes=67_000_000),
        cost_estimate=pl.CostEstimate(
            flops=count * nb * 20 * TWO * BLK * 1024, bytes_accessed=count * (6 << 20), transcendentals=0
        ),
        name="band_backward",
    )(*args)


def finish_kernel(slot_ref, dk_in, dv_in, dm_ref, *rest, segments):
    backs, (dk_ref, dv_ref) = rest[:-2], rest[-2:]
    rows = dk_in.shape[0]
    mine = slot_ref.shape[1]
    at = lax.broadcasted_iota(jnp.int32, (rows, mine), 0) + pl.program_id(0) * rows
    pick = (at == slot_ref[...]).astype(f32).astype(bf16)
    for g, pair, pos, count in segments:
        to, of = slice(pair * SPAN, (pair + count) * SPAN), slice(pos * SPAN, (pos + count) * SPAN)
        back = backs[g]
        dk = dk_in[:, to].astype(f32) + dot(pick, dm_ref[:mine, to], NN)
        dv = dv_in[:, to].astype(f32) + dot(pick, dm_ref[mine:, to], NN)
        dk_ref[:, to] = (dk + back[0, :, of].astype(f32)).astype(bf16)
        dv_ref[:, to] = (dv + back[1, :, of].astype(f32)).astype(bf16)


def finish(slots, dko, dvo, dmem, backs, segments):
    tokens, width = dko.shape
    mine = slots.shape[0]
    step = 2 * BLK
    row = pl.BlockSpec((step, width), lambda r: (r, 0))
    return pl.pallas_call(
        functools.partial(finish_kernel, segments=segments),
        grid=(tokens // step,),
        in_specs=[pl.BlockSpec((1, mine), lambda r: (0, 0)), row, row, pl.BlockSpec((2 * mine, width), lambda r: (0, 0))]
        + [pl.BlockSpec((2, step, b.shape[-1]), lambda r: (0, r, 0)) for b in backs],
        out_specs=[row, row],
        out_shape=[jax.ShapeDtypeStruct((tokens, width), bf16)] * 2,
        compiler_params=pltpu.CompilerParams(vmem_limit_bytes=67_000_000),
        cost_estimate=pl.CostEstimate(flops=1 << 26, bytes_accessed=6 << 20, transcendentals=0),
        name="finish_rows",
    )(slots[None, :], dko, dvo, dmem, *backs)


def place_kernel(where_ref, *rest, plane, nfam, scale, flip):
    parts, (out_ref, buf, sems) = rest[:plane], rest[-3:]
    rows = parts[0].shape[0]
    piece = rows // nfam
    side, spot, fam = (where_ref[0] & 1) ^ flip, lax.div(where_ref[0], 2), where_ref[1]
    copies = []
    for i, part in enumerate(parts):
        at = pl.multiple_of((side * plane + (spot ^ i)) * rows, rows)
        for k in range(nfam):
            row = pl.multiple_of((fam ^ k) * piece, piece)
            buf[i, pl.ds(row, piece), :] = part[k * piece : (k + 1) * piece, :].astype(f32) * scale
        copies.append(pltpu.make_async_copy(buf.at[i], out_ref.at[pl.ds(at, rows), :], sems.at[i]))
        copies[-1].start()
    for copy in copies:
        copy.wait()


def place(where, parts, nfam, scale, flip, carry):
    rows, width = parts[0].shape
    n = len(parts)
    more = [] if carry is None else [carry]
    return pl.pallas_call(
        functools.partial(place_kernel, plane=n, nfam=nfam, scale=scale, flip=flip),
        in_specs=[pl.BlockSpec(memory_space=pltpu.SMEM)] + [pl.BlockSpec(memory_space=pltpu.VMEM)] * n + [ANY] * len(more),
        out_specs=ANY,
        out_shape=jax.ShapeDtypeStruct((2 * n * rows, width), f32),
        scratch_shapes=[pltpu.VMEM((n, rows, width), f32), pltpu.SemaphoreType.DMA((n,))],
        input_output_aliases={1 + n: 0} if more else {},
        compiler_params=pltpu.CompilerParams(vmem_limit_bytes=67_000_000),
        cost_estimate=pl.CostEstimate(flops=1 << 20, bytes_accessed=3 << 20, transcendentals=0),
        name="place_rows",
    )(where, *parts, *more)


def swap(x, axis, bits):
    return lax.ppermute(x, axis, [(i, i ^ bits) for i in range(lax.axis_size(axis))])


def bits_of(n):
    out, b = [], 1
    while b < n:
        out.append(b)
        b *= 2
    return out


def mirrored(n):
    order = [0]
    for bit in reversed(bits_of(n)):
        order = order + [i + bit for i in order]
    return order


def gather_rows(x, axis, me):
    for bit in reversed(bits_of(lax.axis_size(axis))):
        other = swap(x, axis, bit)
        upper = (me & bit) != 0
        x = jnp.where(upper, jnp.concatenate([other, x], 0), jnp.concatenate([x, other], 0))
    return x


def exchange(part, axis, shift, me, n):
    return [part(me)] + [swap(part(me ^ k).astype(bf16), axis, k << shift) for k in range(1, n)]


def spread(x, axis, shift, n):
    return [x] + [swap(x, axis, k << shift) for k in range(1, n)]


def total_of(parts):
    return sum([x.astype(f32) for x in parts[1:]], parts[0].astype(f32))


def groups_of(pairs):
    if pairs % 8:
        return [pairs], [(0, 0, pairs)], [pairs]
    u = pairs // 8
    return [3 * u, 5 * u], [(0, 0, u), (1, 0, 5 * u), (0, u, 2 * u)], [6 * u, 2 * u]


def per_device(queries, key_rows, value_rows, cotangent, out_weight, prot_blocks, last_fill, memory_slots):
    q, k, v, cot = queries[0], key_rows[0], value_rows[0], cotangent[0]
    slots = memory_slots[0]
    tokens, width = q.shape
    nctx, nfam = lax.axis_size("ctx"), lax.axis_size("fam")
    me, fam = lax.axis_index("ctx"), lax.axis_index("fam")
    total = slots.shape[0]
    mine = total // nctx
    pairs = width // SPAN
    fsizes, bplan, dhs = groups_of(pairs)
    fstarts = [sum(fsizes[:i]) for i in range(len(fsizes))]
    shift = [(i, i + 1) for i in range(nctx - 1)]
    back = [(i + 1, i) for i in range(nctx - 1)]
    where = jnp.stack([me, fam]).astype(jnp.int32)
    rows, *halos = prepare(where, memory_slots, k, v, mine, [n * SPAN for n in fsizes])
    mem = gather_rows(rows, "ctx", me)
    halos = [lax.ppermute(x, "ctx", shift) for x in halos]
    grad_attn = dot(cot, out_weight, NT).astype(bf16)
    order = mirrored(nctx)
    carry, saved = [], []
    for i, (at, count) in enumerate(zip(fstarts, fsizes)):
        send, kept, pt, ga = forward(
            where, prot_blocks, last_fill, memory_slots, q, cot, grad_attn, k, v, halos[i], mem, order,
            at, count, carry)
        carry = [send, kept]
        saved.append((pt, ga))
    spot, plane = me >> 1, nctx // 2
    at = lambda x, j, axis: lax.dynamic_index_in_dim(x, j, axis, keepdims=False)
    sent = swap(send, "ctx", 1)
    carry, backs, segments, i = [], [], [], 0
    for total_dh in dhs:
        done = 0
        while done < total_dh:
            j, r, count = bplan[i]
            pt, ga = saved[j]
            out = backward(
                q, pt, ga, k, v, halos[j], halos[j], mem, fstarts[j] + r, count,
                0, (r, fsizes[j] + r), r, carry, total_dh, done)
            carry = list(out)
            segments.append((len(backs), fstarts[j] + r, done, count))
            done, i = done + count, i + 1
        backs.append(lax.ppermute(carry.pop(), "ctx", back))
    got = exchange(lambda j: at(sent, j, 0).astype(f32) + at(kept, j, 0).astype(f32), "ctx", 1, spot, plane)
    rows = width // nctx
    mem_grad = total_of([x[rows:] for x in got]).astype(bf16)
    piece = lambda j: total_of([lax.dynamic_slice_in_dim(x, j * (rows // nfam), rows // nfam) for x in got])
    w = total_of(exchange(piece, "fam", 0, fam, nfam)).astype(bf16)
    w = jnp.concatenate(spread(w, "fam", 0, nfam), 0)
    parts = spread(w, "ctx", 1, plane)
    others = [swap(x, "ctx", 1) for x in parts]
    scale = (nfam * nctx * tokens) ** -0.5
    weight = place(where, parts, nfam, scale, 0, None)
    weight = place(where, others, nfam, scale, 1, weight)
    dq, dko, dvo = carry
    backs = [x.reshape(2, W, -1) for x in backs]
    dk, dv = finish(lax.dynamic_slice_in_dim(slots, me * mine, mine), dko, dvo, mem_grad, backs, segments)
    return dq[None], dk[None], dv[None], weight


def solution(mesh):
    row = P("fam", "ctx", None)
    small = P("fam", None)

    return jax.shard_map(
        per_device,
        mesh=mesh,
        in_specs=(row, row, row, row, P(), small, small, small),
        out_specs=(row, row, row, P()),
        check_vma=False,
    )
```

```python
import functools

import jax
import jax.numpy as jnp
from jax import lax
from jax.experimental import pallas as pl
from jax.experimental.pallas import tpu as pltpu
from jax.sharding import PartitionSpec as P


HEAD_DIM = 64
W = 512
BLK = 128
SPAN = 2 * HEAD_DIM
TWO = 2 * BLK
FAR = W // BLK
NEG = -1e30
NT = (((1,), (1,)), ((), ()))
NN = (((1,), (0,)), ((), ()))
TN = (((0,), (0,)), ((), ()))
f32 = jnp.float32
bf16 = jnp.bfloat16


def dot(a, b, dims):
    return lax.dot_general(a, b, dims, preferred_element_type=f32)


def by_head(x, first):
    zero = jnp.zeros_like(x)
    return jnp.concatenate([jnp.where(first, x, zero), jnp.where(first, zero, x)], 0)


def join_heads(x, first):
    return jnp.where(first, x[:BLK], x[BLK:])


def fill_keys(dst, halo, own, memory):
    h, o = halo.shape[0], own.shape[0]
    dst[0:h, :SPAN] = halo[...]
    dst[h : h + o, :SPAN] = own[...]
    dst[h + o :, :SPAN] = memory[...]


def tables(me, blocks_ref, fill_ref, slots_ref, info, bias, nb, tokens, order):
    nprot, slots = blocks_ref.shape[1], slots_ref.shape[1]
    mine = slots // len(order)
    begin = jnp.int32(0)
    first, left, pads = [0] * nb, [0] * nb, []
    for p in range(nprot):
        end = begin + blocks_ref[0, p]
        real = (end - 1) * BLK + fill_ref[0, p]
        pads.append((real, end * BLK))
        for b in range(nb):
            block = me * nb + b
            inside = (block >= begin) & (block < end)
            first[b] = jnp.where(inside, begin, first[b])
            left[b] = jnp.where(inside, real - block * BLK, left[b])
        begin = end
    for b in range(nb):
        info[0, b] = first[b] - (me * nb - FAR)
        info[1, b] = left[b]
    row = lax.broadcasted_iota(jnp.int32, (BLK, BLK), 0)
    for g in range(slots // BLK):
        lanes = jnp.broadcast_to(slots_ref[:, g * BLK : (g + 1) * BLK], (BLK, BLK))
        source = lanes.T + (row + g * BLK) // mine * tokens
        bad = jnp.zeros((BLK, BLK), f32)
        for lo, hi in pads:
            bad = jnp.where((source >= lo) & (source < hi), 1.0, bad)
        for b in range(nb):
            seen = jnp.where((source < first[b] * BLK) & (bad == 0.0), 0.0, NEG)
            for j in range(g * BLK // mine, (g + 1) * BLK // mine):
                i = order.index(j)
                bias[b, i * mine : (i + 1) * mine, :] = seen[j * mine - g * BLK : (j + 1) * mine - g * BLK]


def forward_kernel(
    me_ref, blocks_ref, fill_ref, q_ref, cot_ref, g_ref, ko_ref, vo_ref, kh_ref, vh_ref, km_ref, vm_ref, slots_ref,
    *rest, nb, order, start
):
    send_ref, keep_ref, pt, ga_ref, ke, ve, q2s, pm, mb_ref, at_ref, w_buf, dm_buf, sems, info_ref = rest[-14:]
    slots = km_ref.shape[0]
    mine = slots // len(order)
    ext = kh_ref.shape[0] + ko_ref.shape[0]

    @pl.when(pl.program_id(0) == 0)
    def _():
        tables(me_ref[0], blocks_ref, fill_ref, slots_ref, info_ref, mb_ref, nb, ko_ref.shape[0], order)

    fill_keys(ke, kh_ref, ko_ref, km_ref)
    fill_keys(ve, vh_ref, vo_ref, vm_ref)
    ve[:, SPAN:] = jnp.ones((ve.shape[0], SPAN), bf16)
    first = lax.broadcasted_iota(jnp.int32, (BLK, SPAN), 1) < HEAD_DIM
    tri = (
        lax.broadcasted_iota(jnp.int32, (BLK, TWO), 0)
        <= lax.broadcasted_iota(jnp.int32, (BLK, TWO), 1) % BLK
    )
    lane = lax.broadcasted_iota(jnp.int32, (TWO, SPAN), 1)
    row = lax.broadcasted_iota(jnp.int32, (TWO, SPAN), 0) % BLK
    unit = jnp.asarray(HEAD_DIM**-0.5, bf16)
    at = lambda b: (slice(b * BLK, (b + 1) * BLK), slice(b * TWO, (b + 1) * TWO), slice(b * BLK, (b + FAR + 1) * BLK))
    scores, outs = {}, {}

    def score(b):
        rows, cols, band = at(b)
        q2 = by_head(q_ref[rows, :] * unit, first)
        q2s[cols, :] = q2
        scores[b] = (dot(ke[band, :], q2, NT), dot(ke[ext:, :], q2, NT))

    def exponentials(b):
        _, cols, _ = at(b)
        s, sm = scores.pop(b)
        sm = sm + jnp.concatenate([mb_ref[b], mb_ref[b]], 1)
        off = [jnp.where(e + b >= info_ref[0, b], 0.0, NEG).astype(f32) for e in range(FAR)]
        ends = jnp.where(tri, s[FAR * BLK :, :], s[:BLK, :] + off[0])
        mid = [s[e * BLK : (e + 1) * BLK, :] for e in range(1, FAR)]
        m = jnp.maximum(jnp.max(ends, 0, keepdims=True), jnp.max(sm, 0, keepdims=True))
        for e in range(1, FAR):
            m = jnp.maximum(m, jnp.max(mid[e - 1], 0, keepdims=True) + off[e])
        for e in range(1, FAR):
            pt[0, (b + e) * BLK : (b + e + 1) * BLK, cols] = jnp.exp(
                mid[e - 1] - (m - off[e])
            ).astype(bf16)
        pm[:, cols] = jnp.exp(sm - m).astype(bf16)
        p = jnp.exp(ends - m).astype(bf16)
        zero = jnp.zeros_like(p)
        pt[0, b * BLK : (b + 1) * BLK, cols] = jnp.where(tri, zero, p)
        pt[0, (b + FAR) * BLK : (b + FAR + 1) * BLK, cols] = jnp.where(tri, p, zero)

    def attend(b):
        _, cols, band = at(b)
        outs[b] = dot(pt[0, band, cols], ve[band, :], TN) + dot(pm[:, cols], ve[ext:, :], TN)

    def gradients(b):
        rows, cols, _ = at(b)
        o = outs.pop(b)
        scale = jnp.where(row < info_ref[1, b], 1.0 / o[:, SPAN:], 0.0)
        o = o[:, :SPAN] * scale
        at_ref[rows, :] = join_heads(o, first).astype(bf16)
        g2 = (by_head(g_ref[rows, :].astype(f32), first) * scale).astype(bf16)
        d = -jnp.sum(g2.astype(f32) * o, 1, keepdims=True)
        high = d.astype(bf16).astype(f32)
        ga_ref[0, cols, :SPAN] = g2
        ga_ref[0, cols, SPAN:] = jnp.where(
            lane == 0, high, jnp.where(lane == 1, d - high, 0.0)
        ).astype(bf16)

    def memory(b):
        _, cols, _ = at(b)
        dp = dot(ve[ext:, :], ga_ref[0, cols, :], NT)
        pt[0, ext:, cols] = (pm[:, cols].astype(f32) * dp).astype(bf16)

    for t in range(nb + 4):
        for stage, lag in ((score, 0), (attend, 2), (exponentials, 1), (memory, 4), (gradients, 3)):
            if 0 <= t - lag < nb:
                stage(t - lag)
    step, plane, width = pl.program_id(0), len(order) // 2, cot_ref.shape[1]
    core, slot, rows = me_ref[0] & 1, lax.rem(step, 2), width // len(order)
    dk = dot(pt[0, ext:, :], q2s[...], NN).astype(bf16)
    dv = dot(pm[...], ga_ref[0, :, :SPAN], NN).astype(bf16)
    for i, j in enumerate(order):
        part = slice(i * mine, (i + 1) * mine)
        dm_buf[slot, j % 2, j // 2, :mine, :] = dk[part]
        dm_buf[slot, j % 2, j // 2, mine:, :] = dv[part]
    w_buf[slot] = dot(at_ref[...], cot_ref[...], TN).astype(bf16)

    def copies(at, slot):
        pair = start + at
        out = []
        for t in range(max(1, SPAN // rows)):
            block = pair * (SPAN // rows) + t
            out.append((block // plane == core, lambda ref, t=t, block=block: pltpu.make_async_copy(
                w_buf.at[slot, pl.ds(t * rows, rows), :], ref.at[lax.rem(block, plane), pl.ds(0, rows), :],
                sems.at[slot, 2 + t])))
        for side in range(2):
            out.append((core == side, lambda ref, side=side: pltpu.make_async_copy(
                dm_buf.at[slot, side],
                ref.at[:, pl.ds(rows, 2 * mine), pl.ds(pl.multiple_of(pair * SPAN, SPAN), SPAN)],
                sems.at[slot, side])))
        return out

    for stays, copy in copies(step, slot):

        @pl.when(stays)
        def _():
            copy(keep_ref).start()

        @pl.when(jnp.logical_not(stays))
        def _():
            copy(send_ref).start()

    @pl.when(step > 0)
    def _():
        for _, copy in copies(step - 1, 1 - slot):
            copy(keep_ref).wait()

    @pl.when(step == pl.num_programs(0) - 1)
    def _():
        for _, copy in copies(step, slot):
            copy(keep_ref).wait()


def backward_kernel(
    q_ref, pt_ref, ga_ref, ko_ref, vo_ref, kh_ref, vh_ref, km_ref, *rest, nb
):
    dq_ref, dko_ref, dvo_ref, dh_ref, ke, ve, q2, ds = rest[-8:]
    hrows = kh_ref.shape[0]
    ext = hrows + ko_ref.shape[0]
    fill_keys(ke, kh_ref, ko_ref, km_ref)
    ve[0:hrows, :SPAN] = vh_ref[...]
    ve[hrows:, :SPAN] = vo_ref[...]
    ve[:, SPAN:] = jnp.ones((ve.shape[0], SPAN), bf16)
    first = lax.broadcasted_iota(jnp.int32, (BLK, SPAN), 1) < HEAD_DIM
    unit = HEAD_DIM**-0.5
    for b in range(nb):
        rows, cols = slice(b * BLK, (b + 1) * BLK), slice(b * TWO, (b + 1) * TWO)
        band = slice(b * BLK, (b + FAR + 1) * BLK)
        q2[cols, :] = by_head(q_ref[rows, :] * jnp.asarray(unit, bf16), first)
        ga = ga_ref[0, cols, :]
        dp = dot(ve[band, :], ga, NT)
        ds[band, cols] = (pt_ref[0, band, cols].astype(f32) * dp).astype(bf16)
        dq = dot(ds[band, cols], ke[band, :], TN) + dot(pt_ref[0, ext:, cols], ke[ext:, :], TN)
        dq_ref[rows, :] = (join_heads(dq, first) * unit).astype(bf16)
    for e in range(ext // BLK):
        cols = slice(max(0, e - FAR) * TWO, (min(nb - 1, e) + 1) * TWO)
        rows = slice(e * BLK, (e + 1) * BLK)
        dv = dot(pt_ref[0, rows, cols], ga_ref[0, cols, :SPAN], NN)
        dk = dot(ds[rows, cols], q2[cols, :], NN)
        if e * BLK < hrows:
            dh_ref[rows, :] = dk.astype(bf16)
            dh_ref[hrows + e * BLK : hrows + (e + 1) * BLK, :] = dv.astype(bf16)
        else:
            own = slice(e * BLK - hrows, (e + 1) * BLK - hrows)
            dko_ref[own, :] = dk.astype(bf16)
            dvo_ref[own, :] = dv.astype(bf16)


def columns(rows, start):
    return pl.BlockSpec((rows, SPAN), lambda p, *_: (0, p + start))


ANY = pl.BlockSpec(memory_space=pl.ANY)


def forward(me, blocks, fill, slot_row, q, cot, g, ko, vo, halo, mem, order, start, count, carry):
    tokens, width = q.shape
    slots, hrows, nb, pairs = mem.shape[0], halo.shape[0], tokens // BLK, width // SPAN
    keys = hrows + tokens + slots
    smem = pl.BlockSpec(memory_space=pltpu.SMEM)
    members, plane = len(order), len(order) // 2
    rows, extra = width // members, 2 * slots // members
    out = jax.ShapeDtypeStruct((plane, rows + extra, width), bf16)
    args = [me, blocks, fill, q, cot, g, ko, vo, halo, halo, mem, mem, slot_row]
    specs = [
        smem, smem, smem, columns(tokens, start), pl.BlockSpec((tokens, width), lambda p: (0, 0)),
        columns(tokens, start), columns(tokens, start), columns(tokens, start),
        columns(hrows, 0), columns(hrows, count), columns(slots, start), columns(slots, pairs + start),
        pl.BlockSpec((1, slots), lambda p: (0, 0)),
    ]
    alias = {}
    if carry:
        alias = {len(args) + i: i for i in range(len(carry))}
        args += carry
        specs += [ANY] * len(carry)
    return pl.pallas_call(
        functools.partial(forward_kernel, nb=nb, order=order, start=start),
        grid=(count,),
        in_specs=specs,
        out_specs=[
            ANY, ANY,
            pl.BlockSpec((1, keys, nb * TWO), lambda p: (p, 0, 0)),
            pl.BlockSpec((1, nb * TWO, 2 * SPAN), lambda p: (p, 0, 0)),
        ],
        scratch_shapes=[
            pltpu.VMEM((keys, SPAN), bf16), pltpu.VMEM((keys, 2 * SPAN), bf16),
            pltpu.VMEM((nb * TWO, SPAN), bf16), pltpu.VMEM((slots, nb * TWO), bf16),
            pltpu.VMEM((nb, slots, BLK), f32),
            pltpu.VMEM((tokens, SPAN), bf16), pltpu.VMEM((2, SPAN, width), bf16),
            pltpu.VMEM((2, 2, plane, extra, SPAN), bf16), pltpu.SemaphoreType.DMA((2, 2 + SPAN // rows)),
            pltpu.SMEM((2, nb), jnp.int32),
        ],
        out_shape=[
            out, out,
            jax.ShapeDtypeStruct((count, keys, nb * TWO), bf16),
            jax.ShapeDtypeStruct((count, nb * TWO, 2 * SPAN), bf16),
        ],
        input_output_aliases=alias,
        compiler_params=pltpu.CompilerParams(vmem_limit_bytes=67_000_000),
        cost_estimate=pl.CostEstimate(
            flops=count * nb * 12 * TWO * BLK * 1024, bytes_accessed=count * (4 << 20), transcendentals=count << 20
        ),
        name="band_forward",
    )(*args)


def rows_kernel(me_ref, slots_ref, k_ref, v_ref, rows_ref):
    tokens, width = k_ref.shape
    mine = rows_ref.shape[0]
    row = lax.broadcasted_iota(jnp.int32, (mine, tokens), 0)
    slot = jnp.zeros((mine, tokens), jnp.int32)
    for r in range(mine):
        slot = jnp.where(row == r, slots_ref[0, me_ref[0] * mine + r], slot)
    pick = (slot == lax.broadcasted_iota(jnp.int32, (mine, tokens), 1)).astype(f32).astype(bf16)
    rows_ref[:, :width] = dot(pick, k_ref[...], NN).astype(bf16)
    rows_ref[:, width:] = dot(pick, v_ref[...], NN).astype(bf16)


def memory_rows(me, slots, k, v, mine):
    smem, vmem = pl.BlockSpec(memory_space=pltpu.SMEM), pl.BlockSpec(memory_space=pltpu.VMEM)
    return pl.pallas_call(
        rows_kernel,
        in_specs=[smem, smem, vmem, vmem],
        out_specs=vmem,
        out_shape=jax.ShapeDtypeStruct((mine, 2 * k.shape[1]), bf16),
        compiler_params=pltpu.CompilerParams(vmem_limit_bytes=67_000_000),
        name="memory_rows",
    )(me, slots, k, v)


def halo_kernel(k_ref, v_ref, *halos, sizes):
    edge, at = k_ref.shape[0] - W, 0
    for halo, size in zip(halos, sizes):
        halo[:, :size] = k_ref[edge:, at : at + size]
        halo[:, size:] = v_ref[edge:, at : at + size]
        at += size


def halo_groups(k, v, sizes):
    vmem = pl.BlockSpec(memory_space=pltpu.VMEM)
    return pl.pallas_call(
        functools.partial(halo_kernel, sizes=sizes),
        in_specs=[vmem, vmem],
        out_specs=[vmem] * len(sizes),
        out_shape=[jax.ShapeDtypeStruct((W, 2 * size), bf16) for size in sizes],
        compiler_params=pltpu.CompilerParams(vmem_limit_bytes=67_000_000),
        cost_estimate=pl.CostEstimate(flops=0, bytes_accessed=4 << 20, transcendentals=0),
        name="halo_groups",
    )(k, v)


def backward(q, pt, ga, ko, vo, kh, vh, km, start, count, base, halo_at, at, carry, dh_total, dh_at):
    tokens, width = q.shape
    slots, hrows, nb = km.shape[0], kh.shape[0], tokens // BLK
    keys = hrows + tokens + slots
    kc, vc = halo_at
    args = [q, pt, ga, ko, vo, kh, vh, km]
    specs = [
        columns(tokens, start),
        pl.BlockSpec((1, keys, nb * TWO), lambda p, *_: (p + at, 0, 0)),
        pl.BlockSpec((1, nb * TWO, 2 * SPAN), lambda p, *_: (p + at, 0, 0)),
        columns(tokens, start), columns(tokens, start),
        columns(hrows, kc), columns(hrows, vc), columns(slots, base + start),
    ]
    alias = {}
    if carry:
        alias = {len(args) + i: i for i in range(len(carry))}
        args += carry
        specs += [ANY] * len(carry)
    return pl.pallas_call(
        functools.partial(backward_kernel, nb=nb),
        grid=(count,),
        in_specs=specs,
        out_specs=[
            columns(tokens, start), columns(tokens, start), columns(tokens, start),
            columns(2 * hrows, dh_at),
        ],
        scratch_shapes=[
            pltpu.VMEM((keys, SPAN), bf16), pltpu.VMEM((keys - slots, 2 * SPAN), bf16),
            pltpu.VMEM((nb * TWO, SPAN), bf16), pltpu.VMEM((keys - slots, nb * TWO), bf16),
        ],
        out_shape=[
            jax.ShapeDtypeStruct((tokens, width), bf16),
            jax.ShapeDtypeStruct((tokens, width), bf16),
            jax.ShapeDtypeStruct((tokens, width), bf16),
            jax.ShapeDtypeStruct((2 * hrows, dh_total * SPAN), bf16),
        ],
        input_output_aliases=alias,
        compiler_params=pltpu.CompilerParams(vmem_limit_bytes=67_000_000),
        cost_estimate=pl.CostEstimate(
            flops=count * nb * 20 * TWO * BLK * 1024, bytes_accessed=count * (6 << 20), transcendentals=0
        ),
        name="band_backward",
    )(*args)


def finish_kernel(slot_ref, dk_in, dv_in, dm_ref, *rest, segments):
    backs, (dk_ref, dv_ref) = rest[:-2], rest[-2:]
    rows = dk_in.shape[0]
    mine = slot_ref.shape[1]
    at = lax.broadcasted_iota(jnp.int32, (rows, mine), 0) + pl.program_id(0) * rows
    pick = (at == slot_ref[...]).astype(f32).astype(bf16)
    for g, pair, pos, count in segments:
        to, of = slice(pair * SPAN, (pair + count) * SPAN), slice(pos * SPAN, (pos + count) * SPAN)
        back = backs[g]
        dk = dk_in[:, to].astype(f32) + dot(pick, dm_ref[:mine, to], NN)
        dv = dv_in[:, to].astype(f32) + dot(pick, dm_ref[mine:, to], NN)
        dk_ref[:, to] = (dk + back[0, :, of].astype(f32)).astype(bf16)
        dv_ref[:, to] = (dv + back[1, :, of].astype(f32)).astype(bf16)


def finish(slots, dko, dvo, dmem, backs, segments):
    tokens, width = dko.shape
    mine = slots.shape[0]
    step = 2 * BLK
    row = pl.BlockSpec((step, width), lambda r: (r, 0))
    return pl.pallas_call(
        functools.partial(finish_kernel, segments=segments),
        grid=(tokens // step,),
        in_specs=[pl.BlockSpec((1, mine), lambda r: (0, 0)), row, row, pl.BlockSpec((2 * mine, width), lambda r: (0, 0))]
        + [pl.BlockSpec((2, step, b.shape[-1]), lambda r: (0, r, 0)) for b in backs],
        out_specs=[row, row],
        out_shape=[jax.ShapeDtypeStruct((tokens, width), bf16)] * 2,
        compiler_params=pltpu.CompilerParams(vmem_limit_bytes=67_000_000),
        cost_estimate=pl.CostEstimate(flops=1 << 26, bytes_accessed=6 << 20, transcendentals=0),
        name="finish_rows",
    )(slots[None, :], dko, dvo, dmem, *backs)


def place_kernel(where_ref, *rest, plane, nfam, scale, flip):
    parts, (out_ref, buf, sems) = rest[:plane], rest[-3:]
    rows = parts[0].shape[0]
    piece = rows // nfam
    side, spot, fam = (where_ref[0] & 1) ^ flip, lax.div(where_ref[0], 2), where_ref[1]
    copies = []
    for i, part in enumerate(parts):
        at = pl.multiple_of((side * plane + (spot ^ i)) * rows, rows)
        for k in range(nfam):
            row = pl.multiple_of((fam ^ k) * piece, piece)
            buf[i, pl.ds(row, piece), :] = part[k * piece : (k + 1) * piece, :].astype(f32) * scale
        copies.append(pltpu.make_async_copy(buf.at[i], out_ref.at[pl.ds(at, rows), :], sems.at[i]))
        copies[-1].start()
    for copy in copies:
        copy.wait()


def place(where, parts, nfam, scale, flip, carry):
    rows, width = parts[0].shape
    n = len(parts)
    more = [] if carry is None else [carry]
    return pl.pallas_call(
        functools.partial(place_kernel, plane=n, nfam=nfam, scale=scale, flip=flip),
        in_specs=[pl.BlockSpec(memory_space=pltpu.SMEM)] + [pl.BlockSpec(memory_space=pltpu.VMEM)] * n + [ANY] * len(more),
        out_specs=ANY,
        out_shape=jax.ShapeDtypeStruct((2 * n * rows, width), f32),
        scratch_shapes=[pltpu.VMEM((n, rows, width), f32), pltpu.SemaphoreType.DMA((n,))],
        input_output_aliases={1 + n: 0} if more else {},
        compiler_params=pltpu.CompilerParams(vmem_limit_bytes=67_000_000),
        cost_estimate=pl.CostEstimate(flops=1 << 20, bytes_accessed=3 << 20, transcendentals=0),
        name="place_rows",
    )(where, *parts, *more)


def swap(x, axis, bits):
    return lax.ppermute(x, axis, [(i, i ^ bits) for i in range(lax.axis_size(axis))])


def bits_of(n):
    out, b = [], 1
    while b < n:
        out.append(b)
        b *= 2
    return out


def mirrored(n):
    order = [0]
    for bit in reversed(bits_of(n)):
        order = order + [i + bit for i in order]
    return order


def gather_rows(x, axis, me):
    for bit in reversed(bits_of(lax.axis_size(axis))):
        other = swap(x, axis, bit)
        upper = (me & bit) != 0
        x = jnp.where(upper, jnp.concatenate([other, x], 0), jnp.concatenate([x, other], 0))
    return x


def exchange(part, axis, shift, me, n):
    return [part(me)] + [swap(part(me ^ k).astype(bf16), axis, k << shift) for k in range(1, n)]


def spread(x, axis, shift, n):
    return [x] + [swap(x, axis, k << shift) for k in range(1, n)]


def total_of(parts):
    return sum([x.astype(f32) for x in parts[1:]], parts[0].astype(f32))


def groups_of(pairs):
    if pairs % 8:
        return [pairs], [(0, 0, pairs)], [pairs]
    u = pairs // 8
    return [3 * u, 5 * u], [(0, 0, u), (1, 0, 5 * u), (0, u, 2 * u)], [6 * u, 2 * u]


def per_device(queries, key_rows, value_rows, cotangent, out_weight, prot_blocks, last_fill, memory_slots):
    q, k, v, cot = queries[0], key_rows[0], value_rows[0], cotangent[0]
    slots = memory_slots[0]
    tokens, width = q.shape
    nctx, nfam = lax.axis_size("ctx"), lax.axis_size("fam")
    me, fam = lax.axis_index("ctx"), lax.axis_index("fam")
    total = slots.shape[0]
    mine = total // nctx
    pairs = width // SPAN
    fsizes, bplan, dhs = groups_of(pairs)
    fstarts = [sum(fsizes[:i]) for i in range(len(fsizes))]
    shift = [(i, i + 1) for i in range(nctx - 1)]
    back = [(i + 1, i) for i in range(nctx - 1)]
    where = jnp.stack([me]).astype(jnp.int32)
    rows = memory_rows(where, memory_slots, k, v, mine)
    halos = halo_groups(k, v, [n * SPAN for n in fsizes])
    mem = gather_rows(rows, "ctx", me)
    halos = [lax.ppermute(x, "ctx", shift) for x in halos]
    grad_attn = dot(cot, out_weight, NT).astype(bf16)
    order = mirrored(nctx)
    carry, saved = [], []
    for i, (at, count) in enumerate(zip(fstarts, fsizes)):
        send, kept, pt, ga = forward(
            where, prot_blocks, last_fill, memory_slots, q, cot, grad_attn, k, v, halos[i], mem, order,
            at, count, carry)
        carry = [send, kept]
        saved.append((pt, ga))
    spot, plane = me >> 1, nctx // 2
    at = lambda x, j, axis: lax.dynamic_index_in_dim(x, j, axis, keepdims=False)
    sent = swap(send, "ctx", 1)
    carry, backs, segments, i = [], [], [], 0
    for total_dh in dhs:
        done = 0
        while done < total_dh:
            j, r, count = bplan[i]
            pt, ga = saved[j]
            out = backward(
                q, pt, ga, k, v, halos[j], halos[j], mem, fstarts[j] + r, count,
                0, (r, fsizes[j] + r), r, carry, total_dh, done)
            carry = list(out)
            segments.append((len(backs), fstarts[j] + r, done, count))
            done, i = done + count, i + 1
        backs.append(lax.ppermute(carry.pop(), "ctx", back))
    got = exchange(lambda j: at(sent, j, 0).astype(f32) + at(kept, j, 0).astype(f32), "ctx", 1, spot, plane)
    rows = width // nctx
    mem_grad = total_of([x[rows:] for x in got]).astype(bf16)
    piece = lambda j: total_of([lax.dynamic_slice_in_dim(x, j * (rows // nfam), rows // nfam) for x in got])
    w = total_of(exchange(piece, "fam", 0, fam, nfam)).astype(bf16)
    w = jnp.concatenate(spread(w, "fam", 0, nfam), 0)
    parts = spread(w, "ctx", 1, plane)
    others = [swap(x, "ctx", 1) for x in parts]
    scale = (nfam * nctx * tokens) ** -0.5
    where = jnp.stack([me, fam]).astype(jnp.int32)
    weight = place(where, parts, nfam, scale, 0, None)
    weight = place(where, others, nfam, scale, 1, weight)
    dq, dko, dvo = carry
    backs = [x.reshape(2, W, -1) for x in backs]
    dk, dv = finish(lax.dynamic_slice_in_dim(slots, me * mine, mine), dko, dvo, mem_grad, backs, segments)
    return dq[None], dk[None], dv[None], weight


def solution(mesh):
    row = P("fam", "ctx", None)
    small = P("fam", None)

    return jax.shard_map(
        per_device,
        mesh=mesh,
        in_specs=(row, row, row, row, P(), small, small, small),
        out_specs=(row, row, row, P()),
        check_vma=False,
    )
```

```python
import functools

import jax
import jax.numpy as jnp
from jax import lax
from jax.experimental import pallas as pl
from jax.experimental.pallas import tpu as pltpu
from jax.sharding import PartitionSpec as P


HEAD_DIM = 64
W = 512
BLK = 128
SPAN = 2 * HEAD_DIM
TWO = 2 * BLK
FAR = W // BLK
NEG = -1e30
NT = (((1,), (1,)), ((), ()))
NN = (((1,), (0,)), ((), ()))
TN = (((0,), (0,)), ((), ()))
f32 = jnp.float32
bf16 = jnp.bfloat16


def dot(a, b, dims):
    return lax.dot_general(a, b, dims, preferred_element_type=f32)


def by_head(x, first):
    zero = jnp.zeros_like(x)
    return jnp.concatenate([jnp.where(first, x, zero), jnp.where(first, zero, x)], 0)


def join_heads(x, first):
    return jnp.where(first, x[:BLK], x[BLK:])


def fill_keys(dst, halo, own, memory):
    h, o = halo.shape[0], own.shape[0]
    dst[0:h, :SPAN] = halo[...]
    dst[h : h + o, :SPAN] = own[...]
    dst[h + o :, :SPAN] = memory[...]


def tables(me, blocks_ref, fill_ref, slots_ref, info, bias, nb, tokens, order):
    nprot, slots = blocks_ref.shape[1], slots_ref.shape[1]
    mine = slots // len(order)
    begin = jnp.int32(0)
    first, left, pads = [0] * nb, [0] * nb, []
    for p in range(nprot):
        end = begin + blocks_ref[0, p]
        real = (end - 1) * BLK + fill_ref[0, p]
        pads.append((real, end * BLK))
        for b in range(nb):
            block = me * nb + b
            inside = (block >= begin) & (block < end)
            first[b] = jnp.where(inside, begin, first[b])
            left[b] = jnp.where(inside, real - block * BLK, left[b])
        begin = end
    for b in range(nb):
        info[0, b] = first[b] - (me * nb - FAR)
        info[1, b] = left[b]
    row = lax.broadcasted_iota(jnp.int32, (BLK, BLK), 0)
    for g in range(slots // BLK):
        lanes = jnp.broadcast_to(slots_ref[:, g * BLK : (g + 1) * BLK], (BLK, BLK))
        source = lanes.T + (row + g * BLK) // mine * tokens
        bad = jnp.zeros((BLK, BLK), f32)
        for lo, hi in pads:
            bad = jnp.where((source >= lo) & (source < hi), 1.0, bad)
        for b in range(nb):
            seen = jnp.where((source < first[b] * BLK) & (bad == 0.0), 0.0, NEG)
            for j in range(g * BLK // mine, (g + 1) * BLK // mine):
                i = order.index(j)
                bias[b, i * mine : (i + 1) * mine, :] = seen[j * mine - g * BLK : (j + 1) * mine - g * BLK]


def forward_kernel(
    me_ref, blocks_ref, fill_ref, q_ref, cot_ref, g_ref, ko_ref, vo_ref, kh_ref, vh_ref, km_ref, vm_ref, slots_ref,
    *rest, nb, order, start
):
    send_ref, keep_ref, pt, ga_ref, ke, ve, q2s, pm, mb_ref, at_ref, w_buf, dm_buf, sems, info_ref = rest[-14:]
    slots = km_ref.shape[0]
    mine = slots // len(order)
    ext = kh_ref.shape[0] + ko_ref.shape[0]

    @pl.when(pl.program_id(0) == 0)
    def _():
        tables(me_ref[0], blocks_ref, fill_ref, slots_ref, info_ref, mb_ref, nb, ko_ref.shape[0], order)

    fill_keys(ke, kh_ref, ko_ref, km_ref)
    fill_keys(ve, vh_ref, vo_ref, vm_ref)
    ve[:, SPAN:] = jnp.ones((ve.shape[0], SPAN), bf16)
    first = lax.broadcasted_iota(jnp.int32, (BLK, SPAN), 1) < HEAD_DIM
    tri = (
        lax.broadcasted_iota(jnp.int32, (BLK, TWO), 0)
        <= lax.broadcasted_iota(jnp.int32, (BLK, TWO), 1) % BLK
    )
    lane = lax.broadcasted_iota(jnp.int32, (TWO, SPAN), 1)
    row = lax.broadcasted_iota(jnp.int32, (TWO, SPAN), 0) % BLK
    unit = jnp.asarray(HEAD_DIM**-0.5, bf16)
    at = lambda b: (slice(b * BLK, (b + 1) * BLK), slice(b * TWO, (b + 1) * TWO), slice(b * BLK, (b + FAR + 1) * BLK))
    scores, outs = {}, {}

    def score(b):
        rows, cols, band = at(b)
        q2 = by_head(q_ref[rows, :] * unit, first)
        q2s[cols, :] = q2
        scores[b] = (dot(ke[band, :], q2, NT), dot(ke[ext:, :], q2, NT))

    def exponentials(b):
        _, cols, _ = at(b)
        s, sm = scores.pop(b)
        sm = sm + jnp.concatenate([mb_ref[b], mb_ref[b]], 1)
        off = [jnp.where(e + b >= info_ref[0, b], 0.0, NEG).astype(f32) for e in range(FAR)]
        ends = jnp.where(tri, s[FAR * BLK :, :], s[:BLK, :] + off[0])
        mid = [s[e * BLK : (e + 1) * BLK, :] for e in range(1, FAR)]
        m = jnp.maximum(jnp.max(ends, 0, keepdims=True), jnp.max(sm, 0, keepdims=True))
        for e in range(1, FAR):
            m = jnp.maximum(m, jnp.max(mid[e - 1], 0, keepdims=True) + off[e])
        for e in range(1, FAR):
            pt[0, (b + e) * BLK : (b + e + 1) * BLK, cols] = jnp.exp(
                mid[e - 1] - (m - off[e])
            ).astype(bf16)
        pm[:, cols] = jnp.exp(sm - m).astype(bf16)
        p = jnp.exp(ends - m).astype(bf16)
        zero = jnp.zeros_like(p)
        pt[0, b * BLK : (b + 1) * BLK, cols] = jnp.where(tri, zero, p)
        pt[0, (b + FAR) * BLK : (b + FAR + 1) * BLK, cols] = jnp.where(tri, p, zero)

    def attend(b):
        _, cols, band = at(b)
        outs[b] = dot(pt[0, band, cols], ve[band, :], TN) + dot(pm[:, cols], ve[ext:, :], TN)

    def gradients(b):
        rows, cols, _ = at(b)
        o = outs.pop(b)
        scale = jnp.where(row < info_ref[1, b], 1.0 / o[:, SPAN:], 0.0)
        o = o[:, :SPAN] * scale
        at_ref[rows, :] = join_heads(o, first).astype(bf16)
        g2 = (by_head(g_ref[rows, :].astype(f32), first) * scale).astype(bf16)
        d = -jnp.sum(g2.astype(f32) * o, 1, keepdims=True)
        high = d.astype(bf16).astype(f32)
        ga_ref[0, cols, :SPAN] = g2
        ga_ref[0, cols, SPAN:] = jnp.where(
            lane == 0, high, jnp.where(lane == 1, d - high, 0.0)
        ).astype(bf16)

    def memory(b):
        _, cols, _ = at(b)
        dp = dot(ve[ext:, :], ga_ref[0, cols, :], NT)
        pt[0, ext:, cols] = (pm[:, cols].astype(f32) * dp).astype(bf16)

    for t in range(nb + 4):
        for stage, lag in ((score, 0), (attend, 2), (exponentials, 1), (memory, 4), (gradients, 3)):
            if 0 <= t - lag < nb:
                stage(t - lag)
    step, plane, width = pl.program_id(0), len(order) // 2, cot_ref.shape[1]
    core, slot, rows = me_ref[0] & 1, lax.rem(step, 2), width // len(order)
    dk = dot(pt[0, ext:, :], q2s[...], NN).astype(bf16)
    dv = dot(pm[...], ga_ref[0, :, :SPAN], NN).astype(bf16)
    for i, j in enumerate(order):
        part = slice(i * mine, (i + 1) * mine)
        dm_buf[slot, j % 2, j // 2, :mine, :] = dk[part]
        dm_buf[slot, j % 2, j // 2, mine:, :] = dv[part]
    w_buf[slot] = dot(at_ref[...], cot_ref[...], TN).astype(bf16)

    def copies(at, slot):
        pair = start + at
        out = []
        for t in range(max(1, SPAN // rows)):
            block = pair * (SPAN // rows) + t
            out.append((block // plane == core, lambda ref, t=t, block=block: pltpu.make_async_copy(
                w_buf.at[slot, pl.ds(t * rows, rows), :], ref.at[lax.rem(block, plane), pl.ds(0, rows), :],
                sems.at[slot, 2 + t])))
        for side in range(2):
            out.append((core == side, lambda ref, side=side: pltpu.make_async_copy(
                dm_buf.at[slot, side],
                ref.at[:, pl.ds(rows, 2 * mine), pl.ds(pl.multiple_of(pair * SPAN, SPAN), SPAN)],
                sems.at[slot, side])))
        return out

    for stays, copy in copies(step, slot):

        @pl.when(stays)
        def _():
            copy(keep_ref).start()

        @pl.when(jnp.logical_not(stays))
        def _():
            copy(send_ref).start()

    @pl.when(step > 0)
    def _():
        for _, copy in copies(step - 1, 1 - slot):
            copy(keep_ref).wait()

    @pl.when(step == pl.num_programs(0) - 1)
    def _():
        for _, copy in copies(step, slot):
            copy(keep_ref).wait()


def backward_kernel(
    q_ref, pt_ref, ga_ref, ko_ref, vo_ref, kh_ref, vh_ref, km_ref, *rest, nb
):
    dq_ref, dko_ref, dvo_ref, dh_ref, ke, ve, q2, ds = rest[-8:]
    hrows = kh_ref.shape[0]
    ext = hrows + ko_ref.shape[0]
    fill_keys(ke, kh_ref, ko_ref, km_ref)
    ve[0:hrows, :SPAN] = vh_ref[...]
    ve[hrows:, :SPAN] = vo_ref[...]
    ve[:, SPAN:] = jnp.ones((ve.shape[0], SPAN), bf16)
    first = lax.broadcasted_iota(jnp.int32, (BLK, SPAN), 1) < HEAD_DIM
    unit = HEAD_DIM**-0.5
    for b in range(nb):
        rows, cols = slice(b * BLK, (b + 1) * BLK), slice(b * TWO, (b + 1) * TWO)
        band = slice(b * BLK, (b + FAR + 1) * BLK)
        q2[cols, :] = by_head(q_ref[rows, :] * jnp.asarray(unit, bf16), first)
        ga = ga_ref[0, cols, :]
        dp = dot(ve[band, :], ga, NT)
        ds[band, cols] = (pt_ref[0, band, cols].astype(f32) * dp).astype(bf16)
        dq = dot(ds[band, cols], ke[band, :], TN) + dot(pt_ref[0, ext:, cols], ke[ext:, :], TN)
        dq_ref[rows, :] = (join_heads(dq, first) * unit).astype(bf16)
    for e in range(ext // BLK):
        cols = slice(max(0, e - FAR) * TWO, (min(nb - 1, e) + 1) * TWO)
        rows = slice(e * BLK, (e + 1) * BLK)
        dv = dot(pt_ref[0, rows, cols], ga_ref[0, cols, :SPAN], NN)
        dk = dot(ds[rows, cols], q2[cols, :], NN)
        if e * BLK < hrows:
            dh_ref[rows, :] = dk.astype(bf16)
            dh_ref[hrows + e * BLK : hrows + (e + 1) * BLK, :] = dv.astype(bf16)
        else:
            own = slice(e * BLK - hrows, (e + 1) * BLK - hrows)
            dko_ref[own, :] = dk.astype(bf16)
            dvo_ref[own, :] = dv.astype(bf16)


def columns(rows, start):
    return pl.BlockSpec((rows, SPAN), lambda p, *_: (0, p + start))


ANY = pl.BlockSpec(memory_space=pl.ANY)


def forward(me, blocks, fill, slot_row, q, cot, g, ko, vo, halo, mem, order, start, count, carry):
    tokens, width = q.shape
    slots, hrows, nb, pairs = mem.shape[0], halo.shape[0], tokens // BLK, width // SPAN
    keys = hrows + tokens + slots
    smem = pl.BlockSpec(memory_space=pltpu.SMEM)
    members, plane = len(order), len(order) // 2
    rows, extra = width // members, 2 * slots // members
    out = jax.ShapeDtypeStruct((plane, rows + extra, width), bf16)
    args = [me, blocks, fill, q, cot, g, ko, vo, halo, halo, mem, mem, slot_row]
    specs = [
        smem, smem, smem, columns(tokens, start), pl.BlockSpec((tokens, width), lambda p: (0, 0)),
        columns(tokens, start), columns(tokens, start), columns(tokens, start),
        columns(hrows, 0), columns(hrows, count), columns(slots, start), columns(slots, pairs + start),
        pl.BlockSpec((1, slots), lambda p: (0, 0)),
    ]
    alias = {}
    if carry:
        alias = {len(args) + i: i for i in range(len(carry))}
        args += carry
        specs += [ANY] * len(carry)
    return pl.pallas_call(
        functools.partial(forward_kernel, nb=nb, order=order, start=start),
        grid=(count,),
        in_specs=specs,
        out_specs=[
            ANY, ANY,
            pl.BlockSpec((1, keys, nb * TWO), lambda p: (p, 0, 0)),
            pl.BlockSpec((1, nb * TWO, 2 * SPAN), lambda p: (p, 0, 0)),
        ],
        scratch_shapes=[
            pltpu.VMEM((keys, SPAN), bf16), pltpu.VMEM((keys, 2 * SPAN), bf16),
            pltpu.VMEM((nb * TWO, SPAN), bf16), pltpu.VMEM((slots, nb * TWO), bf16),
            pltpu.VMEM((nb, slots, BLK), f32),
            pltpu.VMEM((tokens, SPAN), bf16), pltpu.VMEM((2, SPAN, width), bf16),
            pltpu.VMEM((2, 2, plane, extra, SPAN), bf16), pltpu.SemaphoreType.DMA((2, 2 + SPAN // rows)),
            pltpu.SMEM((2, nb), jnp.int32),
        ],
        out_shape=[
            out, out,
            jax.ShapeDtypeStruct((count, keys, nb * TWO), bf16),
            jax.ShapeDtypeStruct((count, nb * TWO, 2 * SPAN), bf16),
        ],
        input_output_aliases=alias,
        compiler_params=pltpu.CompilerParams(vmem_limit_bytes=67_000_000),
        cost_estimate=pl.CostEstimate(
            flops=count * nb * 12 * TWO * BLK * 1024, bytes_accessed=count * (4 << 20), transcendentals=count << 20
        ),
        name="band_forward",
    )(*args)


def rows_kernel(me_ref, slots_ref, k_ref, v_ref, rows_ref):
    tokens, width = k_ref.shape
    mine = rows_ref.shape[0]
    row = lax.broadcasted_iota(jnp.int32, (mine, tokens), 0)
    slot = jnp.zeros((mine, tokens), jnp.int32)
    for r in range(mine):
        slot = jnp.where(row == r, slots_ref[0, me_ref[0] * mine + r], slot)
    pick = (slot == lax.broadcasted_iota(jnp.int32, (mine, tokens), 1)).astype(f32).astype(bf16)
    rows_ref[:, :width] = dot(pick, k_ref[...], NN).astype(bf16)
    rows_ref[:, width:] = dot(pick, v_ref[...], NN).astype(bf16)


def memory_rows(me, slots, k, v, mine):
    smem, vmem = pl.BlockSpec(memory_space=pltpu.SMEM), pl.BlockSpec(memory_space=pltpu.VMEM)
    return pl.pallas_call(
        rows_kernel,
        in_specs=[smem, smem, vmem, vmem],
        out_specs=vmem,
        out_shape=jax.ShapeDtypeStruct((mine, 2 * k.shape[1]), bf16),
        compiler_params=pltpu.CompilerParams(vmem_limit_bytes=67_000_000),
        name="memory_rows",
    )(me, slots, k, v)


def halo_kernel(k_ref, v_ref, *halos, sizes):
    edge, at = k_ref.shape[0] - W, 0
    for halo, size in zip(halos, sizes):
        halo[:, :size] = k_ref[edge:, at : at + size]
        halo[:, size:] = v_ref[edge:, at : at + size]
        at += size


def halo_groups(k, v, sizes):
    vmem = pl.BlockSpec(memory_space=pltpu.VMEM)
    return pl.pallas_call(
        functools.partial(halo_kernel, sizes=sizes),
        in_specs=[vmem, vmem],
        out_specs=[vmem] * len(sizes),
        out_shape=[jax.ShapeDtypeStruct((W, 2 * size), bf16) for size in sizes],
        compiler_params=pltpu.CompilerParams(vmem_limit_bytes=67_000_000),
        cost_estimate=pl.CostEstimate(flops=0, bytes_accessed=4 << 20, transcendentals=0),
        name="halo_groups",
    )(k, v)


def backward(q, pt, ga, ko, vo, kh, vh, km, start, count, base, halo_at, at, carry, dh_total, dh_at):
    tokens, width = q.shape
    slots, hrows, nb = km.shape[0], kh.shape[0], tokens // BLK
    keys = hrows + tokens + slots
    kc, vc = halo_at
    args = [q, pt, ga, ko, vo, kh, vh, km]
    specs = [
        columns(tokens, start),
        pl.BlockSpec((1, keys, nb * TWO), lambda p, *_: (p + at, 0, 0)),
        pl.BlockSpec((1, nb * TWO, 2 * SPAN), lambda p, *_: (p + at, 0, 0)),
        columns(tokens, start), columns(tokens, start),
        columns(hrows, kc), columns(hrows, vc), columns(slots, base + start),
    ]
    alias = {}
    if carry:
        alias = {len(args) + i: i for i in range(len(carry))}
        args += carry
        specs += [ANY] * len(carry)
    return pl.pallas_call(
        functools.partial(backward_kernel, nb=nb),
        grid=(count,),
        in_specs=specs,
        out_specs=[
            columns(tokens, start), columns(tokens, start), columns(tokens, start),
            columns(2 * hrows, dh_at),
        ],
        scratch_shapes=[
            pltpu.VMEM((keys, SPAN), bf16), pltpu.VMEM((keys - slots, 2 * SPAN), bf16),
            pltpu.VMEM((nb * TWO, SPAN), bf16), pltpu.VMEM((keys - slots, nb * TWO), bf16),
        ],
        out_shape=[
            jax.ShapeDtypeStruct((tokens, width), bf16),
            jax.ShapeDtypeStruct((tokens, width), bf16),
            jax.ShapeDtypeStruct((tokens, width), bf16),
            jax.ShapeDtypeStruct((2 * hrows, dh_total * SPAN), bf16),
        ],
        input_output_aliases=alias,
        compiler_params=pltpu.CompilerParams(vmem_limit_bytes=67_000_000),
        cost_estimate=pl.CostEstimate(
            flops=count * nb * 20 * TWO * BLK * 1024, bytes_accessed=count * (6 << 20), transcendentals=0
        ),
        name="band_backward",
    )(*args)


def finish_kernel(slot_ref, dk_in, dv_in, dm_ref, *rest, segments):
    backs, (dk_ref, dv_ref) = rest[:-2], rest[-2:]
    rows = dk_in.shape[0]
    mine = slot_ref.shape[1]
    at = lax.broadcasted_iota(jnp.int32, (rows, mine), 0) + pl.program_id(0) * rows
    pick = (at == slot_ref[...]).astype(f32).astype(bf16)
    for g, pair, pos, count in segments:
        to, of = slice(pair * SPAN, (pair + count) * SPAN), slice(pos * SPAN, (pos + count) * SPAN)
        back = backs[g]
        dk = dk_in[:, to].astype(f32) + dot(pick, dm_ref[:mine, to], NN)
        dv = dv_in[:, to].astype(f32) + dot(pick, dm_ref[mine:, to], NN)
        dk_ref[:, to] = (dk + back[0, :, of].astype(f32)).astype(bf16)
        dv_ref[:, to] = (dv + back[1, :, of].astype(f32)).astype(bf16)


def finish(slots, dko, dvo, dmem, backs, segments):
    tokens, width = dko.shape
    mine = slots.shape[0]
    step = 2 * BLK
    row = pl.BlockSpec((step, width), lambda r: (r, 0))
    return pl.pallas_call(
        functools.partial(finish_kernel, segments=segments),
        grid=(tokens // step,),
        in_specs=[pl.BlockSpec((1, mine), lambda r: (0, 0)), row, row, pl.BlockSpec((2 * mine, width), lambda r: (0, 0))]
        + [pl.BlockSpec((2, step, b.shape[-1]), lambda r: (0, r, 0)) for b in backs],
        out_specs=[row, row],
        out_shape=[jax.ShapeDtypeStruct((tokens, width), bf16)] * 2,
        compiler_params=pltpu.CompilerParams(vmem_limit_bytes=67_000_000),
        cost_estimate=pl.CostEstimate(flops=1 << 26, bytes_accessed=6 << 20, transcendentals=0),
        name="finish_rows",
    )(slots[None, :], dko, dvo, dmem, *backs)


def finish_rest_kernel(slot_ref, dk_in, dv_in, mk_ref, mv_ref, back_ref, dk_old, dv_old, dk_ref, dv_ref):
    tokens, mine = dk_in.shape[0], slot_ref.shape[1]
    pick = (lax.broadcasted_iota(jnp.int32, (tokens, mine), 0) == slot_ref[...]).astype(f32).astype(bf16)
    dk = dk_in[...].astype(f32) + dot(pick, mk_ref[...], NN)
    dv = dv_in[...].astype(f32) + dot(pick, mv_ref[...], NN)
    dk_ref[...] = (dk + back_ref[0].astype(f32)).astype(bf16)
    dv_ref[...] = (dv + back_ref[1].astype(f32)).astype(bf16)


def finish_rest(slots, dko, dvo, dmem, back, pair, count, carry):
    tokens, width = dko.shape
    mine = slots.shape[0]
    col = lambda rows, j: pl.BlockSpec((rows, SPAN), lambda p: (j, p + pair))
    return pl.pallas_call(
        finish_rest_kernel,
        grid=(count,),
        in_specs=[
            pl.BlockSpec((1, mine), lambda p: (0, 0)), col(tokens, 0), col(tokens, 0), col(mine, 0), col(mine, 1),
            pl.BlockSpec((2, tokens, SPAN), lambda p: (0, 0, p)), ANY, ANY,
        ],
        out_specs=[col(tokens, 0), col(tokens, 0)],
        out_shape=[jax.ShapeDtypeStruct((tokens, width), bf16)] * 2,
        input_output_aliases={6: 0, 7: 1},
        compiler_params=pltpu.CompilerParams(vmem_limit_bytes=67_000_000),
        cost_estimate=pl.CostEstimate(flops=1 << 24, bytes_accessed=2 << 20, transcendentals=0),
        name="finish_rest",
    )(slots[None, :], dko, dvo, dmem, dmem, back, *carry)


def place_kernel(me_ref, fam_ref, *rest, spots, plane, nfam, scale):
    n = len(spots)
    parts, (out_ref, buf, sems) = rest[:n], rest[-3:]
    rows = parts[0].shape[0]
    piece = rows // nfam
    core, spot, fam = me_ref[0] & 1, lax.div(me_ref[0], 2), fam_ref[0]
    copies = []
    for i, (part, (flip, other)) in enumerate(zip(parts, spots)):
        at = pl.multiple_of(((core ^ flip) * plane + (spot ^ other)) * rows, rows)
        for k in range(nfam):
            row = pl.multiple_of((fam ^ k) * piece, piece)
            buf[i, pl.ds(row, piece), :] = part[k * piece : (k + 1) * piece, :].astype(f32) * scale
        copies.append(pltpu.make_async_copy(buf.at[i], out_ref.at[pl.ds(at, rows), :], sems.at[i]))
        copies[-1].start()
    for copy in copies:
        copy.wait()


def place(me, fam, parts, spots, plane, nfam, scale, carry):
    rows, width = parts[0].shape
    n = len(parts)
    more = [] if carry is None else [carry]
    smem, vmem = pl.BlockSpec(memory_space=pltpu.SMEM), pl.BlockSpec(memory_space=pltpu.VMEM)
    return pl.pallas_call(
        functools.partial(place_kernel, spots=spots, plane=plane, nfam=nfam, scale=scale),
        in_specs=[smem, smem] + [vmem] * n + [ANY] * len(more),
        out_specs=ANY,
        out_shape=jax.ShapeDtypeStruct((2 * plane * rows, width), f32),
        scratch_shapes=[pltpu.VMEM((n, rows, width), f32), pltpu.SemaphoreType.DMA((n,))],
        input_output_aliases={2 + n: 0} if more else {},
        compiler_params=pltpu.CompilerParams(vmem_limit_bytes=67_000_000),
        cost_estimate=pl.CostEstimate(flops=1 << 20, bytes_accessed=3 << 20, transcendentals=0),
        name="place_rows",
    )(me, fam, *parts, *more)


def swap(x, axis, bits):
    return lax.ppermute(x, axis, [(i, i ^ bits) for i in range(lax.axis_size(axis))])


def bits_of(n):
    out, b = [], 1
    while b < n:
        out.append(b)
        b *= 2
    return out


def mirrored(n):
    order = [0]
    for bit in reversed(bits_of(n)):
        order = order + [i + bit for i in order]
    return order


def gather_rows(x, axis, me):
    for bit in reversed(bits_of(lax.axis_size(axis))):
        other = swap(x, axis, bit)
        upper = (me & bit) != 0
        x = jnp.where(upper, jnp.concatenate([other, x], 0), jnp.concatenate([x, other], 0))
    return x


def exchange(part, axis, shift, me, n):
    return [part(me)] + [swap(part(me ^ k).astype(bf16), axis, k << shift) for k in range(1, n)]


def spread(x, axis, shift, n):
    return [x] + [swap(x, axis, k << shift) for k in range(1, n)]


def total_of(parts):
    return sum([x.astype(f32) for x in parts[1:]], parts[0].astype(f32))


def groups_of(pairs):
    if pairs % 8:
        return [pairs], [(0, 0, pairs)], [pairs]
    u = pairs // 8
    return [3 * u, 5 * u], [(0, 0, u), (1, 0, 5 * u), (0, u, u), (0, 2 * u, u)], [7 * u, u]


def per_device(queries, key_rows, value_rows, cotangent, out_weight, prot_blocks, last_fill, memory_slots):
    q, k, v, cot = queries[0], key_rows[0], value_rows[0], cotangent[0]
    slots = memory_slots[0]
    tokens, width = q.shape
    nctx, nfam = lax.axis_size("ctx"), lax.axis_size("fam")
    me, fam = lax.axis_index("ctx"), lax.axis_index("fam")
    total = slots.shape[0]
    mine = total // nctx
    pairs = width // SPAN
    fsizes, bplan, dhs = groups_of(pairs)
    fstarts = [sum(fsizes[:i]) for i in range(len(fsizes))]
    shift = [(i, i + 1) for i in range(nctx - 1)]
    back = [(i + 1, i) for i in range(nctx - 1)]
    where = jnp.stack([me]).astype(jnp.int32)
    rows = memory_rows(where, memory_slots, k, v, mine)
    halos = halo_groups(k, v, [n * SPAN for n in fsizes])
    mem = gather_rows(rows, "ctx", me)
    halos = [lax.ppermute(x, "ctx", shift) for x in halos]
    grad_attn = dot(cot, out_weight, NT).astype(bf16)
    order = mirrored(nctx)
    carry, saved = [], []
    for i, (at, count) in enumerate(zip(fstarts, fsizes)):
        send, kept, pt, ga = forward(
            where, prot_blocks, last_fill, memory_slots, q, cot, grad_attn, k, v, halos[i], mem, order,
            at, count, carry)
        carry = [send, kept]
        saved.append((pt, ga))
    spot, plane = me >> 1, nctx // 2
    at = lambda x, j, axis: lax.dynamic_index_in_dim(x, j, axis, keepdims=False)
    sent = swap(send, "ctx", 1)
    carry, backs, segments, i = [], [], [], 0
    for total_dh in dhs:
        done = 0
        while done < total_dh:
            j, r, count = bplan[i]
            pt, ga = saved[j]
            out = backward(
                q, pt, ga, k, v, halos[j], halos[j], mem, fstarts[j] + r, count,
                0, (r, fsizes[j] + r), r, carry, total_dh, done)
            carry = list(out)
            segments.append((len(backs), fstarts[j] + r, done, count))
            done, i = done + count, i + 1
        backs.append(lax.ppermute(carry.pop(), "ctx", back))
    got = exchange(lambda j: at(sent, j, 0).astype(f32) + at(kept, j, 0).astype(f32), "ctx", 1, spot, plane)
    rows = width // nctx
    mem_grad = total_of([x[rows:] for x in got]).astype(bf16)
    piece = lambda j: total_of([lax.dynamic_slice_in_dim(x, j * (rows // nfam), rows // nfam) for x in got])
    w = total_of(exchange(piece, "fam", 0, fam, nfam)).astype(bf16)
    w = jnp.concatenate(spread(w, "fam", 0, nfam), 0)
    parts = spread(w, "ctx", 1, plane)
    others = [swap(x, "ctx", 1) for x in parts]
    scale = (nfam * nctx * tokens) ** -0.5
    who = jnp.stack([fam]).astype(jnp.int32)
    weight = place(where, who, [parts[0], others[0]], [(0, 0), (1, 0)], plane, nfam, scale, None)
    spots = [(flip, k) for flip in range(2) for k in range(1, plane)]
    weight = place(where, who, parts[1:] + others[1:], spots, plane, nfam, scale, weight)
    dq, dko, dvo = carry
    backs = [x.reshape(2, W, -1) for x in backs]
    own_slots = lax.dynamic_slice_in_dim(slots, me * mine, mine)
    grads = finish(own_slots, dko, dvo, mem_grad, backs[:1], [x for x in segments if x[0] == 0])
    for i, x in enumerate(backs[1:], 1):
        _, pair, _, count = [x for x in segments if x[0] == i][0]
        grads = finish_rest(own_slots, dko, dvo, mem_grad, x, pair, count, grads)
    dk, dv = grads
    return dq[None], dk[None], dv[None], weight


def solution(mesh):
    row = P("fam", "ctx", None)
    small = P("fam", None)

    return jax.shard_map(
        per_device,
        mesh=mesh,
        in_specs=(row, row, row, row, P(), small, small, small),
        out_specs=(row, row, row, P()),
        check_vma=False,
    )
```

```python
import functools

import jax
import jax.numpy as jnp
from jax import lax
from jax.experimental import pallas as pl
from jax.experimental.pallas import tpu as pltpu
from jax.sharding import PartitionSpec as P


HEAD_DIM = 64
W = 512
BLK = 128
SPAN = 2 * HEAD_DIM
TWO = 2 * BLK
FAR = W // BLK
NEG = -1e30
NT = (((1,), (1,)), ((), ()))
NN = (((1,), (0,)), ((), ()))
TN = (((0,), (0,)), ((), ()))
f32 = jnp.float32
bf16 = jnp.bfloat16


def dot(a, b, dims):
    return lax.dot_general(a, b, dims, preferred_element_type=f32)


def by_head(x, first):
    zero = jnp.zeros_like(x)
    return jnp.concatenate([jnp.where(first, x, zero), jnp.where(first, zero, x)], 0)


def join_heads(x, first):
    return jnp.where(first, x[:BLK], x[BLK:])


def fill_keys(dst, halo, own, memory):
    h, o = halo.shape[0], own.shape[0]
    dst[0:h, :SPAN] = halo[...]
    dst[h : h + o, :SPAN] = own[...]
    dst[h + o :, :SPAN] = memory[...]


def tables(me, blocks_ref, fill_ref, slots_ref, info, bias, nb, tokens, order):
    nprot, slots = blocks_ref.shape[1], slots_ref.shape[1]
    mine = slots // len(order)
    begin = jnp.int32(0)
    first, left, pads = [0] * nb, [0] * nb, []
    for p in range(nprot):
        end = begin + blocks_ref[0, p]
        real = (end - 1) * BLK + fill_ref[0, p]
        pads.append((real, end * BLK))
        for b in range(nb):
            block = me * nb + b
            inside = (block >= begin) & (block < end)
            first[b] = jnp.where(inside, begin, first[b])
            left[b] = jnp.where(inside, real - block * BLK, left[b])
        begin = end
    for b in range(nb):
        info[0, b] = first[b] - (me * nb - FAR)
        info[1, b] = left[b]
    row = lax.broadcasted_iota(jnp.int32, (BLK, BLK), 0)
    for g in range(slots // BLK):
        lanes = jnp.broadcast_to(slots_ref[:, g * BLK : (g + 1) * BLK], (BLK, BLK))
        source = lanes.T + (row + g * BLK) // mine * tokens
        bad = jnp.zeros((BLK, BLK), f32)
        for lo, hi in pads:
            bad = jnp.where((source >= lo) & (source < hi), 1.0, bad)
        for b in range(nb):
            seen = jnp.where((source < first[b] * BLK) & (bad == 0.0), 0.0, NEG)
            for j in range(g * BLK // mine, (g + 1) * BLK // mine):
                i = order.index(j)
                bias[b, i * mine : (i + 1) * mine, :] = seen[j * mine - g * BLK : (j + 1) * mine - g * BLK]


def forward_kernel(
    me_ref, blocks_ref, fill_ref, q_ref, cot_ref, g_ref, ko_ref, vo_ref, kh_ref, vh_ref, km_ref, vm_ref, slots_ref,
    *rest, nb, order, start
):
    send_ref, keep_ref, pt, ga_ref, ke, ve, q2s, pm, mb_ref, at_ref, w_buf, dm_buf, sems, info_ref = rest[-14:]
    slots = km_ref.shape[0]
    mine = slots // len(order)
    ext = kh_ref.shape[0] + ko_ref.shape[0]

    @pl.when(pl.program_id(0) == 0)
    def _():
        tables(me_ref[0], blocks_ref, fill_ref, slots_ref, info_ref, mb_ref, nb, ko_ref.shape[0], order)

    fill_keys(ke, kh_ref, ko_ref, km_ref)
    fill_keys(ve, vh_ref, vo_ref, vm_ref)
    ve[:, SPAN:] = jnp.ones((ve.shape[0], SPAN), bf16)
    first = lax.broadcasted_iota(jnp.int32, (BLK, SPAN), 1) < HEAD_DIM
    tri = (
        lax.broadcasted_iota(jnp.int32, (BLK, TWO), 0)
        <= lax.broadcasted_iota(jnp.int32, (BLK, TWO), 1) % BLK
    )
    lane = lax.broadcasted_iota(jnp.int32, (TWO, SPAN), 1)
    row = lax.broadcasted_iota(jnp.int32, (TWO, SPAN), 0) % BLK
    unit = jnp.asarray(HEAD_DIM**-0.5, bf16)
    at = lambda b: (slice(b * BLK, (b + 1) * BLK), slice(b * TWO, (b + 1) * TWO), slice(b * BLK, (b + FAR + 1) * BLK))
    scores, outs = {}, {}

    def score(b):
        rows, cols, band = at(b)
        q2 = by_head(q_ref[rows, :] * unit, first)
        q2s[cols, :] = q2
        scores[b] = (dot(ke[band, :], q2, NT), dot(ke[ext:, :], q2, NT))

    def exponentials(b):
        _, cols, _ = at(b)
        s, sm = scores.pop(b)
        sm = sm + jnp.concatenate([mb_ref[b], mb_ref[b]], 1)
        off = [jnp.where(e + b >= info_ref[0, b], 0.0, NEG).astype(f32) for e in range(FAR)]
        ends = jnp.where(tri, s[FAR * BLK :, :], s[:BLK, :] + off[0])
        mid = [s[e * BLK : (e + 1) * BLK, :] for e in range(1, FAR)]
        m = jnp.maximum(jnp.max(ends, 0, keepdims=True), jnp.max(sm, 0, keepdims=True))
        for e in range(1, FAR):
            m = jnp.maximum(m, jnp.max(mid[e - 1], 0, keepdims=True) + off[e])
        for e in range(1, FAR):
            pt[0, (b + e) * BLK : (b + e + 1) * BLK, cols] = jnp.exp(
                mid[e - 1] - (m - off[e])
            ).astype(bf16)
        pm[:, cols] = jnp.exp(sm - m).astype(bf16)
        p = jnp.exp(ends - m).astype(bf16)
        zero = jnp.zeros_like(p)
        pt[0, b * BLK : (b + 1) * BLK, cols] = jnp.where(tri, zero, p)
        pt[0, (b + FAR) * BLK : (b + FAR + 1) * BLK, cols] = jnp.where(tri, p, zero)

    def attend(b):
        _, cols, band = at(b)
        outs[b] = dot(pt[0, band, cols], ve[band, :], TN) + dot(pm[:, cols], ve[ext:, :], TN)

    def gradients(b):
        rows, cols, _ = at(b)
        o = outs.pop(b)
        scale = jnp.where(row < info_ref[1, b], 1.0 / o[:, SPAN:], 0.0)
        o = o[:, :SPAN] * scale
        at_ref[rows, :] = join_heads(o, first).astype(bf16)
        g2 = (by_head(g_ref[rows, :].astype(f32), first) * scale).astype(bf16)
        d = -jnp.sum(g2.astype(f32) * o, 1, keepdims=True)
        high = d.astype(bf16).astype(f32)
        ga_ref[0, cols, :SPAN] = g2
        ga_ref[0, cols, SPAN:] = jnp.where(
            lane == 0, high, jnp.where(lane == 1, d - high, 0.0)
        ).astype(bf16)

    def memory(b):
        _, cols, _ = at(b)
        dp = dot(ve[ext:, :], ga_ref[0, cols, :], NT)
        pt[0, ext:, cols] = (pm[:, cols].astype(f32) * dp).astype(bf16)

    for t in range(nb + 4):
        for stage, lag in ((score, 0), (attend, 2), (exponentials, 1), (memory, 4), (gradients, 3)):
            if 0 <= t - lag < nb:
                stage(t - lag)
    step, plane, width = pl.program_id(0), len(order) // 2, cot_ref.shape[1]
    core, slot, rows = me_ref[0] & 1, lax.rem(step, 2), width // len(order)
    dk = dot(pt[0, ext:, :], q2s[...], NN).astype(bf16)
    dv = dot(pm[...], ga_ref[0, :, :SPAN], NN).astype(bf16)
    for i, j in enumerate(order):
        part = slice(i * mine, (i + 1) * mine)
        dm_buf[slot, j % 2, j // 2, :mine, :] = dk[part]
        dm_buf[slot, j % 2, j // 2, mine:, :] = dv[part]
    w_buf[slot] = dot(at_ref[...], cot_ref[...], TN).astype(bf16)

    def copies(at, slot):
        pair = start + at
        out = []
        for t in range(max(1, SPAN // rows)):
            block = pair * (SPAN // rows) + t
            out.append((block // plane == core, lambda ref, t=t, block=block: pltpu.make_async_copy(
                w_buf.at[slot, pl.ds(t * rows, rows), :], ref.at[lax.rem(block, plane), pl.ds(0, rows), :],
                sems.at[slot, 2 + t])))
        for side in range(2):
            out.append((core == side, lambda ref, side=side: pltpu.make_async_copy(
                dm_buf.at[slot, side],
                ref.at[:, pl.ds(rows, 2 * mine), pl.ds(pl.multiple_of(pair * SPAN, SPAN), SPAN)],
                sems.at[slot, side])))
        return out

    for stays, copy in copies(step, slot):

        @pl.when(stays)
        def _():
            copy(keep_ref).start()

        @pl.when(jnp.logical_not(stays))
        def _():
            copy(send_ref).start()

    @pl.when(step > 0)
    def _():
        for _, copy in copies(step - 1, 1 - slot):
            copy(keep_ref).wait()

    @pl.when(step == pl.num_programs(0) - 1)
    def _():
        for _, copy in copies(step, slot):
            copy(keep_ref).wait()


def backward_kernel(
    q_ref, pt_ref, ga_ref, ko_ref, vo_ref, kh_ref, vh_ref, km_ref, *rest, nb
):
    dq_ref, dko_ref, dvo_ref, dh_ref, ke, ve, q2, ds = rest[-8:]
    hrows = kh_ref.shape[0]
    ext = hrows + ko_ref.shape[0]
    fill_keys(ke, kh_ref, ko_ref, km_ref)
    ve[0:hrows, :SPAN] = vh_ref[...]
    ve[hrows:, :SPAN] = vo_ref[...]
    ve[:, SPAN:] = jnp.ones((ve.shape[0], SPAN), bf16)
    first = lax.broadcasted_iota(jnp.int32, (BLK, SPAN), 1) < HEAD_DIM
    unit = HEAD_DIM**-0.5
    for b in range(nb):
        rows, cols = slice(b * BLK, (b + 1) * BLK), slice(b * TWO, (b + 1) * TWO)
        band = slice(b * BLK, (b + FAR + 1) * BLK)
        q2[cols, :] = by_head(q_ref[rows, :] * jnp.asarray(unit, bf16), first)
        ga = ga_ref[0, cols, :]
        dp = dot(ve[band, :], ga, NT)
        ds[band, cols] = (pt_ref[0, band, cols].astype(f32) * dp).astype(bf16)
        dq = dot(ds[band, cols], ke[band, :], TN) + dot(pt_ref[0, ext:, cols], ke[ext:, :], TN)
        dq_ref[rows, :] = (join_heads(dq, first) * unit).astype(bf16)
    for e in range(ext // BLK):
        cols = slice(max(0, e - FAR) * TWO, (min(nb - 1, e) + 1) * TWO)
        rows = slice(e * BLK, (e + 1) * BLK)
        dv = dot(pt_ref[0, rows, cols], ga_ref[0, cols, :SPAN], NN)
        dk = dot(ds[rows, cols], q2[cols, :], NN)
        if e * BLK < hrows:
            dh_ref[rows, :] = dk.astype(bf16)
            dh_ref[hrows + e * BLK : hrows + (e + 1) * BLK, :] = dv.astype(bf16)
        else:
            own = slice(e * BLK - hrows, (e + 1) * BLK - hrows)
            dko_ref[own, :] = dk.astype(bf16)
            dvo_ref[own, :] = dv.astype(bf16)


def columns(rows, start):
    return pl.BlockSpec((rows, SPAN), lambda p, *_: (0, p + start))


ANY = pl.BlockSpec(memory_space=pl.ANY)


def forward(me, blocks, fill, slot_row, q, cot, g, ko, vo, halo, mem, order, start, count, carry):
    tokens, width = q.shape
    slots, hrows, nb, pairs = mem.shape[0], halo.shape[0], tokens // BLK, width // SPAN
    keys = hrows + tokens + slots
    smem = pl.BlockSpec(memory_space=pltpu.SMEM)
    members, plane = len(order), len(order) // 2
    rows, extra = width // members, 2 * slots // members
    out = jax.ShapeDtypeStruct((plane, rows + extra, width), bf16)
    args = [me, blocks, fill, q, cot, g, ko, vo, halo, halo, mem, mem, slot_row]
    specs = [
        smem, smem, smem, columns(tokens, start), pl.BlockSpec((tokens, width), lambda p: (0, 0)),
        columns(tokens, start), columns(tokens, start), columns(tokens, start),
        columns(hrows, 0), columns(hrows, count), columns(slots, start), columns(slots, pairs + start),
        pl.BlockSpec((1, slots), lambda p: (0, 0)),
    ]
    alias = {}
    if carry:
        alias = {len(args) + i: i for i in range(len(carry))}
        args += carry
        specs += [ANY] * len(carry)
    return pl.pallas_call(
        functools.partial(forward_kernel, nb=nb, order=order, start=start),
        grid=(count,),
        in_specs=specs,
        out_specs=[
            ANY, ANY,
            pl.BlockSpec((1, keys, nb * TWO), lambda p: (p, 0, 0)),
            pl.BlockSpec((1, nb * TWO, 2 * SPAN), lambda p: (p, 0, 0)),
        ],
        scratch_shapes=[
            pltpu.VMEM((keys, SPAN), bf16), pltpu.VMEM((keys, 2 * SPAN), bf16),
            pltpu.VMEM((nb * TWO, SPAN), bf16), pltpu.VMEM((slots, nb * TWO), bf16),
            pltpu.VMEM((nb, slots, BLK), f32),
            pltpu.VMEM((tokens, SPAN), bf16), pltpu.VMEM((2, SPAN, width), bf16),
            pltpu.VMEM((2, 2, plane, extra, SPAN), bf16), pltpu.SemaphoreType.DMA((2, 2 + SPAN // rows)),
            pltpu.SMEM((2, nb), jnp.int32),
        ],
        out_shape=[
            out, out,
            jax.ShapeDtypeStruct((count, keys, nb * TWO), bf16),
            jax.ShapeDtypeStruct((count, nb * TWO, 2 * SPAN), bf16),
        ],
        input_output_aliases=alias,
        compiler_params=pltpu.CompilerParams(vmem_limit_bytes=67_000_000),
        cost_estimate=pl.CostEstimate(
            flops=count * nb * 12 * TWO * BLK * 1024, bytes_accessed=count * (4 << 20), transcendentals=count << 20
        ),
        name="band_forward",
    )(*args)


def rows_kernel(me_ref, slots_ref, k_ref, v_ref, rows_ref):
    tokens, width = k_ref.shape
    mine = rows_ref.shape[0]
    row = lax.broadcasted_iota(jnp.int32, (mine, tokens), 0)
    slot = jnp.zeros((mine, tokens), jnp.int32)
    for r in range(mine):
        slot = jnp.where(row == r, slots_ref[0, me_ref[0] * mine + r], slot)
    pick = (slot == lax.broadcasted_iota(jnp.int32, (mine, tokens), 1)).astype(f32).astype(bf16)
    rows_ref[:, :width] = dot(pick, k_ref[...], NN).astype(bf16)
    rows_ref[:, width:] = dot(pick, v_ref[...], NN).astype(bf16)


def memory_rows(me, slots, k, v, mine):
    smem, vmem = pl.BlockSpec(memory_space=pltpu.SMEM), pl.BlockSpec(memory_space=pltpu.VMEM)
    return pl.pallas_call(
        rows_kernel,
        in_specs=[smem, smem, vmem, vmem],
        out_specs=vmem,
        out_shape=jax.ShapeDtypeStruct((mine, 2 * k.shape[1]), bf16),
        compiler_params=pltpu.CompilerParams(vmem_limit_bytes=67_000_000),
        name="memory_rows",
    )(me, slots, k, v)


def halo_kernel(k_ref, v_ref, *halos, sizes):
    edge, at = k_ref.shape[0] - W, 0
    for halo, size in zip(halos, sizes):
        halo[:, :size] = k_ref[edge:, at : at + size]
        halo[:, size:] = v_ref[edge:, at : at + size]
        at += size


def halo_groups(k, v, sizes):
    vmem = pl.BlockSpec(memory_space=pltpu.VMEM)
    return pl.pallas_call(
        functools.partial(halo_kernel, sizes=sizes),
        in_specs=[vmem, vmem],
        out_specs=[vmem] * len(sizes),
        out_shape=[jax.ShapeDtypeStruct((W, 2 * size), bf16) for size in sizes],
        compiler_params=pltpu.CompilerParams(vmem_limit_bytes=67_000_000),
        cost_estimate=pl.CostEstimate(flops=0, bytes_accessed=4 << 20, transcendentals=0),
        name="halo_groups",
    )(k, v)


def backward(q, pt, ga, ko, vo, kh, vh, km, start, count, base, halo_at, at, carry, dh_total, dh_at):
    tokens, width = q.shape
    slots, hrows, nb = km.shape[0], kh.shape[0], tokens // BLK
    keys = hrows + tokens + slots
    kc, vc = halo_at
    args = [q, pt, ga, ko, vo, kh, vh, km]
    specs = [
        columns(tokens, start),
        pl.BlockSpec((1, keys, nb * TWO), lambda p, *_: (p + at, 0, 0)),
        pl.BlockSpec((1, nb * TWO, 2 * SPAN), lambda p, *_: (p + at, 0, 0)),
        columns(tokens, start), columns(tokens, start),
        columns(hrows, kc), columns(hrows, vc), columns(slots, base + start),
    ]
    alias = {}
    if carry:
        alias = {len(args) + i: i for i in range(len(carry))}
        args += carry
        specs += [ANY] * len(carry)
    return pl.pallas_call(
        functools.partial(backward_kernel, nb=nb),
        grid=(count,),
        in_specs=specs,
        out_specs=[
            columns(tokens, start), columns(tokens, start), columns(tokens, start),
            columns(2 * hrows, dh_at),
        ],
        scratch_shapes=[
            pltpu.VMEM((keys, SPAN), bf16), pltpu.VMEM((keys - slots, 2 * SPAN), bf16),
            pltpu.VMEM((nb * TWO, SPAN), bf16), pltpu.VMEM((keys - slots, nb * TWO), bf16),
        ],
        out_shape=[
            jax.ShapeDtypeStruct((tokens, width), bf16),
            jax.ShapeDtypeStruct((tokens, width), bf16),
            jax.ShapeDtypeStruct((tokens, width), bf16),
            jax.ShapeDtypeStruct((2 * hrows, dh_total * SPAN), bf16),
        ],
        input_output_aliases=alias,
        compiler_params=pltpu.CompilerParams(vmem_limit_bytes=67_000_000),
        cost_estimate=pl.CostEstimate(
            flops=count * nb * 20 * TWO * BLK * 1024, bytes_accessed=count * (6 << 20), transcendentals=0
        ),
        name="band_backward",
    )(*args)


def picks(me, slots_ref, base, rows, mine):
    column = lax.broadcasted_iota(jnp.int32, (rows, mine), 1)
    slot = jnp.zeros((rows, mine), jnp.int32)
    for r in range(mine):
        slot = jnp.where(column == r, slots_ref[0, me * mine + r], slot)
    at = lax.broadcasted_iota(jnp.int32, (rows, mine), 0) + base
    return (at == slot).astype(f32).astype(bf16)


def finish_kernel(me_ref, slots_ref, dk_in, dv_in, dm_ref, *rest, segments):
    backs, (dk_ref, dv_ref) = rest[:-2], rest[-2:]
    rows = dk_in.shape[0]
    mine = dm_ref.shape[0] // 2
    pick = picks(me_ref[0], slots_ref, pl.program_id(0) * rows, rows, mine)
    for g, pair, pos, count in segments:
        to, of = slice(pair * SPAN, (pair + count) * SPAN), slice(pos * SPAN, (pos + count) * SPAN)
        back = backs[g]
        dk = dk_in[:, to].astype(f32) + dot(pick, dm_ref[:mine, to], NN)
        dv = dv_in[:, to].astype(f32) + dot(pick, dm_ref[mine:, to], NN)
        dk_ref[:, to] = (dk + back[0, :, of].astype(f32)).astype(bf16)
        dv_ref[:, to] = (dv + back[1, :, of].astype(f32)).astype(bf16)


def finish(me, slots, dko, dvo, dmem, backs, segments):
    tokens, width = dko.shape
    mine = dmem.shape[0] // 2
    smem = pl.BlockSpec(memory_space=pltpu.SMEM)
    step = 2 * BLK
    row = pl.BlockSpec((step, width), lambda r: (r, 0))
    return pl.pallas_call(
        functools.partial(finish_kernel, segments=segments),
        grid=(tokens // step,),
        in_specs=[smem, smem, row, row, pl.BlockSpec((2 * mine, width), lambda r: (0, 0))]
        + [pl.BlockSpec((2, step, b.shape[-1]), lambda r: (0, r, 0)) for b in backs],
        out_specs=[row, row],
        out_shape=[jax.ShapeDtypeStruct((tokens, width), bf16)] * 2,
        compiler_params=pltpu.CompilerParams(vmem_limit_bytes=67_000_000),
        cost_estimate=pl.CostEstimate(flops=1 << 26, bytes_accessed=6 << 20, transcendentals=0),
        name="finish_rows",
    )(me, slots, dko, dvo, dmem, *backs)


def finish_rest_kernel(me_ref, slots_ref, dk_in, dv_in, mk_ref, mv_ref, back_ref, dk_old, dv_old, dk_ref, dv_ref):
    pick = picks(me_ref[0], slots_ref, 0, dk_in.shape[0], mk_ref.shape[0])
    dk = dk_in[...].astype(f32) + dot(pick, mk_ref[...], NN)
    dv = dv_in[...].astype(f32) + dot(pick, mv_ref[...], NN)
    dk_ref[...] = (dk + back_ref[0].astype(f32)).astype(bf16)
    dv_ref[...] = (dv + back_ref[1].astype(f32)).astype(bf16)


def finish_rest(me, slots, dko, dvo, dmem, back, pair, count, carry):
    tokens, width = dko.shape
    mine = dmem.shape[0] // 2
    smem = pl.BlockSpec(memory_space=pltpu.SMEM)
    col = lambda rows, j: pl.BlockSpec((rows, SPAN), lambda p: (j, p + pair))
    return pl.pallas_call(
        finish_rest_kernel,
        grid=(count,),
        in_specs=[
            smem, smem, col(tokens, 0), col(tokens, 0), col(mine, 0), col(mine, 1),
            pl.BlockSpec((2, tokens, SPAN), lambda p: (0, 0, p)), ANY, ANY,
        ],
        out_specs=[col(tokens, 0), col(tokens, 0)],
        out_shape=[jax.ShapeDtypeStruct((tokens, width), bf16)] * 2,
        input_output_aliases={7: 0, 8: 1},
        compiler_params=pltpu.CompilerParams(vmem_limit_bytes=67_000_000),
        cost_estimate=pl.CostEstimate(flops=1 << 24, bytes_accessed=2 << 20, transcendentals=0),
        name="finish_rest",
    )(me, slots, dko, dvo, dmem, dmem, back, *carry)


def place_kernel(me_ref, fam_ref, *rest, spots, plane, nfam, scale):
    n = len(spots)
    parts, (out_ref, buf, sems) = rest[:n], rest[-3:]
    rows = parts[0].shape[0]
    piece = rows // nfam
    core, spot, fam = me_ref[0] & 1, lax.div(me_ref[0], 2), fam_ref[0]
    copies = []
    for i, (part, (flip, other)) in enumerate(zip(parts, spots)):
        at = pl.multiple_of(((core ^ flip) * plane + (spot ^ other)) * rows, rows)
        for k in range(nfam):
            row = pl.multiple_of((fam ^ k) * piece, piece)
            buf[i, pl.ds(row, piece), :] = part[k * piece : (k + 1) * piece, :].astype(f32) * scale
        copies.append(pltpu.make_async_copy(buf.at[i], out_ref.at[pl.ds(at, rows), :], sems.at[i]))
        copies[-1].start()
    for copy in copies:
        copy.wait()


def place(me, fam, parts, spots, plane, nfam, scale, carry):
    rows, width = parts[0].shape
    n = len(parts)
    more = [] if carry is None else [carry]
    smem, vmem = pl.BlockSpec(memory_space=pltpu.SMEM), pl.BlockSpec(memory_space=pltpu.VMEM)
    return pl.pallas_call(
        functools.partial(place_kernel, spots=spots, plane=plane, nfam=nfam, scale=scale),
        in_specs=[smem, smem] + [vmem] * n + [ANY] * len(more),
        out_specs=ANY,
        out_shape=jax.ShapeDtypeStruct((2 * plane * rows, width), f32),
        scratch_shapes=[pltpu.VMEM((n, rows, width), f32), pltpu.SemaphoreType.DMA((n,))],
        input_output_aliases={2 + n: 0} if more else {},
        compiler_params=pltpu.CompilerParams(vmem_limit_bytes=67_000_000),
        cost_estimate=pl.CostEstimate(flops=1 << 20, bytes_accessed=3 << 20, transcendentals=0),
        name="place_rows",
    )(me, fam, *parts, *more)


def swap(x, axis, bits):
    return lax.ppermute(x, axis, [(i, i ^ bits) for i in range(lax.axis_size(axis))])


def bits_of(n):
    out, b = [], 1
    while b < n:
        out.append(b)
        b *= 2
    return out


def mirrored(n):
    order = [0]
    for bit in reversed(bits_of(n)):
        order = order + [i + bit for i in order]
    return order


def gather_rows(x, axis, me):
    for bit in reversed(bits_of(lax.axis_size(axis))):
        other = swap(x, axis, bit)
        upper = (me & bit) != 0
        x = jnp.where(upper, jnp.concatenate([other, x], 0), jnp.concatenate([x, other], 0))
    return x


def exchange(part, axis, shift, me, n):
    return [part(me)] + [swap(part(me ^ k).astype(bf16), axis, k << shift) for k in range(1, n)]


def spread(x, axis, shift, n):
    return [x] + [swap(x, axis, k << shift) for k in range(1, n)]


def total_of(parts):
    return sum([x.astype(f32) for x in parts[1:]], parts[0].astype(f32))


def groups_of(pairs):
    if pairs % 8:
        return [pairs], [(0, 0, pairs)], [pairs]
    u = pairs // 8
    return [3 * u, 5 * u], [(0, 0, u), (1, 0, 5 * u), (0, u, u), (0, 2 * u, u)], [7 * u, u]


def per_device(queries, key_rows, value_rows, cotangent, out_weight, prot_blocks, last_fill, memory_slots):
    q, k, v, cot = queries[0], key_rows[0], value_rows[0], cotangent[0]
    slots = memory_slots[0]
    tokens, width = q.shape
    nctx, nfam = lax.axis_size("ctx"), lax.axis_size("fam")
    me, fam = lax.axis_index("ctx"), lax.axis_index("fam")
    total = slots.shape[0]
    mine = total // nctx
    pairs = width // SPAN
    fsizes, bplan, dhs = groups_of(pairs)
    fstarts = [sum(fsizes[:i]) for i in range(len(fsizes))]
    shift = [(i, i + 1) for i in range(nctx - 1)]
    back = [(i + 1, i) for i in range(nctx - 1)]
    where = jnp.stack([me]).astype(jnp.int32)
    rows = memory_rows(where, memory_slots, k, v, mine)
    halos = halo_groups(k, v, [n * SPAN for n in fsizes])
    mem = gather_rows(rows, "ctx", me)
    halos = [lax.ppermute(x, "ctx", shift) for x in halos]
    grad_attn = dot(cot, out_weight, NT).astype(bf16)
    order = mirrored(nctx)
    carry, saved = [], []
    for i, (at, count) in enumerate(zip(fstarts, fsizes)):
        send, kept, pt, ga = forward(
            where, prot_blocks, last_fill, memory_slots, q, cot, grad_attn, k, v, halos[i], mem, order,
            at, count, carry)
        carry = [send, kept]
        saved.append((pt, ga))
    spot, plane = me >> 1, nctx // 2
    at = lambda x, j, axis: lax.dynamic_index_in_dim(x, j, axis, keepdims=False)
    sent = swap(send, "ctx", 1)
    carry, backs, segments, i = [], [], [], 0
    for total_dh in dhs:
        done = 0
        while done < total_dh:
            j, r, count = bplan[i]
            pt, ga = saved[j]
            out = backward(
                q, pt, ga, k, v, halos[j], halos[j], mem, fstarts[j] + r, count,
                0, (r, fsizes[j] + r), r, carry, total_dh, done)
            carry = list(out)
            segments.append((len(backs), fstarts[j] + r, done, count))
            done, i = done + count, i + 1
        backs.append(lax.ppermute(carry.pop(), "ctx", back))
    both = lambda j, x, y: at(x, j, 0).astype(f32) + at(y, j, 0).astype(f32)
    got = exchange(lambda j: both(j, sent, kept), "ctx", 1, spot, plane)
    got[0] = both(spot, *lax.optimization_barrier((sent, kept)))
    rows = width // nctx
    mem_grad = total_of([x[rows:] for x in got]).astype(bf16)
    piece = lambda j: total_of([lax.dynamic_slice_in_dim(x, j * (rows // nfam), rows // nfam) for x in got])
    w = total_of(exchange(piece, "fam", 0, fam, nfam)).astype(bf16)
    w = jnp.concatenate(spread(w, "fam", 0, nfam), 0)
    parts = spread(w, "ctx", 1, plane)
    others = [swap(x, "ctx", 1) for x in parts]
    scale = (nfam * nctx * tokens) ** -0.5
    who = jnp.stack([fam]).astype(jnp.int32)
    weight = place(where, who, [parts[0], others[0]], [(0, 0), (1, 0)], plane, nfam, scale, None)
    spots = [(flip, k) for flip in range(2) for k in range(1, plane)]
    weight = place(where, who, parts[1:] + others[1:], spots, plane, nfam, scale, weight)
    dq, dko, dvo = carry
    backs = [x.reshape(2, W, -1) for x in backs]
    grads = finish(where, memory_slots, dko, dvo, mem_grad, backs[:1], [x for x in segments if x[0] == 0])
    for i, x in enumerate(backs[1:], 1):
        _, pair, _, count = [x for x in segments if x[0] == i][0]
        grads = finish_rest(where, memory_slots, dko, dvo, mem_grad, x, pair, count, grads)
    dk, dv = grads
    return dq[None], dk[None], dv[None], weight


def solution(mesh):
    row = P("fam", "ctx", None)
    small = P("fam", None)

    return jax.shard_map(
        per_device,
        mesh=mesh,
        in_specs=(row, row, row, row, P(), small, small, small),
        out_specs=(row, row, row, P()),
        check_vma=False,
    )
```

```python
import functools

import jax
import jax.numpy as jnp
from jax import lax
from jax.experimental import pallas as pl
from jax.experimental.pallas import tpu as pltpu
from jax.sharding import PartitionSpec as P


HEAD_DIM = 64
W = 512
BLK = 128
SPAN = 2 * HEAD_DIM
TWO = 2 * BLK
FAR = W // BLK
NEG = -1e30
NT = (((1,), (1,)), ((), ()))
NN = (((1,), (0,)), ((), ()))
TN = (((0,), (0,)), ((), ()))
f32 = jnp.float32
bf16 = jnp.bfloat16


def dot(a, b, dims):
    return lax.dot_general(a, b, dims, preferred_element_type=f32)


def by_head(x, first):
    zero = jnp.zeros_like(x)
    return jnp.concatenate([jnp.where(first, x, zero), jnp.where(first, zero, x)], 0)


def join_heads(x, first):
    return jnp.where(first, x[:BLK], x[BLK:])


def fill_keys(dst, halo, own, memory):
    h, o = halo.shape[0], own.shape[0]
    dst[0:h, :SPAN] = halo[...]
    dst[h : h + o, :SPAN] = own[...]
    dst[h + o :, :SPAN] = memory[...]


def tables(me, blocks_ref, fill_ref, slots_ref, info, bias, nb, tokens, order):
    nprot, slots = blocks_ref.shape[1], slots_ref.shape[1]
    mine = slots // len(order)
    begin = jnp.int32(0)
    first, left, pads = [0] * nb, [0] * nb, []
    for p in range(nprot):
        end = begin + blocks_ref[0, p]
        real = (end - 1) * BLK + fill_ref[0, p]
        pads.append((real, end * BLK))
        for b in range(nb):
            block = me * nb + b
            inside = (block >= begin) & (block < end)
            first[b] = jnp.where(inside, begin, first[b])
            left[b] = jnp.where(inside, real - block * BLK, left[b])
        begin = end
    for b in range(nb):
        info[0, b] = first[b] - (me * nb - FAR)
        info[1, b] = left[b]
    row = lax.broadcasted_iota(jnp.int32, (BLK, BLK), 0)
    for g in range(slots // BLK):
        lanes = jnp.broadcast_to(slots_ref[:, g * BLK : (g + 1) * BLK], (BLK, BLK))
        source = lanes.T + (row + g * BLK) // mine * tokens
        bad = jnp.zeros((BLK, BLK), f32)
        for lo, hi in pads:
            bad = jnp.where((source >= lo) & (source < hi), 1.0, bad)
        for b in range(nb):
            seen = jnp.where((source < first[b] * BLK) & (bad == 0.0), 0.0, NEG)
            for j in range(g * BLK // mine, (g + 1) * BLK // mine):
                i = order.index(j)
                bias[b, i * mine : (i + 1) * mine, :] = seen[j * mine - g * BLK : (j + 1) * mine - g * BLK]


def forward_kernel(
    me_ref, blocks_ref, fill_ref, q_ref, cot_ref, g_ref, ko_ref, vo_ref, kh_ref, vh_ref, km_ref, vm_ref, slots_ref,
    *rest, nb, order, start
):
    send_ref, keep_ref, pt, ga_ref, ke, ve, q2s, pm, mb_ref, at_ref, w_buf, dm_buf, sems, info_ref = rest[-14:]
    slots = km_ref.shape[0]
    mine = slots // len(order)
    ext = kh_ref.shape[0] + ko_ref.shape[0]

    @pl.when(pl.program_id(0) == 0)
    def _():
        tables(me_ref[0], blocks_ref, fill_ref, slots_ref, info_ref, mb_ref, nb, ko_ref.shape[0], order)

    fill_keys(ke, kh_ref, ko_ref, km_ref)
    fill_keys(ve, vh_ref, vo_ref, vm_ref)
    ve[:, SPAN:] = jnp.ones((ve.shape[0], SPAN), bf16)
    first = lax.broadcasted_iota(jnp.int32, (BLK, SPAN), 1) < HEAD_DIM
    tri = (
        lax.broadcasted_iota(jnp.int32, (BLK, TWO), 0)
        <= lax.broadcasted_iota(jnp.int32, (BLK, TWO), 1) % BLK
    )
    lane = lax.broadcasted_iota(jnp.int32, (TWO, SPAN), 1)
    row = lax.broadcasted_iota(jnp.int32, (TWO, SPAN), 0) % BLK
    unit = jnp.asarray(HEAD_DIM**-0.5, bf16)
    at = lambda b: (slice(b * BLK, (b + 1) * BLK), slice(b * TWO, (b + 1) * TWO), slice(b * BLK, (b + FAR + 1) * BLK))
    scores, outs = {}, {}

    def score(b):
        rows, cols, band = at(b)
        q2 = by_head(q_ref[rows, :] * unit, first)
        q2s[cols, :] = q2
        scores[b] = (dot(ke[band, :], q2, NT), dot(ke[ext:, :], q2, NT))

    def exponentials(b):
        _, cols, _ = at(b)
        s, sm = scores.pop(b)
        sm = sm + jnp.concatenate([mb_ref[b], mb_ref[b]], 1)
        off = [jnp.where(e + b >= info_ref[0, b], 0.0, NEG).astype(f32) for e in range(FAR)]
        ends = jnp.where(tri, s[FAR * BLK :, :], s[:BLK, :] + off[0])
        mid = [s[e * BLK : (e + 1) * BLK, :] for e in range(1, FAR)]
        m = jnp.maximum(jnp.max(ends, 0, keepdims=True), jnp.max(sm, 0, keepdims=True))
        for e in range(1, FAR):
            m = jnp.maximum(m, jnp.max(mid[e - 1], 0, keepdims=True) + off[e])
        for e in range(1, FAR):
            pt[0, (b + e) * BLK : (b + e + 1) * BLK, cols] = jnp.exp(
                mid[e - 1] - (m - off[e])
            ).astype(bf16)
        pm[:, cols] = jnp.exp(sm - m).astype(bf16)
        p = jnp.exp(ends - m).astype(bf16)
        zero = jnp.zeros_like(p)
        pt[0, b * BLK : (b + 1) * BLK, cols] = jnp.where(tri, zero, p)
        pt[0, (b + FAR) * BLK : (b + FAR + 1) * BLK, cols] = jnp.where(tri, p, zero)

    def attend(b):
        _, cols, band = at(b)
        outs[b] = dot(pt[0, band, cols], ve[band, :], TN) + dot(pm[:, cols], ve[ext:, :], TN)

    def gradients(b):
        rows, cols, _ = at(b)
        o = outs.pop(b)
        scale = jnp.where(row < info_ref[1, b], 1.0 / o[:, SPAN:], 0.0)
        o = o[:, :SPAN] * scale
        at_ref[rows, :] = join_heads(o, first).astype(bf16)
        g2 = (by_head(g_ref[rows, :].astype(f32), first) * scale).astype(bf16)
        d = -jnp.sum(g2.astype(f32) * o, 1, keepdims=True)
        high = d.astype(bf16).astype(f32)
        ga_ref[0, cols, :SPAN] = g2
        ga_ref[0, cols, SPAN:] = jnp.where(
            lane == 0, high, jnp.where(lane == 1, d - high, 0.0)
        ).astype(bf16)

    def memory(b):
        _, cols, _ = at(b)
        dp = dot(ve[ext:, :], ga_ref[0, cols, :], NT)
        pt[0, ext:, cols] = (pm[:, cols].astype(f32) * dp).astype(bf16)

    for t in range(nb + 4):
        for stage, lag in ((score, 0), (attend, 2), (exponentials, 1), (memory, 4), (gradients, 3)):
            if 0 <= t - lag < nb:
                stage(t - lag)
    step, plane, width = pl.program_id(0), len(order) // 2, cot_ref.shape[1]
    core, slot, rows = me_ref[0] & 1, lax.rem(step, 2), width // len(order)
    dk = dot(pt[0, ext:, :], q2s[...], NN).astype(bf16)
    dv = dot(pm[...], ga_ref[0, :, :SPAN], NN).astype(bf16)
    for i, j in enumerate(order):
        part = slice(i * mine, (i + 1) * mine)
        dm_buf[slot, j % 2, j // 2, :mine, :] = dk[part]
        dm_buf[slot, j % 2, j // 2, mine:, :] = dv[part]
    w_buf[slot] = dot(at_ref[...], cot_ref[...], TN).astype(bf16)

    def copies(at, slot):
        pair = start + at
        out = []
        for t in range(max(1, SPAN // rows)):
            block = pair * (SPAN // rows) + t
            out.append((block // plane == core, lambda ref, t=t, block=block: pltpu.make_async_copy(
                w_buf.at[slot, pl.ds(t * rows, rows), :], ref.at[lax.rem(block, plane), pl.ds(0, rows), :],
                sems.at[slot, 2 + t])))
        for side in range(2):
            out.append((core == side, lambda ref, side=side: pltpu.make_async_copy(
                dm_buf.at[slot, side],
                ref.at[:, pl.ds(rows, 2 * mine), pl.ds(pl.multiple_of(pair * SPAN, SPAN), SPAN)],
                sems.at[slot, side])))
        return out

    for stays, copy in copies(step, slot):

        @pl.when(stays)
        def _():
            copy(keep_ref).start()

        @pl.when(jnp.logical_not(stays))
        def _():
            copy(send_ref).start()

    @pl.when(step > 0)
    def _():
        for _, copy in copies(step - 1, 1 - slot):
            copy(keep_ref).wait()

    @pl.when(step == pl.num_programs(0) - 1)
    def _():
        for _, copy in copies(step, slot):
            copy(keep_ref).wait()


def backward_kernel(
    q_ref, pt_ref, ga_ref, ko_ref, vo_ref, kh_ref, vh_ref, km_ref, *rest, nb
):
    dq_ref, dko_ref, dvo_ref, dh_ref, ke, ve, q2, ds = rest[-8:]
    hrows = kh_ref.shape[0]
    ext = hrows + ko_ref.shape[0]
    fill_keys(ke, kh_ref, ko_ref, km_ref)
    ve[0:hrows, :SPAN] = vh_ref[...]
    ve[hrows:, :SPAN] = vo_ref[...]
    ve[:, SPAN:] = jnp.ones((ve.shape[0], SPAN), bf16)
    first = lax.broadcasted_iota(jnp.int32, (BLK, SPAN), 1) < HEAD_DIM
    unit = HEAD_DIM**-0.5
    for b in range(nb):
        rows, cols = slice(b * BLK, (b + 1) * BLK), slice(b * TWO, (b + 1) * TWO)
        band = slice(b * BLK, (b + FAR + 1) * BLK)
        q2[cols, :] = by_head(q_ref[rows, :] * jnp.asarray(unit, bf16), first)
        ga = ga_ref[0, cols, :]
        dp = dot(ve[band, :], ga, NT)
        ds[band, cols] = (pt_ref[0, band, cols].astype(f32) * dp).astype(bf16)
        dq = dot(ds[band, cols], ke[band, :], TN) + dot(pt_ref[0, ext:, cols], ke[ext:, :], TN)
        dq_ref[rows, :] = (join_heads(dq, first) * unit).astype(bf16)
    for e in range(ext // BLK):
        cols = slice(max(0, e - FAR) * TWO, (min(nb - 1, e) + 1) * TWO)
        rows = slice(e * BLK, (e + 1) * BLK)
        dv = dot(pt_ref[0, rows, cols], ga_ref[0, cols, :SPAN], NN)
        dk = dot(ds[rows, cols], q2[cols, :], NN)
        if e * BLK < hrows:
            dh_ref[rows, :] = dk.astype(bf16)
            dh_ref[hrows + e * BLK : hrows + (e + 1) * BLK, :] = dv.astype(bf16)
        else:
            own = slice(e * BLK - hrows, (e + 1) * BLK - hrows)
            dko_ref[own, :] = dk.astype(bf16)
            dvo_ref[own, :] = dv.astype(bf16)


def columns(rows, start):
    return pl.BlockSpec((rows, SPAN), lambda p, *_: (0, p + start))


ANY = pl.BlockSpec(memory_space=pl.ANY)


def forward(me, blocks, fill, slot_row, q, cot, g, ko, vo, halo, mem, order, start, count, carry):
    tokens, width = q.shape
    slots, hrows, nb, pairs = mem.shape[0], halo.shape[0], tokens // BLK, width // SPAN
    keys = hrows + tokens + slots
    smem = pl.BlockSpec(memory_space=pltpu.SMEM)
    members, plane = len(order), len(order) // 2
    rows, extra = width // members, 2 * slots // members
    out = jax.ShapeDtypeStruct((plane, rows + extra, width), bf16)
    args = [me, blocks, fill, q, cot, g, ko, vo, halo, halo, mem, mem, slot_row]
    specs = [
        smem, smem, smem, columns(tokens, start), pl.BlockSpec((tokens, width), lambda p: (0, 0)),
        columns(tokens, start), columns(tokens, start), columns(tokens, start),
        columns(hrows, 0), columns(hrows, count), columns(slots, start), columns(slots, pairs + start),
        pl.BlockSpec((1, slots), lambda p: (0, 0)),
    ]
    alias = {}
    if carry:
        alias = {len(args) + i: i for i in range(len(carry))}
        args += carry
        specs += [ANY] * len(carry)
    return pl.pallas_call(
        functools.partial(forward_kernel, nb=nb, order=order, start=start),
        grid=(count,),
        in_specs=specs,
        out_specs=[
            ANY, ANY,
            pl.BlockSpec((1, keys, nb * TWO), lambda p: (p, 0, 0)),
            pl.BlockSpec((1, nb * TWO, 2 * SPAN), lambda p: (p, 0, 0)),
        ],
        scratch_shapes=[
            pltpu.VMEM((keys, SPAN), bf16), pltpu.VMEM((keys, 2 * SPAN), bf16),
            pltpu.VMEM((nb * TWO, SPAN), bf16), pltpu.VMEM((slots, nb * TWO), bf16),
            pltpu.VMEM((nb, slots, BLK), f32),
            pltpu.VMEM((tokens, SPAN), bf16), pltpu.VMEM((2, SPAN, width), bf16),
            pltpu.VMEM((2, 2, plane, extra, SPAN), bf16), pltpu.SemaphoreType.DMA((2, 2 + SPAN // rows)),
            pltpu.SMEM((2, nb), jnp.int32),
        ],
        out_shape=[
            out, out,
            jax.ShapeDtypeStruct((count, keys, nb * TWO), bf16),
            jax.ShapeDtypeStruct((count, nb * TWO, 2 * SPAN), bf16),
        ],
        input_output_aliases=alias,
        compiler_params=pltpu.CompilerParams(vmem_limit_bytes=67_000_000),
        cost_estimate=pl.CostEstimate(
            flops=count * nb * 12 * TWO * BLK * 1024, bytes_accessed=count * (4 << 20), transcendentals=count << 20
        ),
        name="band_forward",
    )(*args)


def rows_kernel(me_ref, slots_ref, k_ref, v_ref, rows_ref):
    tokens, width = k_ref.shape
    mine = rows_ref.shape[0]
    row = lax.broadcasted_iota(jnp.int32, (mine, tokens), 0)
    slot = jnp.zeros((mine, tokens), jnp.int32)
    for r in range(mine):
        slot = jnp.where(row == r, slots_ref[0, me_ref[0] * mine + r], slot)
    pick = (slot == lax.broadcasted_iota(jnp.int32, (mine, tokens), 1)).astype(f32).astype(bf16)
    rows_ref[:, :width] = dot(pick, k_ref[...], NN).astype(bf16)
    rows_ref[:, width:] = dot(pick, v_ref[...], NN).astype(bf16)


def memory_rows(me, slots, k, v, mine):
    smem, vmem = pl.BlockSpec(memory_space=pltpu.SMEM), pl.BlockSpec(memory_space=pltpu.VMEM)
    return pl.pallas_call(
        rows_kernel,
        in_specs=[smem, smem, vmem, vmem],
        out_specs=vmem,
        out_shape=jax.ShapeDtypeStruct((mine, 2 * k.shape[1]), bf16),
        compiler_params=pltpu.CompilerParams(vmem_limit_bytes=67_000_000),
        name="memory_rows",
    )(me, slots, k, v)


def halo_kernel(k_ref, v_ref, *halos, sizes):
    edge, at = k_ref.shape[0] - W, 0
    for halo, size in zip(halos, sizes):
        halo[:, :size] = k_ref[edge:, at : at + size]
        halo[:, size:] = v_ref[edge:, at : at + size]
        at += size


def halo_groups(k, v, sizes):
    vmem = pl.BlockSpec(memory_space=pltpu.VMEM)
    return pl.pallas_call(
        functools.partial(halo_kernel, sizes=sizes),
        in_specs=[vmem, vmem],
        out_specs=[vmem] * len(sizes),
        out_shape=[jax.ShapeDtypeStruct((W, 2 * size), bf16) for size in sizes],
        compiler_params=pltpu.CompilerParams(vmem_limit_bytes=67_000_000),
        cost_estimate=pl.CostEstimate(flops=0, bytes_accessed=4 << 20, transcendentals=0),
        name="halo_groups",
    )(k, v)


def backward(q, pt, ga, ko, vo, kh, vh, km, start, count, base, halo_at, at, carry, dh_total, dh_at):
    tokens, width = q.shape
    slots, hrows, nb = km.shape[0], kh.shape[0], tokens // BLK
    keys = hrows + tokens + slots
    kc, vc = halo_at
    args = [q, pt, ga, ko, vo, kh, vh, km]
    specs = [
        columns(tokens, start),
        pl.BlockSpec((1, keys, nb * TWO), lambda p, *_: (p + at, 0, 0)),
        pl.BlockSpec((1, nb * TWO, 2 * SPAN), lambda p, *_: (p + at, 0, 0)),
        columns(tokens, start), columns(tokens, start),
        columns(hrows, kc), columns(hrows, vc), columns(slots, base + start),
    ]
    alias = {}
    if carry:
        alias = {len(args) + i: i for i in range(len(carry))}
        args += carry
        specs += [ANY] * len(carry)
    return pl.pallas_call(
        functools.partial(backward_kernel, nb=nb),
        grid=(count,),
        in_specs=specs,
        out_specs=[
            columns(tokens, start), columns(tokens, start), columns(tokens, start),
            columns(2 * hrows, dh_at),
        ],
        scratch_shapes=[
            pltpu.VMEM((keys, SPAN), bf16), pltpu.VMEM((keys - slots, 2 * SPAN), bf16),
            pltpu.VMEM((nb * TWO, SPAN), bf16), pltpu.VMEM((keys - slots, nb * TWO), bf16),
        ],
        out_shape=[
            jax.ShapeDtypeStruct((tokens, width), bf16),
            jax.ShapeDtypeStruct((tokens, width), bf16),
            jax.ShapeDtypeStruct((tokens, width), bf16),
            jax.ShapeDtypeStruct((2 * hrows, dh_total * SPAN), bf16),
        ],
        input_output_aliases=alias,
        compiler_params=pltpu.CompilerParams(vmem_limit_bytes=67_000_000),
        cost_estimate=pl.CostEstimate(
            flops=count * nb * 20 * TWO * BLK * 1024, bytes_accessed=count * (6 << 20), transcendentals=0
        ),
        name="band_backward",
    )(*args)


def picks(me, slots_ref, base, rows, mine):
    column = lax.broadcasted_iota(jnp.int32, (rows, mine), 1)
    slot = jnp.zeros((rows, mine), jnp.int32)
    for r in range(mine):
        slot = jnp.where(column == r, slots_ref[0, me * mine + r], slot)
    at = lax.broadcasted_iota(jnp.int32, (rows, mine), 0) + base
    return (at == slot).astype(f32).astype(bf16)


def finish_kernel(me_ref, slots_ref, dk_in, dv_in, dm_ref, *rest, segments):
    backs, (dk_ref, dv_ref) = rest[:-2], rest[-2:]
    rows = dk_in.shape[0]
    mine = dm_ref.shape[0] // 2
    pick = picks(me_ref[0], slots_ref, pl.program_id(0) * rows, rows, mine)
    for g, pair, pos, count in segments:
        to, of = slice(pair * SPAN, (pair + count) * SPAN), slice(pos * SPAN, (pos + count) * SPAN)
        back = backs[g]
        dk = dk_in[:, to].astype(f32) + dot(pick, dm_ref[:mine, to], NN)
        dv = dv_in[:, to].astype(f32) + dot(pick, dm_ref[mine:, to], NN)
        dk_ref[:, to] = (dk + back[0, :, of].astype(f32)).astype(bf16)
        dv_ref[:, to] = (dv + back[1, :, of].astype(f32)).astype(bf16)


def finish(me, slots, dko, dvo, dmem, backs, segments):
    tokens, width = dko.shape
    mine = dmem.shape[0] // 2
    smem = pl.BlockSpec(memory_space=pltpu.SMEM)
    step = 2 * BLK
    row = pl.BlockSpec((step, width), lambda r: (r, 0))
    return pl.pallas_call(
        functools.partial(finish_kernel, segments=segments),
        grid=(tokens // step,),
        in_specs=[smem, smem, row, row, pl.BlockSpec((2 * mine, width), lambda r: (0, 0))]
        + [pl.BlockSpec((2, step, b.shape[-1]), lambda r: (0, r, 0)) for b in backs],
        out_specs=[row, row],
        out_shape=[jax.ShapeDtypeStruct((tokens, width), bf16)] * 2,
        compiler_params=pltpu.CompilerParams(vmem_limit_bytes=67_000_000),
        cost_estimate=pl.CostEstimate(flops=1 << 26, bytes_accessed=6 << 20, transcendentals=0),
        name="finish_rows",
    )(me, slots, dko, dvo, dmem, *backs)


def place_kernel(me_ref, fam_ref, *rest, spots, plane, nfam, scale):
    n = len(spots)
    parts, (out_ref, buf, sems) = rest[:n], rest[-3:]
    rows = parts[0].shape[0]
    piece = rows // nfam
    core, spot, fam = me_ref[0] & 1, lax.div(me_ref[0], 2), fam_ref[0]
    copies = []
    for i, (part, (flip, other)) in enumerate(zip(parts, spots)):
        at = pl.multiple_of(((core ^ flip) * plane + (spot ^ other)) * rows, rows)
        for k in range(nfam):
            row = pl.multiple_of((fam ^ k) * piece, piece)
            buf[i, pl.ds(row, piece), :] = part[k * piece : (k + 1) * piece, :].astype(f32) * scale
        copies.append(pltpu.make_async_copy(buf.at[i], out_ref.at[pl.ds(at, rows), :], sems.at[i]))
        copies[-1].start()
    for copy in copies:
        copy.wait()


def place(me, fam, parts, spots, plane, nfam, scale, carry):
    rows, width = parts[0].shape
    n = len(parts)
    more = [] if carry is None else [carry]
    smem, vmem = pl.BlockSpec(memory_space=pltpu.SMEM), pl.BlockSpec(memory_space=pltpu.VMEM)
    return pl.pallas_call(
        functools.partial(place_kernel, spots=spots, plane=plane, nfam=nfam, scale=scale),
        in_specs=[smem, smem] + [vmem] * n + [ANY] * len(more),
        out_specs=ANY,
        out_shape=jax.ShapeDtypeStruct((2 * plane * rows, width), f32),
        scratch_shapes=[pltpu.VMEM((n, rows, width), f32), pltpu.SemaphoreType.DMA((n,))],
        input_output_aliases={2 + n: 0} if more else {},
        compiler_params=pltpu.CompilerParams(vmem_limit_bytes=67_000_000),
        cost_estimate=pl.CostEstimate(flops=1 << 20, bytes_accessed=3 << 20, transcendentals=0),
        name="place_rows",
    )(me, fam, *parts, *more)


def swap(x, axis, bits):
    return lax.ppermute(x, axis, [(i, i ^ bits) for i in range(lax.axis_size(axis))])


def bits_of(n):
    out, b = [], 1
    while b < n:
        out.append(b)
        b *= 2
    return out


def mirrored(n):
    order = [0]
    for bit in reversed(bits_of(n)):
        order = order + [i + bit for i in order]
    return order


def gather_rows(x, axis, me):
    for bit in reversed(bits_of(lax.axis_size(axis))):
        other = swap(x, axis, bit)
        upper = (me & bit) != 0
        x = jnp.where(upper, jnp.concatenate([other, x], 0), jnp.concatenate([x, other], 0))
    return x


def exchange(part, axis, shift, me, n):
    return [part(me)] + [swap(part(me ^ k).astype(bf16), axis, k << shift) for k in range(1, n)]


def spread(x, axis, shift, n):
    return [x] + [swap(x, axis, k << shift) for k in range(1, n)]


def total_of(parts):
    return sum([x.astype(f32) for x in parts[1:]], parts[0].astype(f32))


def groups_of(pairs):
    if pairs % 8:
        return [pairs], [(0, 0, pairs)], [pairs]
    u = pairs // 8
    return [3 * u, 5 * u], [(0, 0, u), (1, 0, 5 * u), (0, u, 2 * u)], [6 * u, 2 * u]


def per_device(queries, key_rows, value_rows, cotangent, out_weight, prot_blocks, last_fill, memory_slots):
    q, k, v, cot = queries[0], key_rows[0], value_rows[0], cotangent[0]
    slots = memory_slots[0]
    tokens, width = q.shape
    nctx, nfam = lax.axis_size("ctx"), lax.axis_size("fam")
    me, fam = lax.axis_index("ctx"), lax.axis_index("fam")
    total = slots.shape[0]
    mine = total // nctx
    pairs = width // SPAN
    fsizes, bplan, dhs = groups_of(pairs)
    fstarts = [sum(fsizes[:i]) for i in range(len(fsizes))]
    shift = [(i, i + 1) for i in range(nctx - 1)]
    back = [(i + 1, i) for i in range(nctx - 1)]
    where = jnp.stack([me]).astype(jnp.int32)
    rows = memory_rows(where, memory_slots, k, v, mine)
    halos = halo_groups(k, v, [n * SPAN for n in fsizes])
    mem = gather_rows(rows, "ctx", me)
    halos = [lax.ppermute(x, "ctx", shift) for x in halos]
    grad_attn = dot(cot, out_weight, NT).astype(bf16)
    order = mirrored(nctx)
    carry, saved = [], []
    for i, (at, count) in enumerate(zip(fstarts, fsizes)):
        send, kept, pt, ga = forward(
            where, prot_blocks, last_fill, memory_slots, q, cot, grad_attn, k, v, halos[i], mem, order,
            at, count, carry)
        carry = [send, kept]
        saved.append((pt, ga))
    spot, plane = me >> 1, nctx // 2
    at = lambda x, j, axis: lax.dynamic_index_in_dim(x, j, axis, keepdims=False)
    sent = swap(send, "ctx", 1)
    carry, backs, segments, i = [], [], [], 0
    for total_dh in dhs:
        done = 0
        while done < total_dh:
            j, r, count = bplan[i]
            pt, ga = saved[j]
            out = backward(
                q, pt, ga, k, v, halos[j], halos[j], mem, fstarts[j] + r, count,
                0, (r, fsizes[j] + r), r, carry, total_dh, done)
            carry = list(out)
            segments.append((len(backs), fstarts[j] + r, done, count))
            done, i = done + count, i + 1
        backs.append(lax.ppermute(carry.pop(), "ctx", back))
    both = lambda j, x, y: at(x, j, 0).astype(f32) + at(y, j, 0).astype(f32)
    got = exchange(lambda j: both(j, sent, kept), "ctx", 1, spot, plane)
    rows = width // nctx
    mem_grad = total_of([x[rows:] for x in got]).astype(bf16)
    piece = lambda j: total_of([lax.dynamic_slice_in_dim(x, j * (rows // nfam), rows // nfam) for x in got])
    w = total_of(exchange(piece, "fam", 0, fam, nfam)).astype(bf16)
    w = jnp.concatenate(spread(w, "fam", 0, nfam), 0)
    parts = spread(w, "ctx", 1, plane)
    others = [swap(x, "ctx", 1) for x in parts]
    scale = (nfam * nctx * tokens) ** -0.5
    who = jnp.stack([fam]).astype(jnp.int32)
    weight = place(where, who, [parts[0], others[0]], [(0, 0), (1, 0)], plane, nfam, scale, None)
    spots = [(flip, k) for flip in range(2) for k in range(1, plane)]
    weight = place(where, who, parts[1:] + others[1:], spots, plane, nfam, scale, weight)
    dq, dko, dvo = carry
    backs = [x.reshape(2, W, -1) for x in backs]
    dk, dv = finish(where, memory_slots, dko, dvo, mem_grad, backs, segments)
    return dq[None], dk[None], dv[None], weight


def solution(mesh):
    row = P("fam", "ctx", None)
    small = P("fam", None)

    return jax.shard_map(
        per_device,
        mesh=mesh,
        in_specs=(row, row, row, row, P(), small, small, small),
        out_specs=(row, row, row, P()),
        check_vma=False,
    )
```
